32 devices in a mesh: dp: 8 (over z, x), tensor: 4 (over y, core).
Axes of the slice: x: 2, y: 2, z: 4, core: 2. Of those that a mesh axis runs over, the one named last changes fastest.
Arguments:
- layer_input: bfloat16 [24576, 768], P(('dp', 'tensor')), may hold values from -6 to 6
- segment_ids: int32 [24, 1024], P('dp'), may hold values from 0 to 3, never falling along the last dimension, each value on 1 to 800 neighbouring positions
- w_query: bfloat16 [768, 768], P(None, 'tensor'), may hold values from -0.21875 to 0.21875
- b_query: bfloat16 [768], P('tensor'), may hold values from -1.5 to 1.5
- w_key: bfloat16 [768, 768], P(None, 'tensor'), may hold values from -0.21875 to 0.21875
- w_value: bfloat16 [768, 768], P(None, 'tensor'), may hold values from -0.21875 to 0.21875
- b_value: bfloat16 [768], P('tensor'), may hold values from -1.5 to 1.5
- w_out: bfloat16 [768, 768], P('tensor'), may hold values from -1.75 to 1.75
- b_out: float32 [768], replicated, may hold values from -1.5 to 1.5
- first_gain: float32 [768], replicated, may hold values from 0.5 to 1.5
- first_shift: float32 [768], replicated, may hold values from -1.5 to 1.5
- w_in: bfloat16 [768, 3072], P(None, 'tensor'), may hold values from -0.21875 to 0.21875
- b_in: bfloat16 [3072], P('tensor'), may hold values from -1.5 to 1.5
- w_back: bfloat16 [3072, 768], P('tensor'), may hold values from -0.21875 to 0.21875
- b_back: float32 [768], replicated, may hold values from -1.5 to 1.5
- second_gain: float32 [768], replicated, may hold values from 0.5 to 1.5
- second_shift: float32 [768], replicated, may hold values from -1.5 to 1.5
- cotangent: bfloat16 [24576, 768], P(('dp', 'tensor')), may hold values from -6 to 6
Outputs:
- layer_output: bfloat16 [24576, 768], P(('dp', 'tensor'))
- input_grad: bfloat16 [24576, 768], P(('dp', 'tensor'))
- grad_w_query: float32 [768, 768], P(None, 'tensor')
- grad_b_query: float32 [768], P('tensor')
- grad_w_key: float32 [768, 768], P(None, 'tensor')
- grad_w_value: float32 [768, 768], P(None, 'tensor')
- grad_b_value: float32 [768], P('tensor')
- grad_w_out: float32 [768, 768], P('tensor')
- grad_b_out: float32 [768], replicated
- grad_first_gain: float32 [768], replicated
- grad_first_shift: float32 [768], replicated
- grad_w_in: float32 [768, 3072], P(None, 'tensor')
- grad_b_in: float32 [3072], P('tensor')
- grad_w_back: float32 [3072, 768], P('tensor')
- grad_b_back: float32 [768], replicated
- grad_second_gain: float32 [768], replicated
- grad_second_shift: float32 [768], replicated
The draws below stay inside these ranges and needn't reach their ends.
Inputs may be any that keep to these rules, and one draw needn't show every extreme that they name: `segment_ids`: along each packed sequence the document numbers never fall; a document spans 1 to 800 tokens, and one document spans exactly that many.
All inputs are finite; a program needn't handle non-finite values.
Results may differ from the reference program's by a relative error of at most 0.023.
Values may be sent and summed in bfloat16 or wider, within the bound.
A program may use at most 128 MiB of HBM per device.

```python
import math
import jax
import jax.numpy as jnp
import numpy as np
from jax import lax

D = 768
HEADS = 12
HEAD_DIM = 64
FF = 3072
LEN = 1024
SEQS = 24
TOKENS = 24576


def levels(own_key, dims, shards, smallest, high):
    loudness = 1.0
    for dim, shards_of in shards:
        heights = jax.random.uniform(jax.random.fold_in(jax.random.fold_in(own_key, 6), dim), (shards_of,), jnp.float32, smallest / len(shards), high / len(shards))
        loudness = loudness * jnp.repeat(jnp.exp(heights), dims[dim] // shards_of).reshape((-1,) + (1,) * (len(dims) - 1 - dim))
    return loudness


def length_profile(amount, total, reach, slope):
    loads = [(1 << 20) // math.isqrt(rank ** slope) + 1 for rank in range(2, amount + 1)]
    rest, counts = total - reach - (amount - 1), [1] * (amount - 1)
    while rest > 0:
        movable = [i for i in range(amount - 1) if counts[i] < reach]
        whole, budget = sum([loads[i] for i in movable]), rest
        for i in movable:
            extra = min(reach - counts[i], max(1, budget * loads[i] // whole), rest)
            counts[i] = counts[i] + extra
            rest = rest - extra
    return np.array([reach] + counts)


def ragged_sizes(rng, number_of, total, limit, skew):
    if number_of == 2:
        one = jax.random.randint(rng, (), max(1, total - limit), min(limit, total - 1) + 1)
        return jnp.stack([one, total - one])
    tallies = jnp.asarray(length_profile(number_of, total, limit, skew), jnp.int32)
    pairs = (number_of - 1) // 2
    giver, sink = tallies[1:1 + 2 * pairs:2], tallies[2:2 + 2 * pairs:2]
    margin = jnp.minimum(giver - 1, limit - sink)
    moved = jax.random.randint(jax.random.fold_in(rng, 1), (pairs,), 0, 1 << 20) % (margin + 1)
    tallies = tallies.at[1:1 + 2 * pairs:2].set(giver - moved).at[2:2 + 2 * pairs:2].set(sink + moved)
    return tallies[jax.random.permutation(jax.random.fold_in(rng, 2), number_of)]


def scatter_about(own_key, dims, deviation, limit, cuts=(), held_as=jnp.bfloat16):
    drawn = jax.random.normal(own_key, dims, jnp.float32) * deviation
    if len(cuts) > 0:
        drawn = levels(own_key, dims, cuts, -0.22, 0.18) * drawn
    return jnp.clip(drawn, min=-limit, max=limit).astype(held_as)


def setup_inputs(seed: int = 0) -> dict:
    keys = jax.random.split(jax.random.key(seed), 19)
    layer_input = scatter_about(keys[0], (TOKENS, D), 1.0, 6.0, ((0, 32),))
    segment_ids = jax.vmap(lambda own: jnp.searchsorted(jnp.cumsum(ragged_sizes(own, max(2, LEN // 256), LEN, LEN * 25 // 32, 2)), jnp.arange(LEN), side="right"))(jax.random.split(keys[1], SEQS)).reshape((SEQS, LEN)).astype(jnp.int32)
    w_query = scatter_about(keys[2], (D, D), D ** -0.5, 0.21875, ((1, 4),))
    b_query = scatter_about(keys[3], (D,), 0.3, 1.5, ((0, 4),))
    w_key = scatter_about(keys[4], (D, D), D ** -0.5, 0.21875, ((1, 4),))
    w_value = scatter_about(keys[5], (D, D), D ** -0.5, 0.21875, ((1, 4),))
    b_value = scatter_about(keys[6], (D,), 0.3, 1.5, ((0, 4),))
    w_out = scatter_about(keys[7], (D, D), (D // 64) ** -0.5, 1.75, ((0, 4),))
    b_out = scatter_about(keys[8], (D,), 0.3, 1.5, (), jnp.float32)
    first_gain = jnp.clip(1.0 + 0.1 * jax.random.normal(keys[9], (D,), jnp.float32), 0.5, 1.5)
    first_shift = scatter_about(keys[10], (D,), 0.3, 1.5, (), jnp.float32)
    w_in = scatter_about(keys[11], (D, FF), D ** -0.5, 0.21875, ((1, 4),))
    b_in = scatter_about(keys[12], (FF,), 0.3, 1.5, ((0, 4),))
    w_back = scatter_about(keys[13], (FF, D), (FF // 4) ** -0.5, 0.21875, ((0, 4),))
    b_back = scatter_about(keys[14], (D,), 0.3, 1.5, (), jnp.float32)
    second_gain = jnp.clip(1.0 + 0.1 * jax.random.normal(keys[15], (D,), jnp.float32), 0.5, 1.5)
    second_shift = scatter_about(keys[16], (D,), 0.3, 1.5, (), jnp.float32)
    cotangent = scatter_about(keys[17], (TOKENS, D), 1.0, 6.0, ((0, 32),))
    return dict(layer_input=layer_input, segment_ids=segment_ids, w_query=w_query, b_query=b_query, w_key=w_key, w_value=w_value, b_value=b_value, w_out=w_out, b_out=b_out, first_gain=first_gain, first_shift=first_shift, w_in=w_in, b_in=b_in, w_back=w_back, b_back=b_back, second_gain=second_gain, second_shift=second_shift, cotangent=cotangent)


@jax.custom_vjp
def low(v):
    return lax.optimization_barrier(v.astype(jnp.bfloat16)).astype(jnp.float32)

@jax.custom_vjp
def low_back(v):
    return v

def low_keep(v):
    return (low(v), None)

def low_pass(kept, grad):
    return (grad,)

def back_keep(v):
    return (v, None)

def back_low(kept, grad):
    return (low(grad),)
low.defvjp(low_keep, low_pass)
low_back.defvjp(back_keep, back_low)
EPSILON = 1e-05

def norm_rows(values, scale_vec, shift_vec):
    center = values - lax.optimization_barrier(jnp.mean(values, axis=-1, keepdims=True))
    spread = lax.optimization_barrier(jnp.mean(center * center, axis=-1, keepdims=True))
    return center * lax.rsqrt(spread + EPSILON) * scale_vec + shift_vec

def attend(pieces):
    query_seq, key_seq, value_seq, segment_seq = pieces
    scores = jnp.einsum('qhd,khd->hqk', query_seq, key_seq, precision=lax.Precision.HIGHEST) * HEAD_DIM ** (-0.5)
    scores = low_back(scores)
    same_doc = segment_seq[:, None] == segment_seq[None, :]
    scores = jnp.where(same_doc[None], scores, -1e+30)
    prob_low = low(jax.nn.softmax(scores, axis=-1))
    return jnp.einsum('hqk,khd->qhd', prob_low, value_seq, precision=lax.Precision.HIGHEST)

def matmul(left_side, right_side):
    return jnp.dot(left_side, right_side, precision=lax.Precision.HIGHEST)

def forward(layer_input, w_query, b_query, w_key, w_value, b_value, w_out, b_out, first_gain, first_shift, w_in, b_in, w_back, b_back, second_gain, second_shift, segment_ids):
    query_rows = low_back(low(matmul(layer_input, w_query) + b_query))
    key_rows = low_back(low(matmul(layer_input, w_key)))
    value_rows = low_back(low(matmul(layer_input, w_value) + b_value))
    shape_four = (SEQS, LEN, HEADS, HEAD_DIM)
    mixed_heads = lax.map(jax.checkpoint(attend), (query_rows.reshape(shape_four), key_rows.reshape(shape_four), value_rows.reshape(shape_four), segment_ids))
    heads_out = low_back(low(mixed_heads.reshape(TOKENS, D)))
    attn_rows = low_back(matmul(heads_out, w_out)) + b_out
    first_norm = norm_rows(layer_input + attn_rows, first_gain, first_shift)
    hidden_pre = low_back(matmul(low(first_norm), w_in) + b_in)
    hidden = low(jax.nn.gelu(hidden_pre, approximate=False))
    second_in = first_norm + low_back(matmul(hidden, w_back)) + b_back
    return norm_rows(second_in, second_gain, second_shift)

def reference(layer_input, segment_ids, w_query, b_query, w_key, w_value, b_value, w_out, b_out, first_gain, first_shift, w_in, b_in, w_back, b_back, second_gain, second_shift, cotangent):
    float_params = [item.astype(jnp.float32) for item in (layer_input, w_query, b_query, w_key, w_value, b_value, w_out, b_out, first_gain, first_shift, w_in, b_in, w_back, b_back, second_gain, second_shift)]

    def run_layer(*values):
        return forward(*values, segment_ids)
    result, pullback = jax.vjp(run_layer, *float_params)
    gradients = pullback(cotangent.astype(jnp.float32))
    return (result.astype(jnp.bfloat16), gradients[0].astype(jnp.bfloat16), gradients[1], gradients[2], gradients[3], gradients[4], gradients[5], gradients[6], gradients[7], gradients[8], gradients[9], gradients[10], gradients[11], gradients[12], gradients[13], gradients[14], gradients[15])
```

```python
import math

import jax
import jax.numpy as jnp
from jax import lax
from jax.experimental import pallas as pl
from jax.experimental.pallas import tpu as pltpu
from jax.sharding import PartitionSpec as P

F32 = jnp.float32
BF = jnp.bfloat16
MESH = pl.DeviceIdType.MESH
HEAD_DIM = 64
EPSILON = 1e-05
BIG = 1e30
LOG2E = 1.0 / math.log(2.0)
QSCALE = HEAD_DIM ** (-0.5) * LOG2E
BLK = 256


def dg(a, b, ca, cb):
    return lax.dot_general(a, b, (((ca,), (cb,)), ((), ())), preferred_element_type=F32)


def where_am_i():
    t = lax.axis_index("tensor")
    d = lax.axis_index("dp")
    core = t + 1 - 2 * (t % 2)
    across = (t + 2) % 4
    diag = 3 - t
    side = d + 1 - 2 * (d % 2)
    return t, d, core, across, diag, side


def block_of(t, i):
    b = 3 * t + i
    middle = (b // 4) % 2
    return middle, b % 4


class Copies:
    def __init__(self, send, recv):
        self.send, self.recv, self.used = send, recv, 0

    def new(self, src, dst, **device):
        k = self.used
        self.used += 1
        return pltpu.make_async_remote_copy(
            src_ref=src,
            dst_ref=dst,
            send_sem=self.send.at[k],
            recv_sem=self.recv.at[k],
            device_id=device,
            device_id_type=MESH,
        )


def greet(devices):
    barrier = pltpu.get_barrier_semaphore()
    for dev in devices:
        pl.semaphore_signal(barrier, inc=1, device_id=dev, device_id_type=MESH)
    pl.semaphore_wait(barrier, len(devices))


def gather_shard(cp, own, gathered, core, across, side, half):
    rows = own.shape[0] // 2
    part = pl.ds(pl.multiple_of(half * rows, rows), rows)
    first = [
        cp.new(own.at[part], gathered.at[1, part], tensor=across),
        cp.new(own, gathered.at[0], tensor=core),
    ]
    second = cp.new(gathered.at[1, part], gathered.at[1, part], dp=side)
    third = cp.new(gathered.at[1], gathered.at[2], tensor=core)
    return first, second, third


def k1(
    x_ref, wt_ref, bias_ref, seg_ref, wout_ref, win_ref,
    qkv_ref, o_ref, lse_ref, xab_ref, wpar_ref, woutg_ref, wing_ref, biasg_ref,
    wt_v, qa, ka, va, send, recv, local,
):
    length = 1024
    t, d, core, across, diag, side = where_am_i()
    y, c = t // 2, t % 2
    half = d % 2
    greet([{"tensor": core}, {"tensor": across}, {"tensor": diag}, {"dp": side}])
    cp = Copies(send, recv)
    rows_out, rows_local = [], []
    for i in range(3):
        middle, blk = block_of(t, i)
        src = x_ref.at[pl.ds(i * BLK, BLK)]
        dst = xab_ref.at[middle, pl.ds(pl.multiple_of(blk * BLK, BLK), BLK)]
        rows_local.append(pltpu.make_async_copy(src, dst, local.at[i]))
        rows_out.append(cp.new(src, dst, tensor=core))
    w_local = pltpu.make_async_copy(wt_ref, wt_v, local.at[3])
    for copy in rows_local + [w_local] + rows_out:
        copy.start()
    rows = wt_ref.shape[0] // 2
    part = pl.ds(pl.multiple_of(half * rows, rows), rows)
    wp_first = cp.new(wt_ref.at[part], wpar_ref.at[part], tensor=across)
    wp_second = cp.new(wpar_ref.at[part], wpar_ref.at[part], dp=side)
    bias_out = [
        cp.new(bias_ref, biasg_ref.at[0], tensor=core),
        cp.new(bias_ref, biasg_ref.at[1], tensor=across),
        cp.new(bias_ref, biasg_ref.at[2], tensor=diag),
    ]
    cross_in = 2 * (1 - y) + c
    cross_slot = pl.ds(pl.multiple_of(cross_in * BLK, BLK), BLK)
    mixed = (t == 1) | (t == 2)
    first_middle = jnp.where(t == 1, 1, 0)
    cross_out = []
    base = cp.used
    for k in range(2):
        src = x_ref.at[pl.ds(pl.multiple_of((first_middle + k) * BLK, BLK), BLK)]
        dst_blk = 2 * y + k
        dst = xab_ref.at[1, pl.ds(pl.multiple_of(dst_blk * BLK, BLK), BLK)]
        cross_out.append(
            pltpu.make_async_remote_copy(
                src_ref=src, dst_ref=dst, send_sem=send.at[base + k], recv_sem=recv.at[base],
                device_id={"tensor": 2 * (1 - y) + k}, device_id_type=MESH,
            )
        )
    cp.used += 2
    cross_arrived = pltpu.make_async_remote_copy(
        src_ref=x_ref.at[pl.ds(0, BLK)], dst_ref=xab_ref.at[1, cross_slot], send_sem=send.at[base],
        recv_sem=recv.at[base], device_id={"tensor": core}, device_id_type=MESH,
    )
    cross_forward = cp.new(xab_ref.at[1, cross_slot], xab_ref.at[1, cross_slot], tensor=core)

    wp_first.start()
    for copy in bias_out:
        copy.start()

    @pl.when(mixed)
    def _():
        for copy in cross_out:
            copy.start()

    out1, out2, out3 = gather_shard(cp, wout_ref, woutg_ref, core, across, side, half)
    in1, in2, in3 = gather_shard(cp, win_ref, wing_ref, core, across, side, half)
    for copy in out1 + in1:
        copy.start()

    def project(g, middle, w, bias):
        col = jnp.transpose(bias)[0:576, 1:2]

        def body(n, _):
            cs = pl.ds(pl.multiple_of(n * BLK, BLK), BLK)
            r = dg(w[...], xab_ref[middle, cs, :], 1, 1) + col
            qkv_ref[g, 0:192, cs] = (r[0:192] * QSCALE).astype(BF)
            qkv_ref[g, 192:576, cs] = r[192:576].astype(BF)
            return 0

        lax.fori_loop(0, length // BLK, body, 0)

    def attend(g, which):
        seg = seg_ref[which]
        row = lax.broadcasted_iota(jnp.int32, (64, length), 0)
        same = (row == seg).astype(F32)
        qa[64:128, :] = same.astype(BF)
        key_mark = ((same - 1.0) * BIG).astype(BF)
        va[64:80, :] = jnp.ones((16, length), BF)

        def unit(h, _):
            r = pl.multiple_of(h * 64, 64)
            qa[0:64, :] = qkv_ref[g, pl.ds(r, 64), :]
            ka[...] = jnp.concatenate([qkv_ref[g, pl.ds(r + 192, 64), :], key_mark], axis=0).T
            va[0:64, :] = qkv_ref[g, pl.ds(r + 384, 64), :]
            s = jnp.dot(ka[...], qa[...], preferred_element_type=F32)
            m = jnp.max(s, axis=0, keepdims=True)
            p = jnp.exp2(s - m).astype(BF)
            o = jnp.dot(va[...], p, preferred_element_type=F32)
            total = o[64:65, :]
            res = (o[0:64] * (1.0 / total)).astype(BF)
            for b in range(4):
                o_ref[g, b, pl.ds(r, 64), :] = res[:, b * BLK : (b + 1) * BLK]
            lse_ref[g * 3 + h] = m + jnp.log2(total)
            return 0

        lax.fori_loop(0, 3, unit, 0)

    for copy in rows_local + [w_local]:
        copy.wait()
    for copy in rows_out:
        copy.wait_recv()
    own_seq = 2 * y
    project(0, 0, wt_v, bias_ref[...])
    attend(0, own_seq)
    wp_first.wait_recv()
    wp_second.start()
    cross_arrived.wait_recv()
    cross_forward.start()
    bias_out[1].wait_recv()
    cross_forward.wait_recv()
    project(2, 1, wt_v, bias_ref[...])
    attend(2, 1)
    out1[0].wait_recv()
    out2.start()
    wp_second.wait_recv()
    project(1, 0, wpar_ref, biasg_ref[1])
    attend(1, own_seq)
    out2.wait_recv()
    out3.start()
    in1[0].wait_recv()
    in2.start()
    in2.wait_recv()
    in3.start()
    for copy in (bias_out[0], bias_out[2], out1[1], in1[1], out3, in3):
        copy.wait_recv()
    for copy in rows_out + [wp_first, wp_second, cross_forward] + bias_out + out1 + in1 + [out2, in2, out3, in3]:
        copy.wait_send()

    @pl.when(mixed)
    def _():
        for copy in cross_out:
            copy.wait_send()


def layer_stats(z):
    mean = jnp.mean(z, axis=-1, keepdims=True)
    cen = z - mean
    var = jnp.mean(cen * cen, axis=-1, keepdims=True)
    inv = lax.rsqrt(var + EPSILON)
    return cen * inv, inv


def k2(
    x_ref, cot_ref, vec_ref, bias_ref, biasg_ref, o_ref, wout_ref, woutg_ref, win_ref, wing_ref, wback_ref,
    out_ref, dz1_ref, do_ref, g_ref, small_ref,
    ot, wo, wi, wb, wbg, h1b, h1t, xh1, inv1, gg, gp, z2, dz2b, dz2t, dz2, send, recv, local,
):
    t, d, core, across, diag, side = where_am_i()
    half = d % 2
    tok = x_ref.shape[0]
    greet([{"tensor": core}, {"tensor": across}, {"tensor": diag}, {"dp": side}])
    cp = Copies(send, recv)

    peers = (t, core, across, diag)
    pending = []
    for j, dev in enumerate(peers):
        for i in range(3):
            middle, blk = block_of(dev, i)
            for second in (False, True) if j < 2 else (False,):
                slot = j + 2 if second else j
                src_group = 1 if second else None
                src = o_ref.at[1 if second else 2 * middle, blk]
                dst = ot.at[i, pl.ds(slot * 192, 192)]
                sem = recv.at[i * 4 + slot]
                if j == 0:
                    copy = pltpu.make_async_copy(src, dst, sem)
                else:
                    k = 3 * (4 + j) + i if not second else 24 + i
                    copy = pltpu.make_async_remote_copy(
                        src_ref=src, dst_ref=dst, send_sem=send.at[k], recv_sem=sem,
                        device_id={"tensor": dev}, device_id_type=MESH,
                    )
                if j == 0 and not second or j == 1 and not second:
                    cond = None
                elif second:
                    cond = middle == 0
                else:
                    cond = middle == 1
                if cond is None:
                    copy.start()
                else:
                    pl.when(cond)(copy.start)
                if j:
                    pending.append((cond, copy))
    cp.used = 27
    b1, b2, b3 = gather_shard(cp, wback_ref, wbg, core, across, side, half)
    for copy in b1:
        copy.start()
    loads = [pltpu.make_async_copy(wout_ref, wo.at[pl.ds(0, 192)], local.at[0])]
    loads += [pltpu.make_async_copy(woutg_ref.at[j], wo.at[pl.ds(192 * (j + 1), 192)], local.at[j + 1]) for j in range(3)]
    loads_in = [pltpu.make_async_copy(win_ref, wi.at[:, pl.ds(0, 768)], local.at[4])]
    loads_in += [pltpu.make_async_copy(wing_ref.at[j], wi.at[:, pl.ds(768 * (j + 1), 768)], local.at[5 + j]) for j in range(3)]
    load_b0 = pltpu.make_async_copy(wback_ref, wb.at[pl.ds(0, 768)], local.at[8])
    for copy in loads + loads_in + [load_b0]:
        copy.start()

    b_out, gain1, shift1, b_back, gain2, shift2 = [vec_ref[k : k + 1, :] for k in range(6)]
    for copy in loads:
        copy.wait()
    for i in range(3):
        for slot in range(4):
            pltpu.make_async_copy(o_ref.at[0, 0], ot.at[i, pl.ds(slot * 192, 192)], recv.at[i * 4 + slot]).wait()

    def first(i, _):
        rs = pl.ds(pl.multiple_of(i * BLK, BLK), BLK)
        z = x_ref[rs, :].astype(F32) + dg(ot[i], wo[...], 0, 0) + b_out
        xh, inv = layer_stats(z)
        xh1[rs, :] = xh
        inv1[rs, :] = inv
        h1b[rs, :] = (xh * gain1 + shift1).astype(BF)
        return 0

    lax.fori_loop(0, 3, first, 0)
    h1t[...] = h1b[...].T
    for copy in loads_in:
        copy.wait()

    def up(n, _):
        cs = pl.ds(pl.multiple_of(n * BLK, BLK), BLK)
        j = n // 3
        low = pl.ds(pl.multiple_of((n % 3) * BLK, BLK), BLK)
        bias = jnp.where(j == 0, bias_ref[0:1, low], biasg_ref[jnp.maximum(j - 1, 0), 0:1, low])
        u = jnp.dot(h1b[...], wi[:, cs], preferred_element_type=F32) + bias
        cdf = 0.5 * (1.0 + lax.erf(u * (2.0 ** -0.5)))
        pdf = jnp.exp(-0.5 * u * u) * (1.0 / math.sqrt(2.0 * math.pi))
        gg[:, cs] = (u * cdf).astype(BF)
        gp[:, cs] = (cdf + u * pdf).astype(BF)
        return 0

    lax.fori_loop(0, 6, up, 0)
    b1[0].wait_recv()
    b2.start()
    lax.fori_loop(6, 12, up, 0)
    b2.wait_recv()
    b3.start()
    b1[1].wait_recv()
    loads_b = [pltpu.make_async_copy(wbg.at[j], wb.at[pl.ds(768 * (j + 1), 768)], local.at[9 + j]) for j in range(3)]
    loads_b[0].start()
    loads_b[1].start()
    b3.wait_recv()
    loads_b[2].start()
    load_b0.wait()
    for copy in loads_b:
        copy.wait()

    def down(n, _):
        cs = pl.ds(pl.multiple_of(n * BLK, BLK), BLK)
        z2[:, cs] = jnp.dot(gg[...], wb[:, cs], preferred_element_type=F32)
        return 0

    lax.fori_loop(0, 3, down, 0)

    def second_norm(i, sums):
        rs = pl.ds(pl.multiple_of(i * BLK, BLK), BLK)
        h1 = xh1[rs, :] * gain1 + shift1
        xh, inv = layer_stats(h1 + z2[rs, :] + b_back)
        out_ref[rs, :] = (xh * gain2 + shift2).astype(BF)
        cot = cot_ref[rs, :].astype(F32)
        dxh = cot * gain2
        dz = inv * (dxh - jnp.mean(dxh, axis=-1, keepdims=True) - xh * jnp.mean(dxh * xh, axis=-1, keepdims=True))
        dz2[rs, :] = dz
        dz2b[rs, :] = dz.astype(BF)
        return (
            sums[0] + jnp.sum(dz, axis=0, keepdims=True),
            sums[1] + jnp.sum(cot * xh, axis=0, keepdims=True),
            sums[2] + jnp.sum(cot, axis=0, keepdims=True),
        )

    zero = jnp.zeros((1, 768), F32)
    s3, s4, s5 = lax.fori_loop(0, 3, second_norm, (zero, zero, zero))
    small_ref[3:4, :] = s3
    small_ref[4:5, :] = s4
    small_ref[5:6, :] = s5
    dz2t[...] = dz2b[...].T

    def back(n, _):
        cs = pl.ds(pl.multiple_of(n * BLK, BLK), BLK)
        j = n // 3
        low = pl.ds(pl.multiple_of((n % 3) * BLK, BLK), BLK)
        g = gg[:, cs]
        g_ref[j, 768:1536, low] = jnp.dot(dz2t[...], g, preferred_element_type=F32).astype(BF)
        du = (dg(dz2b[...], wb[cs, :], 1, 1) * gp[:, cs].astype(F32)).astype(BF)
        gg[:, cs] = du
        small_ref[pl.ds(8 + j, 1), low] = jnp.sum(du.astype(F32), axis=0, keepdims=True)
        g_ref[j, 0:768, low] = jnp.dot(h1t[...], du, preferred_element_type=F32).astype(BF)
        return 0

    lax.fori_loop(0, 12, back, 0)

    def into_h(n, _):
        cs = pl.ds(pl.multiple_of(n * BLK, BLK), BLK)
        z2[:, cs] = dg(gg[...], wi[cs, :], 1, 1) + dz2[:, cs]
        return 0

    lax.fori_loop(0, 3, into_h, 0)

    def first_norm(i, sums):
        rs = pl.ds(pl.multiple_of(i * BLK, BLK), BLK)
        dh = z2[rs, :]
        xh = xh1[rs, :]
        dxh = dh * gain1
        dz = inv1[rs, :] * (dxh - jnp.mean(dxh, axis=-1, keepdims=True) - xh * jnp.mean(dxh * xh, axis=-1, keepdims=True))
        dz1_ref[rs, :] = dz
        dzb = dz.astype(BF)
        dz2b[rs, :] = dzb
        do_ref[i] = dg(wo[...], dzb, 1, 1).astype(BF)
        return (
            sums[0] + jnp.sum(dz, axis=0, keepdims=True),
            sums[1] + jnp.sum(dh * xh, axis=0, keepdims=True),
            sums[2] + jnp.sum(dh, axis=0, keepdims=True),
        )

    s0, s1, s2 = lax.fori_loop(0, 3, first_norm, (zero, zero, zero))
    small_ref[0:1, :] = s0
    small_ref[1:2, :] = s1
    small_ref[2:3, :] = s2
    for j in range(4):
        rows = pl.ds(192 * j, 192)
        acc = jnp.dot(ot[0, rows, :], dz2b[0:BLK, :], preferred_element_type=F32)
        acc += jnp.dot(ot[1, rows, :], dz2b[BLK : 2 * BLK, :], preferred_element_type=F32)
        acc += jnp.dot(ot[2, rows, :], dz2b[2 * BLK : 3 * BLK, :], preferred_element_type=F32)
        g_ref[j, 1536:1728, :] = acc.astype(BF)
    small_ref[6:8, :] = jnp.zeros((2, 768), F32)
    small_ref[12:16, :] = jnp.zeros((4, 768), F32)

    for cond, copy in pending:
        if cond is None:
            copy.wait_send()
        else:
            pl.when(cond)(copy.wait_send)
    for copy in b1 + [b2, b3]:
        copy.wait_send()


def split3(v):
    a = v.astype(BF).astype(F32)
    b = (v - a).astype(BF).astype(F32)
    return a, b, v - a - b


def k3(
    qkv_ref, seg_ref, o_ref, lse_ref, xab_ref, wt_ref, wpar_ref, do_in, dz1_ref,
    din_ref, dw_ref, db_ref,
    do_ref, dq_s, qa, ka, va, da, dk, dv, pab, sbuf, rcore, rmid, rhalf, hsum, send, recv, landed,
):
    length = 1024
    t, d, core, across, diag, side = where_am_i()
    y, c = t // 2, t % 2
    greet([{"tensor": core}, {"tensor": across}, {"tensor": diag}])
    pending = []
    peers = (t, core, across, diag)
    for i in range(3):
        middle, blk = block_of(t, i)
        for j, dev in enumerate(peers):
            src = do_in.at[i, pl.ds(192 * j, 192)]
            group = jnp.where(middle == 1, 2, j // 2)
            dst = do_ref.at[group, blk]
            sem = landed.at[group * 4 + blk]
            if j == 0:
                pltpu.make_async_copy(src, dst, sem).start()
                continue
            if j == 2:
                pl.when(middle == 0)(pltpu.make_async_copy(src, dst, sem).start)
                to, cond = across, middle == 1
            elif j == 1:
                to, cond = core, None
            else:
                to, cond = jnp.where(middle == 1, diag, core), None
            copy = pltpu.make_async_remote_copy(
                src_ref=src, dst_ref=dst, send_sem=send.at[i * 3 + j - 1], recv_sem=sem,
                device_id={"tensor": to}, device_id_type=MESH,
            )
            if cond is None:
                copy.start()
            else:
                pl.when(cond)(copy.start)
            pending.append((cond, copy))

    def attend_back(g, which):
        for blk in range(4):
            pltpu.make_async_copy(do_in.at[0, pl.ds(0, 192)], do_ref.at[g, blk], landed.at[g * 4 + blk]).wait()
        seg = seg_ref[which]
        row = lax.broadcasted_iota(jnp.int32, (64, length), 0)
        same = (row == seg).astype(F32)
        key_mark = jnp.where(row >= 8, 1.0, (same - 1.0) * BIG).astype(BF)

        def unit(h, _):
            r = pl.multiple_of(h * 64, 64)
            hs = pl.ds(r, 64)
            l1, l2, l3 = split3(-lse_ref[g * 3 + h])
            qa[0:64, :] = qkv_ref[g, hs, :]
            qa[64:128, :] = jnp.where(row == 8, l1, jnp.where(row == 9, l2, jnp.where(row == 10, l3, same))).astype(BF)
            ka[...] = jnp.concatenate([qkv_ref[g, pl.ds(r + 192, 64), :], key_mark], axis=0).T
            va[...] = jnp.concatenate([qkv_ref[g, pl.ds(r + 384, 64), :], jnp.ones((64, length), BF)], axis=0).T
            for b in range(4):
                bs = slice(b * BLK, (b + 1) * BLK)
                do = do_ref[g, b, hs, :]
                e1, e2, e3 = split3(-jnp.sum(do.astype(F32) * o_ref[g, b, hs, :].astype(F32), axis=0, keepdims=True))
                da[0:64, bs] = do
                rb = row[:, bs]
                da[64:128, bs] = jnp.where(rb == 8, e1, jnp.where(rb == 9, e2, jnp.where(rb == 10, e3, 0.0))).astype(BF)
            dk[...] = jnp.zeros_like(dk)
            dv[...] = jnp.zeros_like(dv)

            def chunk(n, _):
                cs = pl.ds(pl.multiple_of(n * 512, 512), 512)
                s = jnp.dot(ka[...], qa[:, cs], preferred_element_type=F32)
                p = jnp.exp2(s)
                dp = jnp.dot(va[...], da[:, cs], preferred_element_type=F32)
                pb = p.astype(BF)
                ds = (p * dp).astype(BF)
                dv[...] += dg(da[0:64, cs], pb, 1, 1)
                dk[...] += dg(qa[0:64, cs], ds, 1, 1)
                dq = jnp.dot(qkv_ref[g, pl.ds(r + 192, 64), :], ds, preferred_element_type=F32)
                dq_s[g, hs, cs] = (dq * (HEAD_DIM ** (-0.5))).astype(BF)
                return 0

            lax.fori_loop(0, length // 512, chunk, 0)
            dq_s[g, pl.ds(r + 192, 64), :] = (dk[...] * math.log(2.0)).astype(BF)
            dq_s[g, pl.ds(r + 384, 64), :] = dv[...].astype(BF)
            return 0

        lax.fori_loop(0, 3, unit, 0)

    own_seq = 2 * y
    attend_back(1, own_seq)
    dw_ref[1] = jnp.dot(dq_s[1], xab_ref[0], preferred_element_type=F32).astype(BF)
    attend_back(2, 1)
    attend_back(0, own_seq)
    dw_ref[0] = (
        jnp.dot(dq_s[0], xab_ref[0], preferred_element_type=F32) + jnp.dot(dq_s[2], xab_ref[1], preferred_element_type=F32)
    ).astype(BF)
    db_ref[0] = jnp.broadcast_to(
        jnp.sum(dq_s[0].astype(F32), axis=1, keepdims=True) + jnp.sum(dq_s[2].astype(F32), axis=1, keepdims=True), (576, 128)
    )
    db_ref[1] = jnp.broadcast_to(jnp.sum(dq_s[1].astype(F32), axis=1, keepdims=True), (576, 128))

    def into_x(n, _):
        cs = pl.ds(pl.multiple_of(n * BLK, BLK), BLK)
        ra = dg(dq_s[0, :, cs], wt_ref[...], 0, 0) + dg(dq_s[1, :, cs], wpar_ref[...], 0, 0)
        rb = dg(dq_s[2, :, cs], wt_ref[...], 0, 0)
        pab[0, cs, :] = ra
        pab[1, cs, :] = rb
        sbuf[0, cs, :] = ra.astype(BF)
        sbuf[1, cs, :] = rb.astype(BF)
        return 0

    lax.fori_loop(0, 4, into_x, 0)

    def rows_of(blk):
        return pl.ds(pl.multiple_of(blk * BLK, BLK), BLK)

    base = 9
    outs = []
    for i in range(3):
        middle, blk = block_of(core, i)
        outs.append(
            pltpu.make_async_remote_copy(
                src_ref=sbuf.at[middle, rows_of(blk)], dst_ref=rcore.at[i], send_sem=send.at[base + i],
                recv_sem=recv.at[i], device_id={"tensor": core}, device_id_type=MESH,
            )
        )
    far = 2 * (1 - y)
    outs.append(
        pltpu.make_async_remote_copy(
            src_ref=sbuf.at[1, rows_of(far + 1 - c)], dst_ref=rhalf, send_sem=send.at[base + 3],
            recv_sem=recv.at[3], device_id={"tensor": core}, device_id_type=MESH,
        )
    )
    for copy in reversed(outs):
        copy.start()
    outs[3].wait_recv()
    hsum[...] = (pab[1, rows_of(far + c), :] + rhalf[...].astype(F32)).astype(BF)
    hcopy = pltpu.make_async_remote_copy(
        src_ref=hsum, dst_ref=rmid.at[c], send_sem=send.at[base + 4], recv_sem=recv.at[4 + c],
        device_id={"tensor": 2 * (1 - y) + y}, device_id_type=MESH,
    )
    hcopy.start()
    for i in range(3):
        outs[i].wait_recv()
        middle, blk = block_of(t, i)
        rs = pl.ds(i * BLK, BLK)

        @pl.when(middle == 0)
        def _():
            din_ref[rs, :] = (dz1_ref[rs, :] + pab[0, rows_of(blk), :] + rcore[i].astype(F32)).astype(BF)

        @pl.when(middle == 1)
        def _():
            k = blk % 2
            pltpu.make_async_copy(hsum, rmid.at[k], recv.at[4 + k]).wait()
            din_ref[rs, :] = (
                dz1_ref[rs, :] + pab[1, rows_of(blk), :] + rcore[i].astype(F32) + rmid[k].astype(F32)
            ).astype(BF)

    for copy in outs + [hcopy]:
        copy.wait_send()
    for cond, copy in pending:
        if cond is None:
            copy.wait_send()
        else:
            pl.when(cond)(copy.wait_send)


def vm(*shape, dtype=BF):
    return pltpu.VMEM(shape, dtype)


def sds(*shape, dtype=BF):
    return jax.ShapeDtypeStruct(shape, dtype)


VM = pl.BlockSpec(memory_space=pltpu.VMEM)
ANY = pl.BlockSpec(memory_space=pl.ANY)


def params(cid):
    return pltpu.CompilerParams(collective_id=cid, has_side_effects=True, vmem_limit_bytes=62 * 2**20)


def local_step(
    layer_input, segment_ids, w_query, b_query, w_key, w_value, b_value, w_out, b_out, first_gain, first_shift,
    w_in, b_in, w_back, b_back, second_gain, second_shift, cotangent,
):
    seg = segment_ids.reshape(3, 1, 1024)
    wt = jnp.concatenate([w_query, w_key, w_value], axis=1).T
    zeros = jnp.zeros((192,), F32)
    bias = jnp.stack([b_in.astype(F32), jnp.concatenate([b_query.astype(F32), zeros, b_value.astype(F32), zeros])])
    bias = jnp.concatenate([bias, jnp.zeros((6, 768), F32)])
    vec = jnp.stack([b_out, first_gain, first_shift, b_back, second_gain, second_shift])
    vec = jnp.concatenate([vec, jnp.zeros((2, 768), F32)])
    dma = pltpu.SemaphoreType.DMA

    qkv, o, lse, xab, wpar, woutg, wing, biasg = pl.pallas_call(
        k1,
        out_shape=(
            sds(3, 576, 1024), sds(3, 4, 192, BLK), sds(9, 1, 1024, dtype=F32), sds(2, 1024, 768), sds(576, 768),
            sds(3, 192, 768), sds(3, 768, 768), sds(3, 8, 768, dtype=F32),
        ),
        in_specs=[ANY, ANY, VM, VM, ANY, ANY],
        out_specs=(VM, VM, VM, VM, VM, ANY, ANY, VM),
        scratch_shapes=[vm(576, 768), vm(128, 1024), vm(1024, 128), vm(80, 1024), dma((24,)), dma((24,)), dma((4,))],
        compiler_params=params(0),
        name="attention_forward",
    )(layer_input, wt, bias, seg, w_out, w_in)

    out, dz1, do, g, small, _ = pl.pallas_call(
        lambda *r: k2(*r[:16], *r[17:20], r[20], r[16], *r[21:]),
        out_shape=(
            sds(768, 768), sds(768, 768, dtype=F32), sds(3, 768, BLK), sds(4, 1728, 768), sds(16, 768, dtype=F32),
            sds(3, 768, 768),
        ),
        in_specs=[VM, VM, VM, VM, VM, ANY, ANY, ANY, ANY, ANY, ANY],
        out_specs=(VM, VM, VM, VM, VM, ANY),
        scratch_shapes=[
            vm(3, 768, BLK), vm(768, 768), vm(768, 3072), vm(3072, 768),
            vm(768, 768), vm(768, 768), vm(768, 768, dtype=F32), vm(768, 1, dtype=F32), vm(768, 3072), vm(768, 3072),
            vm(768, 768, dtype=F32), vm(768, 768), vm(768, 768), vm(768, 768, dtype=F32),
            dma((34,)), dma((34,)), dma((12,)),
        ],
        compiler_params=params(1),
        name="feed_forward",
    )(layer_input, cotangent, vec, bias, biasg, o, w_out, woutg, w_in, wing, w_back)

    din, dw, db = pl.pallas_call(
        k3,
        out_shape=(sds(768, 768), sds(2, 576, 768), sds(2, 576, 128, dtype=F32)),
        in_specs=[VM, VM, VM, VM, VM, VM, VM, ANY, VM],
        out_specs=(VM, VM, VM),
        scratch_shapes=[
            vm(3, 4, 192, BLK), vm(3, 576, 1024), vm(128, 1024), vm(1024, 128), vm(1024, 128), vm(128, 1024),
            vm(64, 1024, dtype=F32), vm(64, 1024, dtype=F32), vm(2, 1024, 768, dtype=F32), vm(2, 1024, 768),
            vm(3, BLK, 768), vm(2, BLK, 768), vm(BLK, 768), vm(BLK, 768), dma((14,)), dma((6,)), dma((12,)),
        ],
        compiler_params=params(2),
        name="attention_backward",
    )(qkv, seg, o, lse, xab, wt, wpar, do, dz1)

    def core_swap(v):
        return lax.ppermute(v, "tensor", [(0, 1), (1, 0), (2, 3), (3, 2)])

    def across_swap(v):
        return lax.ppermute(v, "tensor", [(0, 2), (2, 0), (1, 3), (3, 1)])

    bi = small[8:12]
    r1, r3 = core_swap(g[1]), core_swap(g[3])
    p2 = (g[2].astype(F32) + r3.astype(F32)).astype(BF)
    p0 = g[0].astype(F32) + r1.astype(F32) + across_swap(p2).astype(F32)
    pq = dw[0].astype(F32) + across_swap(dw[1]).astype(F32)
    bi0 = bi[0] + core_swap(bi[1])
    bi2 = bi[2] + core_swap(bi[3])
    bi = bi0 + across_swap(bi2)
    bq = db[0, :, 0] + across_swap(db[1, :, 0])
    big = lax.psum((p0.astype(BF), pq.astype(BF)), "dp")
    bi, bq = lax.psum((bi, bq), "dp")
    shared = lax.psum(small[0:6], ("dp", "tensor"))
    gw, gq = big
    gw = gw.astype(F32)
    gq = gq.astype(F32)
    return (
        out, din, gq[0:192].T, bq[0:192], gq[192:384].T, gq[384:576].T, bq[384:576], gw[1536:1728],
        shared[0], shared[1], shared[2], gw[0:768], bi, gw[768:1536].T, shared[3], shared[4], shared[5],
    )


def solution(mesh):
    rows = P(("dp", "tensor"), None)
    in_specs = (
        rows, P("dp", None), P(None, "tensor"), P("tensor"), P(None, "tensor"), P(None, "tensor"), P("tensor"),
        P("tensor", None), P(), P(), P(), P(None, "tensor"), P("tensor"), P("tensor", None), P(), P(), P(), rows,
    )
    out_specs = (
        rows, rows, P(None, "tensor"), P("tensor"), P(None, "tensor"), P(None, "tensor"), P("tensor"),
        P("tensor", None), P(), P(), P(), P(None, "tensor"), P("tensor"), P("tensor", None), P(), P(), P(),
    )
    return jax.shard_map(local_step, mesh=mesh, in_specs=in_specs, out_specs=out_specs, check_vma=False)
```

```python
import math
from functools import partial

import jax
import jax.numpy as jnp
from jax import lax
from jax.experimental import pallas as pl
from jax.experimental.pallas import tpu as pltpu
from jax.sharding import PartitionSpec as P

F32 = jnp.float32
BF = jnp.bfloat16
MESH = pl.DeviceIdType.MESH
HEAD_DIM = 64
EPSILON = 1e-05
BIG = 1e30
LOG2E = 1.0 / math.log(2.0)
QSCALE = HEAD_DIM ** (-0.5) * LOG2E
BLK = 256
IN_EARLY = 1
Y_EARLY = 1
UNIT_STEPS = {
    2: (("after_x", 0),),
    3: (("after_y", 2),),
    4: (("after_x", 1), ("after_end", 0)),
    6: (("after_y", 3), ("after_x", 2), ("after_end", 1), ("after_mate", 0)),
    8: (("after_y", 4), ("after_x", 3), ("after_end", 2), ("after_mate", 1)),
}
TAIL_INPUT = 7
TAIL_STEPS = (
    ("after_y", "p5"), ("after_x", "p4"), ("after_end", "p3"), ("after_mate", "p2"),
    ("after_y", "w0"), ("after_x", "p5"), ("after_end", "p4"), ("after_mate", "p3"),
    ("after_y", "w1"), ("after_x", "w0"), ("after_end", "p5"), ("after_mate", "p4"),
    ("after_y", "w2"), ("after_x", "w1"), ("after_end", "w0"), ("after_mate", "p5"),
    ("after_y", "w3"), ("after_y", "t"), ("after_x", "w2"), ("after_end", "w1"), ("after_mate", "w0"),
    ("after_x", "w3"), ("after_x", "t"), ("after_end", "w2"), ("after_mate", "w1"),
    ("after_end", "w3"), ("after_end", "t"), ("after_mate", "w2"),
    ("after_mate", "w3"), ("after_mate", "t"),
)


def dg(a, b, ca, cb):
    return lax.dot_general(a, b, (((ca,), (cb,)), ((), ())), preferred_element_type=F32)


def where_am_i():
    t = lax.axis_index("tensor")
    d = lax.axis_index("dp")
    core = t + 1 - 2 * (t % 2)
    across = (t + 2) % 4
    diag = 3 - t
    side = d + 1 - 2 * (d % 2)
    return t, d, core, across, diag, side


def block_of(t, i):
    b = 3 * t + i
    middle = (b // 4) % 2
    return middle, b % 4


def greet(devices):
    barrier = pltpu.get_barrier_semaphore()
    for dev in devices:
        pl.semaphore_signal(barrier, inc=1, device_id=dev, device_id_type=MESH)
    pl.semaphore_wait(barrier, len(devices))


def half_rows(half, total, pieces, i):
    n = total // 2 // pieces
    return pl.ds(pl.multiple_of(half * (total // 2) + i * n, n), n)


class Copies:
    def __init__(self, send, recv):
        self.send, self.recv, self.used = send, recv, 0

    def new(self, src, dst, **device):
        k = self.used
        self.used += 1
        return pltpu.make_async_remote_copy(
            src_ref=src,
            dst_ref=dst,
            send_sem=self.send.at[k],
            recv_sem=self.recv.at[k],
            device_id=device,
            device_id_type=MESH,
        )


def start_all(copies):
    for copy in copies:
        copy.start()


def k1(
    x_ref, wt_ref, bias_ref, seg_ref, wout_ref, win_ref,
    qkv_out, o_out, lse_ref, xab_out, wpar_out, woutg_ref, wing_ref, biasg_ref,
    qkv, o_v, xab, w_v, bcol, qa, ka, va, send, recv, local,
):
    length = 1024
    t, d, core, across, diag, side = where_am_i()
    y, c = t // 2, t % 2
    half = d % 2
    greet([{"tensor": core}, {"tensor": across}, {"tensor": diag}, {"dp": side}])
    cp = Copies(send, recv)
    rows_out, rows_local = [], []
    for i in range(3):
        middle, blk = block_of(t, i)
        src = x_ref.at[pl.ds(i * BLK, BLK)]
        dst = xab.at[middle, pl.ds(pl.multiple_of(blk * BLK, BLK), BLK)]
        rows_local.append(pltpu.make_async_copy(src, dst, local.at[i]))
        rows_out.append(cp.new(src, dst, tensor=core))
    w_local = pltpu.make_async_copy(wt_ref, w_v.at[0], local.at[3])
    cross_in = 2 * (1 - y) + c
    cross_slot = pl.ds(pl.multiple_of(cross_in * BLK, BLK), BLK)
    mixed = (t == 1) | (t == 2)
    first_middle = jnp.where(t == 1, 1, 0)
    cross_out = []
    base = cp.used
    for k in range(2):
        src = x_ref.at[pl.ds(pl.multiple_of((first_middle + k) * BLK, BLK), BLK)]
        dst = xab.at[1, pl.ds(pl.multiple_of((2 * y + k) * BLK, BLK), BLK)]
        cross_out.append(
            pltpu.make_async_remote_copy(
                src_ref=src, dst_ref=dst, send_sem=send.at[base + k], recv_sem=recv.at[base],
                device_id={"tensor": 2 * (1 - y) + k}, device_id_type=MESH,
            )
        )
    cp.used += 2
    cross_arrived = pltpu.make_async_remote_copy(
        src_ref=x_ref.at[pl.ds(0, BLK)], dst_ref=xab.at[1, cross_slot], send_sem=send.at[base],
        recv_sem=recv.at[base], device_id={"tensor": core}, device_id_type=MESH,
    )
    cross_forward = cp.new(xab.at[1, cross_slot], xab.at[1, cross_slot], tensor=core)
    wp_first, wp_second = [], []
    for i in range(3):
        part = half_rows(half, 576, 3, i)
        wp_first.append(cp.new(wt_ref.at[part], w_v.at[1, part], tensor=across))
        wp_second.append(cp.new(w_v.at[1, part], w_v.at[1, part], dp=side))
    bias_out = [
        cp.new(bias_ref, biasg_ref.at[0], tensor=core),
        cp.new(bias_ref, biasg_ref.at[1], tensor=across),
        cp.new(bias_ref, biasg_ref.at[2], tensor=diag),
    ]
    part = half_rows(half, 192, 1, 0)
    wo_first = cp.new(wout_ref.at[part], woutg_ref.at[1, part], tensor=across)
    wo_second = cp.new(woutg_ref.at[1, part], woutg_ref.at[1, part], dp=side)
    wo_core = cp.new(wout_ref, woutg_ref.at[0], tensor=core)
    wo_diag = cp.new(woutg_ref.at[1], woutg_ref.at[2], tensor=core)
    wi_first, wi_second, wi_diag = [], [], []
    for i in range(IN_EARLY):
        part = half_rows(half, 768, 3, i)
        wi_first.append(cp.new(win_ref.at[part], wing_ref.at[0, part], tensor=across))
        wi_second.append(cp.new(wing_ref.at[0, part], wing_ref.at[0, part], dp=side))
        for h in range(2):
            both = half_rows(h, 768, 3, i)
            wi_diag.append(cp.new(wing_ref.at[0, both], wing_ref.at[1, both], tensor=core))

    start_all(rows_local + [w_local] + rows_out)
    start_all(bias_out)

    @pl.when(mixed)
    def _():
        start_all(cross_out)

    start_all(wp_first)
    start_all([wo_core, wo_first] + wi_first)

    row64 = lax.broadcasted_iota(jnp.int32, (64, length), 0)
    va[64:80, :] = jnp.ones((16, length), BF)
    factor = jnp.where(lax.broadcasted_iota(jnp.int32, (576, 1), 0) % 192 < 64, QSCALE, 1.0)

    def outgoing(g):
        return [
            pltpu.make_async_copy(qkv.at[g], qkv_out.at[g], local.at[4 + 2 * (g % 3)]),
            pltpu.make_async_copy(o_v.at[g], o_out.at[g], local.at[5 + 2 * (g % 3)]),
        ]

    def at(u, k, copies_recv, copies_start=()):
        @pl.when(u == k)
        def _():
            for copy in copies_recv:
                copy.wait_recv()
            start_all(copies_start)

    def unit(u, _):
        g = (2 * (u // 3)) % 3
        h = u % 3
        par = jnp.where(g == 1, 1, 0)
        middle = jnp.where(g == 2, 1, 0)

        @pl.when(u == 3)
        def _():
            cross_arrived.wait_recv()
            cross_forward.start()
            cross_forward.wait_recv()

        at(u, 4, [wp_first[0]], [wp_second[0]])
        at(u, 5, [wp_first[1]], [wp_second[1]])
        at(u, 6, [wp_first[2]], [wp_second[2]])
        at(u, 6, wp_second + [bias_out[1]])
        at(u, 8, [wo_first], [wo_second])

        @pl.when(h == 0)
        def _():
            @pl.when(u > 0)
            def _():
                start_all(outgoing(jnp.where(g == 2, 0, 2)))

            @pl.when(par == 0)
            def _():
                bcol[...] = jnp.transpose(bias_ref[...])[0:576, 1:2]

            @pl.when(par == 1)
            def _():
                bcol[...] = jnp.transpose(biasg_ref[1])[0:576, 1:2]

            col = bcol[...]

            def body(n, _):
                cs = pl.ds(pl.multiple_of(n * BLK, BLK), BLK)
                r = (dg(w_v[par], xab[middle, cs, :], 1, 1) + col) * factor
                for k in range(3):
                    qkv[g, k, :, cs] = r[192 * k : 192 * (k + 1)].astype(BF)
                return 0

            lax.fori_loop(0, length // BLK, body, 0)
            same = (row64 == seg_ref[jnp.where(g == 2, 1, 2 * y)]).astype(F32)
            qa[64:128, :] = same.astype(BF)
            ka[64:128, :] = ((same - 1.0) * BIG).astype(BF)

        qa[0:64, :] = qkv[g, h, 0:64, :]
        ka[0:64, :] = qkv[g, h, 64:128, :]
        va[0:64, :] = qkv[g, h, 128:192, :]
        s = jnp.dot(ka[...].T, qa[...], preferred_element_type=F32)
        m = jnp.max(s, axis=0, keepdims=True)
        p = jnp.exp2(s - m).astype(BF)
        o = jnp.dot(va[...], p, preferred_element_type=F32)
        total = o[64:65, :]
        res = (o[0:64] * (1.0 / total)).astype(BF)
        hs = pl.ds(pl.multiple_of(h * 64, 64), 64)
        for b in range(4):
            o_v[g, b, hs, :] = res[:, b * BLK : (b + 1) * BLK]
        lse_ref[g * 3 + h] = m + jnp.log2(total)
        return 0

    for copy in rows_local + [w_local]:
        copy.wait()
    for copy in rows_out:
        copy.wait_recv()
    lax.fori_loop(0, 9, unit, 0)
    tail = outgoing(1)
    tail.append(pltpu.make_async_copy(xab, xab_out, local.at[0]))
    tail.append(pltpu.make_async_copy(w_v.at[1], wpar_out, local.at[1]))
    start_all(tail)
    for i in range(IN_EARLY):
        wi_first[i].wait_recv()
        wi_second[i].start()
    wo_second.wait_recv()
    wo_diag.start()
    for i in range(IN_EARLY):
        wi_second[i].wait_recv()
        start_all(wi_diag[2 * i : 2 * i + 2])
    for copy in [bias_out[0], bias_out[2], wo_core, wo_diag] + wi_diag:
        copy.wait_recv()
    for copy in outgoing(0) + outgoing(2) + tail:
        copy.wait()
    sent = rows_out + [cross_forward] + wp_first + wp_second + bias_out + [wo_first, wo_second, wo_core, wo_diag]
    for copy in sent + wi_first + wi_second + wi_diag:
        copy.wait_send()

    @pl.when(mixed)
    def _():
        for copy in cross_out:
            copy.wait_send()

def layer_stats(z):
    mean = jnp.mean(z, axis=-1, keepdims=True)
    cen = z - mean
    var = jnp.mean(cen * cen, axis=-1, keepdims=True)
    inv = lax.rsqrt(var + EPSILON)
    return cen * inv, inv


def k2(
    x_ref, cot_ref, vec_ref, bias_ref, biasg_ref, o_ref, wout_ref, woutg_ref, win_ref, wing_ref, wback_ref,
    out_ref, dz1_ref, do_ref, gf_ref, go_ref, small_ref,
    ot, wo, wi, wb, h1b, h1t, xh1, inv1, gg, gp, z2, dz2b, dz2t, gsend, rc, ry, send, recv, local,
):
    t, d, core, across, diag, side = where_am_i()
    half = d % 2
    greet([{"tensor": core}, {"tensor": across}, {"tensor": diag}, {"dp": side}])

    peers = (t, core, across, diag)
    pending = []
    for j, dev in enumerate(peers):
        for i in range(3):
            middle, blk = block_of(dev, i)
            for second in (False, True) if j < 2 else (False,):
                slot = j + 2 if second else j
                src = o_ref.at[1 if second else 2 * middle, blk]
                dst = ot.at[i, pl.ds(slot * 192, 192)]
                sem = recv.at[i * 4 + slot]
                if j == 0:
                    copy = pltpu.make_async_copy(src, dst, sem)
                else:
                    k = 3 * (j - 1) + i if not second else 9 + i
                    copy = pltpu.make_async_remote_copy(
                        src_ref=src, dst_ref=dst, send_sem=send.at[k], recv_sem=sem,
                        device_id={"tensor": dev}, device_id_type=MESH,
                    )
                if second:
                    cond = middle == 0
                else:
                    cond = None if j < 2 else middle == 1
                if cond is None:
                    copy.start()
                else:
                    pl.when(cond)(copy.start)
                if j:
                    pending.append((cond, copy))
    cp = Copies(send, recv)
    cp.used = 12

    def lanes(j):
        return pl.ds(768 * j, 768)

    in_core = cp.new(win_ref, wi.at[:, lanes(1)], tensor=core)
    in_first, in_second, in_diag, loads_in = [], [], [], [pltpu.make_async_copy(win_ref, wi.at[:, lanes(0)], local.at[4])]
    for i in range(IN_EARLY, 3):
        part = half_rows(half, 768, 3, i)
        in_first.append(cp.new(win_ref.at[part], wi.at[part, lanes(2)], tensor=across))
        in_second.append(cp.new(wi.at[part, lanes(2)], wi.at[part, lanes(2)], dp=side))
        for h in range(2):
            both = half_rows(h, 768, 3, i)
            in_diag.append(cp.new(wi.at[both, lanes(2)], wi.at[both, lanes(3)], tensor=core))
    for i in range(IN_EARLY):
        for h in range(2):
            part = half_rows(h, 768, 3, i)
            for k in range(2):
                loads_in.append(pltpu.make_async_copy(wing_ref.at[k, part], wi.at[part, lanes(2 + k)], local.at[4 + len(loads_in)]))
    back_core = cp.new(wback_ref, wb.at[lanes(1)], tensor=core)
    back_first, back_second, back_diag = [], [], []
    for i in range(3):
        part = half_rows(half, 768, 3, i)
        place = half_rows(half, 768, 3, i)
        place = pl.ds(place.start + 2 * 768, place.size)
        back_first.append(cp.new(wback_ref.at[part], wb.at[place], tensor=across))
        back_second.append(cp.new(wb.at[place], wb.at[place], dp=side))
        for h in range(2):
            n = h * 384 + i * 128
            back_diag.append(cp.new(wb.at[pl.ds(2 * 768 + n, 128)], wb.at[pl.ds(3 * 768 + n, 128)], tensor=core))
    load_b0 = pltpu.make_async_copy(wback_ref, wb.at[lanes(0)], local.at[4 + len(loads_in)])
    start_all(in_first + [in_core, back_core] + back_first)
    loads = [pltpu.make_async_copy(wout_ref, wo.at[pl.ds(0, 192)], local.at[0])]
    loads += [pltpu.make_async_copy(woutg_ref.at[j], wo.at[pl.ds(192 * (j + 1), 192)], local.at[j + 1]) for j in range(3)]
    start_all(loads + loads_in + [load_b0])

    b_out, gain1, shift1, b_back, gain2, shift2 = [vec_ref[k : k + 1, :] for k in range(6)]
    for copy in loads:
        copy.wait()
    for i in range(3):
        for slot in range(4):
            pltpu.make_async_copy(o_ref.at[0, 0], ot.at[i, pl.ds(slot * 192, 192)], recv.at[i * 4 + slot]).wait()

    def first(i, _):
        rs = pl.ds(pl.multiple_of(i * BLK, BLK), BLK)
        z = x_ref[rs, :].astype(F32) + dg(ot[i], wo[...], 0, 0) + b_out
        xh, inv = layer_stats(z)
        xh1[rs, :] = xh
        inv1[rs, :] = inv
        h1b[rs, :] = (xh * gain1 + shift1).astype(BF)
        return 0

    lax.fori_loop(0, 3, first, 0)
    h1t[...] = h1b[...].T
    for copy in loads_in:
        copy.wait()

    def at(n, k, copies_recv, copies_start=()):
        @pl.when(n == k)
        def _():
            for copy in copies_recv:
                copy.wait_recv()
            start_all(copies_start)

    late = len(in_first)

    def up(n, _):
        at(n, 2, in_first[:1], in_second[:1])
        at(n, 3, [in_core])
        if late > 1:
            at(n, 4, in_first[1:], in_second[1:])
        at(n, 6, in_second, in_diag)
        at(n, 7, [back_first[0]], [back_second[0]])
        at(n, 9, in_diag)
        at(n, 9, [back_first[1]], [back_second[1]])
        at(n, 11, [back_first[2]], [back_second[2]])
        cs = pl.ds(pl.multiple_of(n * BLK, BLK), BLK)
        j = n // 3
        low = pl.ds(pl.multiple_of((n % 3) * BLK, BLK), BLK)
        bias = jnp.where(j == 0, bias_ref[0:1, low], biasg_ref[jnp.maximum(j - 1, 0), 0:1, low])
        u = jnp.dot(h1b[...], wi[:, cs], preferred_element_type=F32) + bias
        cdf = 0.5 * (1.0 + lax.erf(u * (2.0 ** -0.5)))
        pdf = jnp.exp(-0.5 * u * u) * (1.0 / math.sqrt(2.0 * math.pi))
        gg[:, cs] = (u * cdf).astype(BF)
        gp[:, cs] = (cdf + u * pdf).astype(BF)
        return 0

    lax.fori_loop(0, 12, up, 0)
    for i in range(3):
        back_second[i].wait_recv()
        start_all(back_diag[2 * i : 2 * i + 2])
    back_core.wait_recv()
    load_b0.wait()
    for copy in back_diag:
        copy.wait_recv()

    def down(n, _):
        cs = pl.ds(pl.multiple_of(n * BLK, BLK), BLK)
        z2[:, cs] = jnp.dot(gg[...], wb[:, cs], preferred_element_type=F32)
        return 0

    lax.fori_loop(0, 3, down, 0)

    def second_norm(i, sums):
        rs = pl.ds(pl.multiple_of(i * BLK, BLK), BLK)
        h1 = xh1[rs, :] * gain1 + shift1
        xh, inv = layer_stats(h1 + z2[rs, :] + b_back)
        out_ref[rs, :] = (xh * gain2 + shift2).astype(BF)
        cot = cot_ref[rs, :].astype(F32)
        dxh = cot * gain2
        dz = inv * (dxh - jnp.mean(dxh, axis=-1, keepdims=True) - xh * jnp.mean(dxh * xh, axis=-1, keepdims=True))
        z2[rs, :] = dz
        dz2b[rs, :] = dz.astype(BF)
        return (
            sums[0] + jnp.sum(dz, axis=0, keepdims=True),
            sums[1] + jnp.sum(cot * xh, axis=0, keepdims=True),
            sums[2] + jnp.sum(cot, axis=0, keepdims=True),
        )

    zero = jnp.zeros((1, 768), F32)
    s3, s4, s5 = lax.fori_loop(0, 3, second_norm, (zero, zero, zero))
    small_ref[3:4, :] = s3
    small_ref[4:5, :] = s4
    small_ref[5:6, :] = s5
    dz2t[...] = dz2b[...].T

    base = cp.used

    def to_core(stage, ch):
        k = base + stage * 3 + ch
        return pltpu.make_async_remote_copy(
            src_ref=gsend.at[stage, ch], dst_ref=rc.at[stage, ch], send_sem=send.at[k], recv_sem=recv.at[k],
            device_id={"tensor": core}, device_id_type=MESH,
        )

    def to_across(ch):
        k = base + 6 + ch
        return pltpu.make_async_remote_copy(
            src_ref=gf_ref.at[1, ch], dst_ref=ry.at[ch], send_sem=send.at[k], recv_sem=recv.at[k],
            device_id={"tensor": across}, device_id_type=MESH,
        )

    def back(m, _):
        stage = m // 6
        ch = (m % 6) // 2
        slot = 3 - 2 * stage - m % 2
        n = slot * 3 + ch
        cs = pl.ds(pl.multiple_of(n * BLK, BLK), BLK)
        low = pl.ds(pl.multiple_of(ch * BLK, BLK), BLK)
        g_back = jnp.dot(dz2t[...], gg[:, cs], preferred_element_type=F32)
        du = (dg(dz2b[...], wb[cs, :], 1, 1) * gp[:, cs].astype(F32)).astype(BF)
        gg[:, cs] = du
        small_ref[pl.ds(8 + slot, 1), low] = jnp.sum(du.astype(F32), axis=0, keepdims=True)
        g_in = jnp.dot(h1t[...], du, preferred_element_type=F32)

        @pl.when(m % 2 == 0)
        def _():
            gsend[stage, ch, 0] = g_in.astype(BF)
            gsend[stage, ch, 1] = g_back.astype(BF)
            to_core(stage, ch).start()

        @pl.when(m % 2 == 1)
        def _():
            to_core(stage, ch).wait_recv()
            gf_ref[1 - stage, ch, 0] = (g_in + rc[stage, ch, 0].astype(F32)).astype(BF)
            gf_ref[1 - stage, ch, 1] = (g_back + rc[stage, ch, 1].astype(F32)).astype(BF)
            pl.when((stage == 0) & (ch < Y_EARLY))(to_across(ch).start)

        return 0

    lax.fori_loop(0, 12, back, 0)

    def into_h(n, _):
        cs = pl.ds(pl.multiple_of(n * BLK, BLK), BLK)
        z2[:, cs] += dg(gg[...], wi[cs, :], 1, 1)
        return 0

    lax.fori_loop(0, 3, into_h, 0)

    def first_norm(i, sums):
        rs = pl.ds(pl.multiple_of(i * BLK, BLK), BLK)
        dh = z2[rs, :]
        xh = xh1[rs, :]
        dxh = dh * gain1
        dz = inv1[rs, :] * (dxh - jnp.mean(dxh, axis=-1, keepdims=True) - xh * jnp.mean(dxh * xh, axis=-1, keepdims=True))
        dz1_ref[rs, :] = dz
        dzb = dz.astype(BF)
        dz2b[rs, :] = dzb
        do_ref[i] = dg(wo[...], dzb, 1, 1).astype(BF)
        return (
            sums[0] + jnp.sum(dz, axis=0, keepdims=True),
            sums[1] + jnp.sum(dh * xh, axis=0, keepdims=True),
            sums[2] + jnp.sum(dh, axis=0, keepdims=True),
        )

    s0, s1, s2 = lax.fori_loop(0, 3, first_norm, (zero, zero, zero))
    small_ref[0:1, :] = s0
    small_ref[1:2, :] = s1
    small_ref[2:3, :] = s2
    for j in range(4):
        rows = pl.ds(192 * j, 192)
        acc = jnp.dot(ot[0, rows, :], dz2b[0:BLK, :], preferred_element_type=F32)
        acc += jnp.dot(ot[1, rows, :], dz2b[BLK : 2 * BLK, :], preferred_element_type=F32)
        acc += jnp.dot(ot[2, rows, :], dz2b[2 * BLK : 3 * BLK, :], preferred_element_type=F32)
        go_ref[j] = acc.astype(BF)
    small_ref[6:8, :] = jnp.zeros((2, 768), F32)
    small_ref[12:16, :] = jnp.zeros((4, 768), F32)

    for cond, copy in pending:
        if cond is None:
            copy.wait_send()
        else:
            pl.when(cond)(copy.wait_send)
    sent = [in_core, back_core] + in_first + in_second + in_diag + back_first + back_second + back_diag
    for copy in sent + [to_core(s, ch) for s in range(2) for ch in range(3)]:
        copy.wait_send()
    for ch in range(Y_EARLY):
        to_across(ch).wait_recv()
        for k in range(2):
            gf_ref[0, ch, k] = (gf_ref[0, ch, k].astype(F32) + ry[ch, k].astype(F32)).astype(BF)
        to_across(ch).wait_send()

def split3(v):
    a = v.astype(BF).astype(F32)
    b = (v - a).astype(BF).astype(F32)
    return a, b, v - a - b


class Piece:
    def __init__(self, value, other, from_y, from_x, from_end, from_mate, final, send, recv, where, fold=None):
        self.value, self.other, self.final = value, other, final
        self.from_y, self.from_x, self.from_end, self.from_mate = from_y, from_x, from_end, from_mate
        self.send, self.recv, self.where, self.fold = send, recv, where, fold

    def copy(self, stage, src, dst, **device):
        return pltpu.make_async_remote_copy(
            src_ref=src, dst_ref=dst, send_sem=self.send.at[stage], recv_sem=self.recv.at[stage],
            device_id=device, device_id_type=MESH,
        )

    def to_y(self):
        return self.copy(0, self.other, self.from_y, tensor=self.where["across"])

    def to_x(self):
        return self.copy(1, self.value, self.from_x, dp=self.where["side"])

    def to_inner(self):
        return self.copy(2, self.value, self.from_end, dp=self.where["pair"])

    def to_mate(self):
        return self.copy(3, self.value, self.from_mate, dp=self.where["mate"])

    def to_end(self):
        return self.copy(4, self.final, self.final, dp=self.where["pair"])

    def add(self, arrived, into):
        into[...] = (self.value[...].astype(F32) + arrived[...].astype(F32)).astype(into.dtype)

    def after_y(self):
        self.to_y().wait_recv()
        if self.fold is None:
            self.add(self.from_y, self.value)
        else:
            self.fold(self)
        self.begin_x()

    def begin_x(self):
        if self.where["line"]:
            self.to_x().start()
        else:
            self.final[...] = self.value[...]

    def after_x(self):
        if not self.where["line"]:
            return
        self.to_x().wait()
        self.add(self.from_x, self.value)
        pl.when(self.where["end"])(lambda: self.to_inner().start())

    def after_end(self):
        if not self.where["line"]:
            return

        @pl.when(self.where["inner"])
        def _():
            self.to_inner().wait_recv()
            self.add(self.from_end, self.value)
            self.to_mate().start()

    def after_mate(self):
        if not self.where["line"]:
            return

        @pl.when(self.where["inner"])
        def _():
            self.to_mate().wait_recv()
            self.add(self.from_mate, self.final)
            self.to_end().start()

    def finish(self, had_y=True):
        if had_y:
            self.to_y().wait_send()
        if not self.where["line"]:
            return

        @pl.when(self.where["end"])
        def _():
            self.to_end().wait_recv()
            self.to_inner().wait_send()

        @pl.when(self.where["inner"])
        def _():
            self.to_mate().wait_send()
            self.to_end().wait_send()


def k3(
    line,
    qkv_ref, seg_ref, o_ref, lse_ref, xab_ref, wt_ref, wpar_ref, do_in, dz1_in, gf_ref, go_ref, small_ref,
    din_ref, ff_ref, fs_ref, sm_ref,
    dz1_ref, do_ref, dq_s, qa, ka, va, da, dk, dv, sbuf, rcore, rmid, rhalf, hsum,
    fv, fy, fx, fe, fm, sv, so, sy, sx, se, sm, rgo, tv, to, tc, ty, tx, te, tm,
    psend, precv, send, recv, landed, local,
):
    length = 1024
    t, d, core, across, diag, side = where_am_i()
    y, c = t // 2, t % 2
    where = {"across": across, "side": side, "line": line}
    known = [{"tensor": core}, {"tensor": across}, {"tensor": diag}]
    if line:
        z = d // 2
        where["pair"] = d + 2 - 4 * (z % 2)
        where["mate"] = d + 2 - 4 * ((z + 1) % 2)
        where["end"] = (z == 0) | (z == 3)
        where["inner"] = (z == 1) | (z == 2)
        known += [{"dp": side}, {"dp": where["pair"]}]
    barrier = pltpu.get_barrier_semaphore()
    for dev in known:
        pl.semaphore_signal(barrier, inc=1, device_id=dev, device_id_type=MESH)
    if line:
        @pl.when(where["inner"])
        def _():
            pl.semaphore_signal(barrier, inc=1, device_id={"dp": where["mate"]}, device_id_type=MESH)
            pl.semaphore_wait(barrier, len(known) + 1)

        @pl.when(where["end"])
        def _():
            pl.semaphore_wait(barrier, len(known))
    else:
        pl.semaphore_wait(barrier, len(known))

    pending = []
    peers = (t, core, across, diag)
    for i in range(3):
        middle, blk = block_of(t, i)
        for j, dev in enumerate(peers):
            src = do_in.at[i, pl.ds(192 * j, 192)]
            group = jnp.where(middle == 1, 2, j // 2)
            dst = do_ref.at[group, blk]
            sem = landed.at[group * 4 + blk]
            if j == 0:
                pltpu.make_async_copy(src, dst, sem).start()
                continue
            if j == 2:
                pl.when(middle == 0)(pltpu.make_async_copy(src, dst, sem).start)
                dev_to, cond = across, middle == 1
            elif j == 1:
                dev_to, cond = core, None
            else:
                dev_to, cond = jnp.where(middle == 1, diag, core), None
            copy = pltpu.make_async_remote_copy(
                src_ref=src, dst_ref=dst, send_sem=send.at[i * 3 + j - 1], recv_sem=sem,
                device_id={"tensor": dev_to}, device_id_type=MESH,
            )
            if cond is None:
                copy.start()
            else:
                pl.when(cond)(copy.start)
            pending.append((cond, copy))

    loads = [pltpu.make_async_copy(gf_ref.at[0, p // 2, p % 2], fv.at[p], local.at[p]) for p in range(6)]
    loads.append(pltpu.make_async_copy(dz1_in, dz1_ref, local.at[6]))
    start_all(loads)
    go_core = [
        pltpu.make_async_remote_copy(
            src_ref=go_ref.at[2 * k + 1], dst_ref=rgo.at[k], send_sem=send.at[9 + k], recv_sem=recv.at[6 + k],
            device_id={"tensor": core}, device_id_type=MESH,
        )
        for k in range(2)
    ]
    small_core = pltpu.make_async_remote_copy(
        src_ref=small_ref, dst_ref=tc, send_sem=send.at[11], recv_sem=recv.at[8],
        device_id={"tensor": core}, device_id_type=MESH,
    )
    start_all(go_core + [small_core])
    big = [
        Piece(fv.at[p], gf_ref.at[1, p // 2, p % 2], fy.at[p], fx.at[p], fe.at[p], fm.at[p], ff_ref.at[p],
              psend.at[p], precv.at[p], where)
        for p in range(6)
    ]
    thin = [
        Piece(sv.at[p], so.at[p], sy.at[p], sx.at[p], se.at[p], sm.at[p], fs_ref.at[p],
              psend.at[6 + p], precv.at[6 + p], where)
        for p in range(4)
    ]

    def fold_small(piece):
        got = ty[...]
        add = jnp.concatenate([got[0:8], got[10:11], jnp.zeros((3, 768), F32), got[13:14], jnp.zeros((3, 768), F32)])
        tv[...] = tv[...] + add

    tiny = Piece(tv, to, ty, tx, te, tm, sm_ref, psend.at[10], precv.at[10], where, fold_small)
    early = 2 * Y_EARLY
    for p in range(early, 6):
        big[p].to_y().start()
    for copy in loads:
        copy.wait()
    for p in range(early):
        big[p].begin_x()

    row64 = lax.broadcasted_iota(jnp.int32, (64, length), 0)

    def rows_of(blk):
        return pl.ds(pl.multiple_of(blk * BLK, BLK), BLK)

    own_seq = 2 * y

    def keep_or_send(middle, blk, r):
        seq = 1 if middle else own_seq
        i = 4 * seq + blk - 3 * t
        mine = (i >= 0) & (i < 3)

        @pl.when(mine)
        def _():
            rs = rows_of(i)
            dz1_ref[rs, :] += r

        @pl.when(jnp.logical_not(mine))
        def _():
            sbuf[1 if middle else 0, rows_of(blk), :] = r.astype(BF)

    def into_middle(n, _):
        keep_or_send(True, n, dg(dq2[:, rows_of(n)], wt_ref[...], 0, 0))
        return 0

    dq0, dq1, dq2 = [dq_s.at[g] for g in range(3)]

    def into_own(n, _):
        r = dg(dq0[:, rows_of(n)], wt_ref[...], 0, 0) + dg(dq1[:, rows_of(n)], wpar_ref[...], 0, 0)
        keep_or_send(False, n, r)
        return 0

    far = 2 * (1 - y)
    half_copy = pltpu.make_async_remote_copy(
        src_ref=sbuf.at[1, rows_of(far + 1 - c)], dst_ref=rhalf, send_sem=send.at[12],
        recv_sem=recv.at[3], device_id={"tensor": core}, device_id_type=MESH,
    )
    far_copy = pltpu.make_async_remote_copy(
        src_ref=hsum, dst_ref=rmid.at[c], send_sem=send.at[13], recv_sem=recv.at[4 + c],
        device_id={"tensor": 2 * (1 - y) + y}, device_id_type=MESH,
    )
    core_copies = []
    for i in range(3):
        middle, blk = block_of(core, i)
        core_copies.append((
            middle,
            pltpu.make_async_remote_copy(
                src_ref=sbuf.at[middle, rows_of(blk)], dst_ref=rcore.at[i], send_sem=send.at[14 + i],
                recv_sem=recv.at[i], device_id={"tensor": core}, device_id_type=MESH,
            ),
        ))

    def unit(u, _):
        g = (u // 3 + 1) % 3
        h = u % 3

        @pl.when(u == 1)
        def _():
            for copy in go_core:
                copy.wait_recv()
            small_core.wait_recv()
            sv[0] = (go_ref[0].astype(F32) + rgo[0].astype(F32)).astype(BF)
            so[0] = (go_ref[2].astype(F32) + rgo[1].astype(F32)).astype(BF)
            thin[0].to_y().start()
            a, b = small_ref[...], tc[...]
            swapped = jnp.concatenate([b[0:8], b[9:10], b[8:9], b[11:12], b[10:11], b[12:16]])
            tv[...] = a + swapped

        @pl.when(u == 3)
        def _():
            for k in range(3):
                so[1 + k] = jnp.dot(dq_s[1, pl.ds(192 * k, 192), :], xab_ref[0], preferred_element_type=F32).astype(BF)
                thin[1 + k].to_y().start()

        @pl.when(u == 6)
        def _():
            lax.fori_loop(0, 4, into_middle, 0)
            half_copy.start()

        for k, steps in UNIT_STEPS.items():
            @pl.when(u == k)
            def _(steps=steps):
                for stage, p in steps:
                    getattr(big[p], stage)()

        @pl.when(u == 7)
        def _():
            half_copy.wait_recv()
            hsum[...] = (sbuf[1, rows_of(far + c), :].astype(F32) + rhalf[...].astype(F32)).astype(BF)
            far_copy.start()

        @pl.when(h == 0)
        def _():
            for blk in range(4):
                pltpu.make_async_copy(do_in.at[0, pl.ds(0, 192)], do_ref.at[g, blk], landed.at[g * 4 + blk]).wait()

        same = (row64 == seg_ref[jnp.where(g == 2, 1, own_seq)]).astype(F32)
        ro = pl.multiple_of(h * 192, 64)
        qh, kh, vh = pl.ds(ro, 64), pl.ds(ro + 64, 64), pl.ds(ro + 128, 64)
        l1, l2, l3 = split3(-lse_ref[g * 3 + h])
        qa[0:64, :] = qkv_ref[g, h, 0:64, :]
        qa[64:128, :] = jnp.where(row64 == 8, l1, jnp.where(row64 == 9, l2, jnp.where(row64 == 10, l3, same))).astype(BF)
        key_mark = jnp.where(row64 >= 8, 1.0, (same - 1.0) * BIG).astype(BF)
        ka[...] = jnp.concatenate([qkv_ref[g, h, 64:128, :], key_mark], axis=0).T
        va[...] = jnp.concatenate([qkv_ref[g, h, 128:192, :], jnp.ones((64, length), BF)], axis=0).T
        hs = pl.ds(pl.multiple_of(h * 64, 64), 64)
        for b in range(4):
            bs = slice(b * BLK, (b + 1) * BLK)
            do = do_ref[g, b, hs, :]
            e1, e2, e3 = split3(-jnp.sum(do.astype(F32) * o_ref[g, b, hs, :].astype(F32), axis=0, keepdims=True))
            da[0:64, bs] = do
            rb = row64[:, bs]
            da[64:128, bs] = jnp.where(rb == 8, e1, jnp.where(rb == 9, e2, jnp.where(rb == 10, e3, 0.0))).astype(BF)
        dk[...] = jnp.zeros_like(dk)
        dv[...] = jnp.zeros_like(dv)

        def chunk(n, _):
            cs = pl.ds(pl.multiple_of(n * 512, 512), 512)
            s = jnp.dot(ka[...], qa[:, cs], preferred_element_type=F32)
            p = jnp.exp2(s)
            dp = jnp.dot(va[...], da[:, cs], preferred_element_type=F32)
            pb = p.astype(BF)
            ds = (p * dp).astype(BF)
            dv[...] += dg(da[0:64, cs], pb, 1, 1)
            dk[...] += dg(qa[0:64, cs], ds, 1, 1)
            dq = jnp.dot(qkv_ref[g, h, 64:128, :], ds, preferred_element_type=F32)
            dq_s[g, qh, cs] = (dq * (HEAD_DIM ** (-0.5))).astype(BF)
            return 0

        lax.fori_loop(0, length // 512, chunk, 0)
        dq_s[g, kh, :] = (dk[...] * math.log(2.0)).astype(BF)
        dq_s[g, vh, :] = dv[...].astype(BF)

        @pl.when(u >= 6)
        def _():
            rows = pl.ds(ro, 192)
            r = jnp.dot(dq_s[0, rows, :], xab_ref[0], preferred_element_type=F32)
            sv[1 + h] = (r + jnp.dot(dq_s[2, rows, :], xab_ref[1], preferred_element_type=F32)).astype(BF)

        return 0

    lax.fori_loop(0, 9, unit, 0)
    ones = jnp.ones((8, length), BF)
    tv[12:13, 0:576] = (dg(ones, dq_s[0], 1, 1) + dg(ones, dq_s[2], 1, 1))[0:1]
    tv[13:14, 0:576] = dg(ones, dq_s[1], 1, 1)[0:1]
    to[...] = tv[...]
    tiny.to_y().start()
    lax.fori_loop(0, 4, into_own, 0)
    for middle, copy in core_copies:
        copy.start()

    named = {"p%d" % p: piece for p, piece in enumerate(big)}
    named.update({"w%d" % p: piece for p, piece in enumerate(thin)})
    named["t"] = tiny
    for k, (stage, name) in enumerate(TAIL_STEPS):
        getattr(named[name], stage)()
        if k == TAIL_INPUT:
            for i in range(3):
                core_copies[i][1].wait_recv()
                middle, blk = block_of(t, i)
                rs = pl.ds(i * BLK, BLK)

                @pl.when(middle == 0)
                def _():
                    din_ref[rs, :] = (dz1_ref[rs, :] + rcore[i].astype(F32)).astype(BF)

                @pl.when(middle == 1)
                def _():
                    k = blk % 2
                    pltpu.make_async_copy(hsum, rmid.at[k], recv.at[4 + k]).wait()
                    din_ref[rs, :] = (dz1_ref[rs, :] + rcore[i].astype(F32) + rmid[k].astype(F32)).astype(BF)

    for p, piece in enumerate(big):
        piece.finish(p >= early)
    for piece in thin + [tiny]:
        piece.finish()
    for copy in [c for _, c in core_copies] + [half_copy, far_copy] + go_core + [small_core]:
        copy.wait_send()
    for cond, copy in pending:
        if cond is None:
            copy.wait_send()
        else:
            pl.when(cond)(copy.wait_send)

def vm(*shape, dtype=BF):
    return pltpu.VMEM(shape, dtype)


def sds(*shape, dtype=BF):
    return jax.ShapeDtypeStruct(shape, dtype)


VM = pl.BlockSpec(memory_space=pltpu.VMEM)
ANY = pl.BlockSpec(memory_space=pl.ANY)


def params(cid):
    return pltpu.CompilerParams(collective_id=cid, has_side_effects=True, vmem_limit_bytes=62 * 2**20)


def local_step(
    line,
    layer_input, segment_ids, w_query, b_query, w_key, w_value, b_value, w_out, b_out, first_gain, first_shift,
    w_in, b_in, w_back, b_back, second_gain, second_shift, cotangent,
):
    seg = segment_ids.reshape(3, 1, 1024)
    wt = jnp.stack([w_query, w_key, w_value]).reshape(3, 768, 3, 64).transpose(2, 0, 3, 1).reshape(576, 768)
    zeros = jnp.zeros((192,), F32)
    heads = jnp.stack([b_query.astype(F32), zeros, b_value.astype(F32)]).reshape(3, 3, 64).transpose(1, 0, 2).reshape(576)
    bias = jnp.stack([b_in.astype(F32), jnp.concatenate([heads, zeros])])
    bias = jnp.concatenate([bias, jnp.zeros((6, 768), F32)])
    vec = jnp.stack([b_out, first_gain, first_shift, b_back, second_gain, second_shift])
    vec = jnp.concatenate([vec, jnp.zeros((2, 768), F32)])
    dma = pltpu.SemaphoreType.DMA

    qkv, o, lse, xab, wpar, woutg, wing, biasg = pl.pallas_call(
        k1,
        out_shape=(
            sds(3, 3, 192, 1024), sds(3, 4, 192, BLK), sds(9, 1, 1024, dtype=F32), sds(2, 1024, 768), sds(576, 768),
            sds(3, 192, 768), sds(2, 768, 768), sds(3, 8, 768, dtype=F32),
        ),
        in_specs=[ANY, ANY, VM, VM, ANY, ANY],
        out_specs=(ANY, ANY, VM, ANY, ANY, ANY, ANY, VM),
        scratch_shapes=[
            vm(3, 3, 192, 1024), vm(3, 4, 192, BLK), vm(2, 1024, 768), vm(2, 576, 768), vm(576, 1, dtype=F32),
            vm(128, 1024), vm(128, 1024), vm(80, 1024), dma((32,)), dma((32,)), dma((10,)),
        ],
        compiler_params=params(0),
        name="attention_forward",
    )(layer_input, wt, bias, seg, w_out, w_in)

    out, dz1, do, gf, go, small = pl.pallas_call(
        k2,
        out_shape=(
            sds(768, 768), sds(768, 768, dtype=F32), sds(3, 768, BLK), sds(2, 3, 2, 768, BLK), sds(4, 192, 768),
            sds(16, 768, dtype=F32),
        ),
        in_specs=[VM, VM, VM, VM, VM, ANY, ANY, ANY, ANY, ANY, ANY],
        out_specs=(VM, VM, VM, VM, VM, VM),
        scratch_shapes=[
            vm(3, 768, BLK), vm(768, 768), vm(768, 3072), vm(3072, 768),
            vm(768, 768), vm(768, 768), vm(768, 768, dtype=F32), vm(768, 1, dtype=F32), vm(768, 3072), vm(768, 3072),
            vm(768, 768, dtype=F32), vm(768, 768), vm(768, 768),
            vm(2, 3, 2, 768, BLK), vm(2, 3, 2, 768, BLK), vm(max(Y_EARLY, 1), 2, 768, BLK),
            dma((48,)), dma((48,)), dma((20,)),
        ],
        compiler_params=params(1),
        name="feed_forward",
    )(layer_input, cotangent, vec, bias, biasg, o, w_out, woutg, w_in, wing, w_back)

    piece, slab, tiny = vm(6, 768, BLK), vm(4, 192, 768), vm(16, 768, dtype=F32)
    din, ff, fs, sm = pl.pallas_call(
        partial(k3, line),
        out_shape=(sds(768, 768), sds(6, 768, BLK), sds(4, 192, 768), sds(16, 768, dtype=F32)),
        in_specs=[VM, VM, VM, VM, VM, VM, VM, ANY, ANY, ANY, VM, VM],
        out_specs=(VM, VM, VM, VM),
        scratch_shapes=[
            vm(768, 768, dtype=F32),
            vm(3, 4, 192, BLK), vm(3, 576, 1024), vm(128, 1024), vm(1024, 128), vm(1024, 128), vm(128, 1024),
            vm(64, 1024, dtype=F32), vm(64, 1024, dtype=F32), vm(2, 1024, 768),
            vm(3, BLK, 768), vm(2, BLK, 768), vm(BLK, 768), vm(BLK, 768),
            piece, piece, piece, piece, piece, slab, slab, slab, slab, slab, slab, vm(2, 192, 768),
            tiny, tiny, tiny, tiny, tiny, tiny, tiny,
            dma((11, 5)), dma((11, 5)), dma((17,)), dma((9,)), dma((12,)), dma((7,)),
        ],
        compiler_params=params(2),
        name="attention_backward",
    )(qkv, seg, o, lse, xab, wt, wpar, do, dz1, gf, go, small)
    if not line:
        ff, fs = lax.psum((ff, fs), "dp")
        sm = lax.psum(sm, "dp")
    ff = ff.astype(F32).reshape(3, 2, 768, BLK)
    g_in = jnp.concatenate([ff[0, 0], ff[1, 0], ff[2, 0]], axis=1)
    g_back = jnp.concatenate([ff[0, 1].T, ff[1, 1].T, ff[2, 1].T], axis=0)
    heads = fs[1:4].astype(F32).reshape(3, 3, 64, 768).transpose(1, 3, 0, 2).reshape(3, 768, 192)
    bq = sm[12, 0:576].reshape(3, 3, 64).transpose(1, 0, 2).reshape(3, 192)
    return (
        out, din, heads[0], bq[0], heads[1], heads[2], bq[2], fs[0].astype(F32),
        sm[0], sm[1], sm[2], g_in, sm[8], g_back, sm[3], sm[4], sm[5],
    )

def solution(mesh):
    rows = P(("dp", "tensor"), None)
    in_specs = (
        rows, P("dp", None), P(None, "tensor"), P("tensor"), P(None, "tensor"), P(None, "tensor"), P("tensor"),
        P("tensor", None), P(), P(), P(), P(None, "tensor"), P("tensor"), P("tensor", None), P(), P(), P(), rows,
    )
    out_specs = (
        rows, rows, P(None, "tensor"), P("tensor"), P(None, "tensor"), P(None, "tensor"), P("tensor"),
        P("tensor", None), P(), P(), P(), P(None, "tensor"), P("tensor"), P("tensor", None), P(), P(), P(),
    )
    line = mesh.shape["dp"] == 8
    return jax.shard_map(partial(local_step, line), mesh=mesh, in_specs=in_specs, out_specs=out_specs, check_vma=False)
```

```python
import math
from functools import partial

import jax
import jax.numpy as jnp
from jax import lax
from jax.experimental import pallas as pl
from jax.experimental.pallas import tpu as pltpu
from jax.sharding import PartitionSpec as P

F32 = jnp.float32
BF = jnp.bfloat16
MESH = pl.DeviceIdType.MESH
HEAD_DIM = 64
EPSILON = 1e-05
BIG = 1e30
LOG2E = 1.0 / math.log(2.0)
QSCALE = HEAD_DIM ** (-0.5) * LOG2E
BLK = 256
Y_EARLY = 2
X_EARLY = 1
UNIT_STEPS = {
    2: (("after_end", 0), ("after_x", 2), ("after_y", 4)),
    4: (("after_end", 1), ("after_mate", 0), ("after_x", 3), ("after_y", 5)),
    5: (("after_end", 2),),
    6: (("after_mate", 1), ("after_x", 4)),
    7: (("after_end", 3),),
    8: (("after_mate", 2), ("after_x", 5), ("after_end", 4)),
}
TAIL_INPUT = 4
TAIL_STEPS = (
    ("after_y", "w0"), ("after_y", "w1"), ("after_mate", "p3"), ("after_end", "p5"), ("after_y", "w2"),
    ("after_x", "w0"), ("after_mate", "p4"), ("after_x", "w1"), ("after_y", "w3"), ("after_y", "t"),
    ("after_end", "w0"), ("after_mate", "p5"), ("after_x", "w2"), ("after_end", "w1"), ("after_mate", "w0"),
    ("after_x", "w3"), ("after_x", "t"), ("after_end", "w2"), ("after_mate", "w1"),
    ("after_end", "w3"), ("after_end", "t"), ("after_mate", "w2"),
    ("after_mate", "w3"), ("after_mate", "t"),
)


def dg(a, b, ca, cb):
    return lax.dot_general(a, b, (((ca,), (cb,)), ((), ())), preferred_element_type=F32)


def where_am_i():
    t = lax.axis_index("tensor")
    d = lax.axis_index("dp")
    core = t + 1 - 2 * (t % 2)
    across = (t + 2) % 4
    diag = 3 - t
    side = d + 1 - 2 * (d % 2)
    return t, d, core, across, diag, side


def block_of(t, i):
    b = 3 * t + i
    middle = (b // 4) % 2
    return middle, b % 4


def greet(devices):
    barrier = pltpu.get_barrier_semaphore()
    for dev in devices:
        pl.semaphore_signal(barrier, inc=1, device_id=dev, device_id_type=MESH)
    pl.semaphore_wait(barrier, len(devices))


def half_rows(half, total, pieces, i):
    n = total // 2 // pieces
    return pl.ds(pl.multiple_of(half * (total // 2) + i * n, n), n)


class Copies:
    def __init__(self, send, recv):
        self.send, self.recv, self.used = send, recv, 0

    def new(self, src, dst, **device):
        k = self.used
        self.used += 1
        return pltpu.make_async_remote_copy(
            src_ref=src,
            dst_ref=dst,
            send_sem=self.send.at[k],
            recv_sem=self.recv.at[k],
            device_id=device,
            device_id_type=MESH,
        )


def start_all(copies):
    for copy in copies:
        copy.start()


def layer_stats(z):
    mean = jnp.mean(z, axis=-1, keepdims=True)
    cen = z - mean
    var = jnp.mean(cen * cen, axis=-1, keepdims=True)
    inv = lax.rsqrt(var + EPSILON)
    return cen * inv, inv


def forward(
    line,
    x_ref, cot_in, wq_ref, wk_ref, wv_ref, bq_ref, bv_ref, bin_ref, v0, v1, v2, v3, v4, v5, seg_ref,
    wout_ref, win_ref, wback_ref,
    qkv_out, o_out, lse_ref, xab_out, wts_out, out_ref, dz1_out, do_ref, gf_ref, go_ref, small_ref,
    qkv, o_v, xab, w_v, bias_ref, biasg_ref, bcol, qa, ka, va,
    cot_ref, ot, wo, wi, wb, h1b, h1t, xh1, inv1, gg, gp, z2, dz2b, dz2t, gsend, rc, ry, rx, send, recv, local,
):
    length = 1024
    t, d, core, across, diag, side = where_am_i()
    y, c = t // 2, t % 2
    half = d % 2
    x_early = X_EARLY if line else 0

    rows_out, rows_local = [], []
    cp = Copies(send, recv)
    cp.used = 12
    for i in range(3):
        middle, blk = block_of(t, i)
        src = x_ref.at[pl.ds(i * BLK, BLK)]
        dst = xab.at[middle, pl.ds(pl.multiple_of(blk * BLK, BLK), BLK)]
        rows_local.append(pltpu.make_async_copy(src, dst, local.at[i]))
        rows_out.append(cp.new(src, dst, tensor=core))
    own = [
        pltpu.make_async_copy(wout_ref, wo.at[pl.ds(0, 192)], local.at[12]),
        pltpu.make_async_copy(win_ref, wi.at[:, pl.ds(0, 768)], local.at[13]),
        pltpu.make_async_copy(wback_ref, wb.at[pl.ds(0, 768)], local.at[14]),
        pltpu.make_async_copy(cot_in, cot_ref, local.at[15]),
    ]
    start_all(rows_local + own)

    for k, ref in enumerate((wq_ref, wk_ref, wv_ref)):
        for h in range(3):
            n = 192 * h + 64 * k
            w_v[0, n : n + 64, :] = ref[64 * h : 64 * h + 64, :]
    bias_ref[...] = jnp.zeros((8, 768), F32)
    bias_ref[0:1, :] = bin_ref[...].astype(F32).reshape(1, 768)
    bq, bv = bq_ref[...].astype(F32).reshape(1, 192), bv_ref[...].astype(F32).reshape(1, 192)
    parts = []
    for h in range(3):
        parts += [bq[:, 64 * h : 64 * h + 64], jnp.zeros((1, 64), F32), bv[:, 64 * h : 64 * h + 64]]
    bias_ref[1:2, 0:576] = jnp.concatenate(parts, axis=1)

    greet([{"tensor": core}, {"tensor": across}, {"tensor": diag}, {"dp": side}])

    mixed = (t == 1) | (t == 2)
    k_out = jnp.where(mixed, 0, 1)
    block_out = pl.ds(pl.multiple_of((2 * y + k_out) * BLK, BLK), BLK)
    block_in = pl.ds(pl.multiple_of((2 * (1 - y) + c) * BLK, BLK), BLK)
    n = cp.used
    cross_out = cp.new(xab.at[1, block_out], xab.at[1, block_out], tensor=2 * (1 - y) + k_out)
    cross_arrived = pltpu.make_async_remote_copy(
        src_ref=xab.at[1, block_out], dst_ref=xab.at[1, block_in], send_sem=send.at[n], recv_sem=recv.at[n],
        device_id={"tensor": core}, device_id_type=MESH,
    )
    cross_forward = cp.new(xab.at[1, block_in], xab.at[1, block_in], tensor=core)
    wp_first, wp_second = [], []
    for i in range(3):
        part = half_rows(half, 576, 3, i)
        wp_first.append(cp.new(w_v.at[0, part], w_v.at[1, part], tensor=across))
        wp_second.append(cp.new(w_v.at[1, part], w_v.at[1, part], dp=side))
    bias_out = [
        cp.new(bias_ref, biasg_ref.at[0], tensor=core),
        cp.new(bias_ref, biasg_ref.at[1], tensor=across),
        cp.new(bias_ref, biasg_ref.at[2], tensor=diag),
    ]
    part = half_rows(half, 192, 1, 0)
    place = pl.ds(part.start + 384, part.size)
    wo_first = cp.new(wout_ref.at[part], wo.at[place], tensor=across)
    wo_second = cp.new(wo.at[place], wo.at[place], dp=side)
    wo_core = cp.new(wout_ref, wo.at[pl.ds(192, 192)], tensor=core)
    wo_diag = cp.new(wo.at[pl.ds(384, 192)], wo.at[pl.ds(576, 192)], tensor=core)

    def lanes(j):
        return pl.ds(768 * j, 768)

    in_core = cp.new(win_ref, wi.at[:, lanes(1)], tensor=core)
    back_core = cp.new(wback_ref, wb.at[lanes(1)], tensor=core)
    in_first, in_second, in_diag, back_first, back_second, back_diag = [], [], [], [], [], []
    for i in range(3):
        part = half_rows(half, 768, 3, i)
        in_first.append(cp.new(win_ref.at[part], wi.at[part, lanes(2)], tensor=across))
        in_second.append(cp.new(wi.at[part, lanes(2)], wi.at[part, lanes(2)], dp=side))
        place = pl.ds(part.start + 2 * 768, part.size)
        back_first.append(cp.new(wback_ref.at[part], wb.at[place], tensor=across))
        back_second.append(cp.new(wb.at[place], wb.at[place], dp=side))
        for h in range(2):
            both = half_rows(h, 768, 3, i)
            in_diag.append(cp.new(wi.at[both, lanes(2)], wi.at[both, lanes(3)], tensor=core))
            m = h * 384 + i * 128
            back_diag.append(cp.new(wb.at[pl.ds(2 * 768 + m, 128)], wb.at[pl.ds(3 * 768 + m, 128)], tensor=core))

    peers = (t, core, across, diag)

    def heads_to_rows(group):
        found = []
        for j, dev in enumerate(peers):
            if group != 2 and j >= 2:
                continue
            for i in range(3):
                middle, blk = block_of(dev, i)
                slot = j + 2 if group == 1 else j
                src, dst = o_v.at[group, blk], ot.at[i, pl.ds(slot * 192, 192)]
                sem = recv.at[i * 4 + slot]
                if j == 0:
                    copy = pltpu.make_async_copy(src, dst, sem)
                else:
                    copy = pltpu.make_async_remote_copy(
                        src_ref=src, dst_ref=dst, send_sem=send.at[9 + i if group == 1 else 3 * (j - 1) + i],
                        recv_sem=sem, device_id={"tensor": dev}, device_id_type=MESH,
                    )
                found.append((j, (middle == 1) if group == 2 else (middle == 0), copy))
        return found

    def start_heads(group):
        for _, cond, copy in heads_to_rows(group):
            pl.when(cond)(copy.start)

    start_all(rows_out + bias_out + wp_first[:1])
    start_all([wo_core, in_core, back_core])
    va[64:80, :] = jnp.ones((16, length), BF)
    row64 = lax.broadcasted_iota(jnp.int32, (64, length), 0)
    factor = jnp.where(lax.broadcasted_iota(jnp.int32, (576, 1), 0) % 192 < 64, QSCALE, 1.0)

    def outgoing(g):
        return [
            pltpu.make_async_copy(qkv.at[g], qkv_out.at[g], local.at[4 + 2 * (g % 3)]),
            pltpu.make_async_copy(o_v.at[g], o_out.at[g], local.at[5 + 2 * (g % 3)]),
        ]

    def at(n, k, copies_recv, copies_start=()):
        @pl.when(n == k)
        def _():
            for copy in copies_recv:
                copy.wait_recv()
            start_all(copies_start)

    def unit(u, _):
        g = (2 * (u // 3)) % 3
        h = u % 3
        par = jnp.where(g == 1, 1, 0)
        middle = jnp.where(g == 2, 1, 0)

        at(u, 1, wp_first[:1], wp_second[:1])

        @pl.when(u == 3)
        def _():
            cross_arrived.wait_recv()
            cross_forward.start()
            start_heads(0)
            cross_forward.wait_recv()

        at(u, 4, wp_first[1:2], wp_second[1:2])
        at(u, 5, wp_first[2:3], wp_second[2:3])

        @pl.when(u == 6)
        def _():
            start_heads(2)
            start_all(in_first[2:] + back_first)

        at(u, 6, [wo_first], [wo_second])
        at(u, 6, wp_second + [bias_out[1]])
        at(u, 7, in_first[:1], in_second[:1])
        at(u, 8, in_first[1:2], in_second[1:2])
        at(u, 8, [wo_second], [wo_diag])

        @pl.when(h == 0)
        def _():
            @pl.when(u > 0)
            def _():
                start_all(outgoing(jnp.where(g == 2, 0, 2)))

            @pl.when(par == 0)
            def _():
                bcol[...] = jnp.transpose(bias_ref[...])[0:576, 1:2]

            @pl.when(par == 1)
            def _():
                bcol[...] = jnp.transpose(biasg_ref[1])[0:576, 1:2]

            col = bcol[...]

            def body(n, _):
                cs = pl.ds(pl.multiple_of(n * BLK, BLK), BLK)
                r = (dg(w_v[par], xab[middle, cs, :], 1, 1) + col) * factor
                for k in range(3):
                    qkv[g, k, :, cs] = r[192 * k : 192 * (k + 1)].astype(BF)
                return 0

            lax.fori_loop(0, length // BLK, body, 0)
            same = (row64 == seg_ref[pl.ds(jnp.where(g == 2, 1, 2 * y), 1), :]).astype(F32)
            qa[64:128, :] = same.astype(BF)
            ka[64:128, :] = ((same - 1.0) * BIG).astype(BF)

        qa[0:64, :] = qkv[g, h, 0:64, :]
        ka[0:64, :] = qkv[g, h, 64:128, :]
        va[0:64, :] = qkv[g, h, 128:192, :]
        s = jnp.dot(ka[...].T, qa[...], preferred_element_type=F32)
        m = jnp.max(s, axis=0, keepdims=True)
        p = jnp.exp2(s - m).astype(BF)
        o = jnp.dot(va[...], p, preferred_element_type=F32)
        total = o[64:65, :]
        res = (o[0:64] * (1.0 / total)).astype(BF)
        hs = pl.ds(pl.multiple_of(h * 64, 64), 64)
        for b in range(4):
            o_v[g, b, hs, :] = res[:, b * BLK : (b + 1) * BLK]
        lse_ref[g * 3 + h] = m + jnp.log2(total)
        return 0

    for copy in rows_local:
        copy.wait()
    for copy in rows_out:
        copy.wait_recv()
    start_all([cross_out] + wp_first[1:] + [wo_first] + in_first[:2])
    lax.fori_loop(0, 9, unit, 0)
    start_heads(1)
    tail = outgoing(1)
    tail.append(pltpu.make_async_copy(xab, xab_out, local.at[10]))
    tail.append(pltpu.make_async_copy(w_v, wts_out, local.at[11]))
    start_all(tail)

    b_out, gain1, shift1, b_back, gain2, shift2 = [v[...].reshape(1, 768) for v in (v0, v1, v2, v3, v4, v5)]
    own[0].wait()
    for copy in [wo_core, wo_diag, bias_out[0], bias_out[2]]:
        copy.wait_recv()
    for i in range(2):
        in_second[i].wait_recv()
        start_all(in_diag[2 * i : 2 * i + 2])
    for i in range(3):
        for slot in range(4):
            pltpu.make_async_copy(o_v.at[0, 0], ot.at[i, pl.ds(slot * 192, 192)], recv.at[i * 4 + slot]).wait()

    def first(i, _):
        rs = pl.ds(pl.multiple_of(i * BLK, BLK), BLK)
        z = x_ref[rs, :].astype(F32) + dg(ot[i], wo[...], 0, 0) + b_out
        xh, inv = layer_stats(z)
        xh1[rs, :] = xh
        inv1[rs, :] = inv
        h1b[rs, :] = (xh * gain1 + shift1).astype(BF)
        return 0

    lax.fori_loop(0, 3, first, 0)
    h1t[...] = h1b[...].T
    own[1].wait()

    def up(n, _):
        at(n, 1, in_first[2:], in_second[2:])
        at(n, 3, [in_core])
        at(n, 4, back_first[:1], back_second[:1])
        at(n, 6, in_second[2:], in_diag[4:])
        at(n, 7, back_first[1:2], back_second[1:2])
        at(n, 9, in_diag)
        at(n, 9, back_second[:1], back_diag[:2])
        at(n, 10, back_first[2:], back_second[2:])
        at(n, 11, back_second[1:2], back_diag[2:4])
        cs = pl.ds(pl.multiple_of(n * BLK, BLK), BLK)
        j = n // 3
        low = pl.ds(pl.multiple_of((n % 3) * BLK, BLK), BLK)
        bias = jnp.where(j == 0, bias_ref[0:1, low], biasg_ref[jnp.maximum(j - 1, 0), 0:1, low])
        u = jnp.dot(h1b[...], wi[:, cs], preferred_element_type=F32) + bias
        cdf = 0.5 * (1.0 + lax.erf(u * (2.0 ** -0.5)))
        pdf = jnp.exp(-0.5 * u * u) * (1.0 / math.sqrt(2.0 * math.pi))
        gg[:, cs] = (u * cdf).astype(BF)
        gp[:, cs] = (cdf + u * pdf).astype(BF)
        return 0

    lax.fori_loop(0, 12, up, 0)
    own[2].wait()
    back_core.wait_recv()

    def down_near(n, _):
        cs = pl.ds(pl.multiple_of(n * BLK, BLK), BLK)
        z2[:, cs] = jnp.dot(gg[:, 0:1536], wb[0:1536, cs], preferred_element_type=F32)
        return 0

    def down_far(n, _):
        cs = pl.ds(pl.multiple_of(n * BLK, BLK), BLK)
        z2[:, cs] += jnp.dot(gg[:, 1536:3072], wb[1536:3072, cs], preferred_element_type=F32)
        return 0

    lax.fori_loop(0, 3, down_near, 0)
    back_second[2].wait_recv()
    start_all(back_diag[4:])
    own[3].wait()
    for copy in back_diag:
        copy.wait_recv()
    lax.fori_loop(0, 3, down_far, 0)

    def second_norm(i, sums):
        rs = pl.ds(pl.multiple_of(i * BLK, BLK), BLK)
        h1 = xh1[rs, :] * gain1 + shift1
        xh, inv = layer_stats(h1 + z2[rs, :] + b_back)
        out_ref[rs, :] = (xh * gain2 + shift2).astype(BF)
        cot = cot_ref[rs, :].astype(F32)
        dxh = cot * gain2
        dz = inv * (dxh - jnp.mean(dxh, axis=-1, keepdims=True) - xh * jnp.mean(dxh * xh, axis=-1, keepdims=True))
        z2[rs, :] = dz
        dz2b[rs, :] = dz.astype(BF)
        return (
            sums[0] + jnp.sum(dz, axis=0, keepdims=True),
            sums[1] + jnp.sum(cot * xh, axis=0, keepdims=True),
            sums[2] + jnp.sum(cot, axis=0, keepdims=True),
        )

    zero = jnp.zeros((1, 768), F32)
    s3, s4, s5 = lax.fori_loop(0, 3, second_norm, (zero, zero, zero))
    small_ref[3:4, :] = s3
    small_ref[4:5, :] = s4
    small_ref[5:6, :] = s5
    dz2t[...] = dz2b[...].T

    base = cp.used

    def to_core(stage, ch):
        k = base + stage * 3 + ch
        return pltpu.make_async_remote_copy(
            src_ref=gsend.at[ch], dst_ref=rc.at[ch], send_sem=send.at[k], recv_sem=recv.at[k],
            device_id={"tensor": core}, device_id_type=MESH,
        )

    def to_across(ch):
        k = base + 6 + ch
        return pltpu.make_async_remote_copy(
            src_ref=gf_ref.at[1, ch], dst_ref=ry.at[ch], send_sem=send.at[k], recv_sem=recv.at[k],
            device_id={"tensor": across}, device_id_type=MESH,
        )

    def to_side(ch):
        k = base + 9 + ch
        return pltpu.make_async_remote_copy(
            src_ref=gf_ref.at[0, ch], dst_ref=rx.at[ch], send_sem=send.at[k], recv_sem=recv.at[k],
            device_id={"dp": side}, device_id_type=MESH,
        )

    def back(m, _):
        stage = m // 6
        ch = (m % 6) // 2
        slot = 3 - 2 * stage - m % 2
        n = slot * 3 + ch
        cs = pl.ds(pl.multiple_of(n * BLK, BLK), BLK)
        low = pl.ds(pl.multiple_of(ch * BLK, BLK), BLK)
        g_back = jnp.dot(dz2t[...], gg[:, cs], preferred_element_type=F32)
        du = (dg(dz2b[...], wb[cs, :], 1, 1) * gp[:, cs].astype(F32)).astype(BF)
        gg[:, cs] = du
        small_ref[pl.ds(8 + slot, 1), low] = jnp.sum(du.astype(F32), axis=0, keepdims=True)
        g_in = jnp.dot(h1t[...], du, preferred_element_type=F32)

        @pl.when(m % 2 == 0)
        def _():
            pl.when(stage == 1)(to_core(0, ch).wait_send)
            gsend[ch, 0] = g_in.astype(BF)
            gsend[ch, 1] = g_back.astype(BF)
            to_core(stage, ch).start()

        @pl.when(m % 2 == 1)
        def _():
            to_core(stage, ch).wait_recv()
            gf_ref[1 - stage, ch, 0] = (g_in + rc[ch, 0].astype(F32)).astype(BF)
            gf_ref[1 - stage, ch, 1] = (g_back + rc[ch, 1].astype(F32)).astype(BF)
            pl.when((stage == 0) & (ch < Y_EARLY))(to_across(ch).start)

        return 0

    lax.fori_loop(0, 12, back, 0)

    def take_y(ch):
        to_across(ch).wait_recv()
        for k in range(2):
            gf_ref[0, ch, k] = (gf_ref[0, ch, k].astype(F32) + ry[ch, k].astype(F32)).astype(BF)

    for ch in range(x_early):
        take_y(ch)
        to_side(ch).start()

    def into_h(n, _):
        cs = pl.ds(pl.multiple_of(n * BLK, BLK), BLK)
        z2[:, cs] += dg(gg[...], wi[cs, :], 1, 1)
        return 0

    lax.fori_loop(0, 3, into_h, 0)

    def first_norm(i, sums):
        rs = pl.ds(pl.multiple_of(i * BLK, BLK), BLK)
        dh = z2[rs, :]
        xh = xh1[rs, :]
        dxh = dh * gain1
        dz = inv1[rs, :] * (dxh - jnp.mean(dxh, axis=-1, keepdims=True) - xh * jnp.mean(dxh * xh, axis=-1, keepdims=True))
        z2[rs, :] = dz
        dzb = dz.astype(BF)
        dz2b[rs, :] = dzb
        do_ref[i] = dg(wo[...], dzb, 1, 1).astype(BF)
        return (
            sums[0] + jnp.sum(dz, axis=0, keepdims=True),
            sums[1] + jnp.sum(dh * xh, axis=0, keepdims=True),
            sums[2] + jnp.sum(dh, axis=0, keepdims=True),
        )

    s0, s1, s2 = lax.fori_loop(0, 3, first_norm, (zero, zero, zero))
    dz1_copy = pltpu.make_async_copy(z2, dz1_out, local.at[0])
    dz1_copy.start()
    small_ref[0:1, :] = s0
    small_ref[1:2, :] = s1
    small_ref[2:3, :] = s2
    for j in range(4):
        rows = pl.ds(192 * j, 192)
        acc = jnp.dot(ot[0, rows, :], dz2b[0:BLK, :], preferred_element_type=F32)
        acc += jnp.dot(ot[1, rows, :], dz2b[BLK : 2 * BLK, :], preferred_element_type=F32)
        acc += jnp.dot(ot[2, rows, :], dz2b[2 * BLK : 3 * BLK, :], preferred_element_type=F32)
        go_ref[j] = acc.astype(BF)
    small_ref[6:8, :] = jnp.zeros((2, 768), F32)
    small_ref[12:16, :] = jnp.zeros((4, 768), F32)

    for group in range(3):
        for j, cond, copy in heads_to_rows(group):
            if j:
                pl.when(cond)(copy.wait_send)
    sent = rows_out + [cross_out, cross_forward] + wp_first + wp_second + bias_out
    sent += [wo_first, wo_second, wo_core, wo_diag, in_core, back_core]
    sent += in_first + in_second + in_diag + back_first + back_second + back_diag
    for copy in sent + [to_core(1, ch) for ch in range(3)]:
        copy.wait_send()
    for copy in outgoing(0) + outgoing(2) + tail + [dz1_copy]:
        copy.wait()
    for ch in range(Y_EARLY):
        if ch >= x_early:
            take_y(ch)
        to_across(ch).wait_send()
    for ch in range(x_early):
        to_side(ch).wait()
        for k in range(2):
            gf_ref[0, ch, k] = (gf_ref[0, ch, k].astype(F32) + rx[ch, k].astype(F32)).astype(BF)


def split3(v):
    a = v.astype(BF).astype(F32)
    b = (v - a).astype(BF).astype(F32)
    return a, b, v - a - b


class Piece:
    def __init__(self, value, other, from_y, from_x, from_end, from_mate, final, send, recv, where, fold=None):
        self.value, self.other, self.final = value, other, final
        self.from_y, self.from_x, self.from_end, self.from_mate = from_y, from_x, from_end, from_mate
        self.send, self.recv, self.where, self.fold = send, recv, where, fold

    def copy(self, stage, src, dst, **device):
        return pltpu.make_async_remote_copy(
            src_ref=src, dst_ref=dst, send_sem=self.send.at[stage], recv_sem=self.recv.at[stage],
            device_id=device, device_id_type=MESH,
        )

    def to_y(self):
        return self.copy(0, self.other, self.from_y, tensor=self.where["across"])

    def to_x(self):
        return self.copy(1, self.value, self.from_x, dp=self.where["side"])

    def to_inner(self):
        return self.copy(2, self.value, self.from_end, dp=self.where["pair"])

    def to_mate(self):
        return self.copy(3, self.value, self.from_mate, dp=self.where["mate"])

    def to_end(self):
        return self.copy(4, self.final, self.final, dp=self.where["pair"])

    def add(self, arrived, into):
        into[...] = (self.value[...].astype(F32) + arrived[...].astype(F32)).astype(into.dtype)

    def after_y(self):
        self.to_y().wait_recv()
        if self.fold is None:
            self.add(self.from_y, self.value)
        else:
            self.fold(self)
        self.begin_x()

    def begin_x(self):
        if self.where["line"]:
            self.to_x().start()
        else:
            self.final[...] = self.value[...]

    def after_x(self):
        if not self.where["line"]:
            return
        self.to_x().wait()
        self.add(self.from_x, self.value)
        self.begin_z()

    def begin_z(self):
        pl.when(self.where["end"])(lambda: self.to_inner().start())

    def after_end(self):
        if not self.where["line"]:
            return

        @pl.when(self.where["inner"])
        def _():
            self.to_inner().wait_recv()
            self.add(self.from_end, self.value)
            self.to_mate().start()

    def after_mate(self):
        if not self.where["line"]:
            return

        @pl.when(self.where["inner"])
        def _():
            self.to_mate().wait_recv()
            self.add(self.from_mate, self.final)
            self.to_end().start()

    def finish(self, had_y=True):
        if had_y:
            self.to_y().wait_send()
        if not self.where["line"]:
            return

        @pl.when(self.where["end"])
        def _():
            self.to_end().wait_recv()
            self.to_inner().wait_send()

        @pl.when(self.where["inner"])
        def _():
            self.to_mate().wait_send()
            self.to_end().wait_send()


def k3(
    line,
    qkv_ref, seg_ref, o_ref, lse_ref, xab_ref, wts_ref, do_in, dz1_in, gf_ref, go_ref, small_ref,
    din_ref, ff_ref, fs_ref, sm_ref,
    dz1_ref, do_ref, dq_s, qa, ka, va, da, dk, dv, sbuf, rcore, rmid, rhalf, hsum,
    fv, fy, fx, fe, fm, sv, so, sy, sx, se, sm, rgo, tv, to, tc, ty, tx, te, tm,
    psend, precv, send, recv, landed, local,
):
    length = 1024
    t, d, core, across, diag, side = where_am_i()
    y, c = t // 2, t % 2
    where = {"across": across, "side": side, "line": line}
    known = [{"tensor": core}, {"tensor": across}, {"tensor": diag}]
    if line:
        z = d // 2
        where["pair"] = d + 2 - 4 * (z % 2)
        where["mate"] = d + 2 - 4 * ((z + 1) % 2)
        where["end"] = (z == 0) | (z == 3)
        where["inner"] = (z == 1) | (z == 2)
        known += [{"dp": side}, {"dp": where["pair"]}]
    barrier = pltpu.get_barrier_semaphore()
    for dev in known:
        pl.semaphore_signal(barrier, inc=1, device_id=dev, device_id_type=MESH)
    if line:
        @pl.when(where["inner"])
        def _():
            pl.semaphore_signal(barrier, inc=1, device_id={"dp": where["mate"]}, device_id_type=MESH)
            pl.semaphore_wait(barrier, len(known) + 1)

        @pl.when(where["end"])
        def _():
            pl.semaphore_wait(barrier, len(known))
    else:
        pl.semaphore_wait(barrier, len(known))

    pending = []
    peers = (t, core, across, diag)
    for i in range(3):
        middle, blk = block_of(t, i)
        for j, dev in enumerate(peers):
            src = do_in.at[i, pl.ds(192 * j, 192)]
            group = jnp.where(middle == 1, 2, j // 2)
            dst = do_ref.at[group, blk]
            sem = landed.at[group * 4 + blk]
            if j == 0:
                pltpu.make_async_copy(src, dst, sem).start()
                continue
            if j == 2:
                pl.when(middle == 0)(pltpu.make_async_copy(src, dst, sem).start)
                dev_to, cond = across, middle == 1
            elif j == 1:
                dev_to, cond = core, None
            else:
                dev_to, cond = jnp.where(middle == 1, diag, core), None
            copy = pltpu.make_async_remote_copy(
                src_ref=src, dst_ref=dst, send_sem=send.at[i * 3 + j - 1], recv_sem=sem,
                device_id={"tensor": dev_to}, device_id_type=MESH,
            )
            if cond is None:
                copy.start()
            else:
                pl.when(cond)(copy.start)
            pending.append((cond, copy))

    loads = [pltpu.make_async_copy(gf_ref.at[0, p // 2, p % 2], fv.at[p], local.at[p]) for p in range(6)]
    loads.append(pltpu.make_async_copy(dz1_in, dz1_ref, local.at[6]))
    start_all(loads)
    go_core = [
        pltpu.make_async_remote_copy(
            src_ref=go_ref.at[2 * k + 1], dst_ref=rgo.at[k], send_sem=send.at[9 + k], recv_sem=recv.at[6 + k],
            device_id={"tensor": core}, device_id_type=MESH,
        )
        for k in range(2)
    ]
    small_core = pltpu.make_async_remote_copy(
        src_ref=small_ref, dst_ref=tc, send_sem=send.at[11], recv_sem=recv.at[8],
        device_id={"tensor": core}, device_id_type=MESH,
    )
    start_all(go_core + [small_core])
    big = [
        Piece(fv.at[p], gf_ref.at[1, p // 2, p % 2], fy.at[p], fx.at[p], fe.at[p], fm.at[p], ff_ref.at[p],
              psend.at[p], precv.at[p], where)
        for p in range(6)
    ]
    thin = [
        Piece(sv.at[p], so.at[p], sy.at[p], sx.at[p], se.at[p], sm.at[p], fs_ref.at[p],
              psend.at[6 + p], precv.at[6 + p], where)
        for p in range(4)
    ]

    def fold_small(piece):
        got = ty[...]
        add = jnp.concatenate([got[0:8], got[10:11], jnp.zeros((3, 768), F32), got[13:14], jnp.zeros((3, 768), F32)])
        tv[...] = tv[...] + add

    tiny = Piece(tv, to, ty, tx, te, tm, sm_ref, psend.at[10], precv.at[10], where, fold_small)
    early = 2 * Y_EARLY
    summed = 2 * X_EARLY if line else 0
    for p in range(early, 6):
        big[p].to_y().start()
    for copy in loads:
        copy.wait()
    for p in range(early):
        if p < summed:
            big[p].begin_z()
        else:
            big[p].begin_x()

    row64 = lax.broadcasted_iota(jnp.int32, (64, length), 0)

    def rows_of(blk):
        return pl.ds(pl.multiple_of(blk * BLK, BLK), BLK)

    own_seq = 2 * y

    def keep_or_send(middle, blk, r):
        seq = 1 if middle else own_seq
        i = 4 * seq + blk - 3 * t
        mine = (i >= 0) & (i < 3)

        @pl.when(mine)
        def _():
            rs = rows_of(i)
            dz1_ref[rs, :] += r

        @pl.when(jnp.logical_not(mine))
        def _():
            sbuf[1 if middle else 0, rows_of(blk), :] = r.astype(BF)

    def into_middle(n, _):
        keep_or_send(True, n, dg(dq2[:, rows_of(n)], wts_ref[0], 0, 0))
        return 0

    dq0, dq1, dq2 = [dq_s.at[g] for g in range(3)]

    def into_own(n, _):
        r = dg(dq0[:, rows_of(n)], wts_ref[0], 0, 0) + dg(dq1[:, rows_of(n)], wts_ref[1], 0, 0)
        keep_or_send(False, n, r)
        return 0

    far = 2 * (1 - y)
    half_copy = pltpu.make_async_remote_copy(
        src_ref=sbuf.at[1, rows_of(far + 1 - c)], dst_ref=rhalf, send_sem=send.at[12],
        recv_sem=recv.at[3], device_id={"tensor": core}, device_id_type=MESH,
    )
    far_copy = pltpu.make_async_remote_copy(
        src_ref=hsum, dst_ref=rmid.at[c], send_sem=send.at[13], recv_sem=recv.at[4 + c],
        device_id={"tensor": 2 * (1 - y) + y}, device_id_type=MESH,
    )
    core_copies = []
    for i in range(3):
        middle, blk = block_of(core, i)
        core_copies.append((
            middle,
            pltpu.make_async_remote_copy(
                src_ref=sbuf.at[middle, rows_of(blk)], dst_ref=rcore.at[i], send_sem=send.at[14 + i],
                recv_sem=recv.at[i], device_id={"tensor": core}, device_id_type=MESH,
            ),
        ))

    def unit(u, _):
        g = (u // 3 + 1) % 3
        h = u % 3

        @pl.when(u == 1)
        def _():
            for copy in go_core:
                copy.wait_recv()
            small_core.wait_recv()
            sv[0] = (go_ref[0].astype(F32) + rgo[0].astype(F32)).astype(BF)
            so[0] = (go_ref[2].astype(F32) + rgo[1].astype(F32)).astype(BF)
            thin[0].to_y().start()
            a, b = small_ref[...], tc[...]
            swapped = jnp.concatenate([b[0:8], b[9:10], b[8:9], b[11:12], b[10:11], b[12:16]])
            tv[...] = a + swapped

        @pl.when(u == 3)
        def _():
            for k in range(3):
                so[1 + k] = jnp.dot(dq_s[1, pl.ds(192 * k, 192), :], xab_ref[0], preferred_element_type=F32).astype(BF)
                thin[1 + k].to_y().start()

        @pl.when(u == 6)
        def _():
            lax.fori_loop(0, 4, into_middle, 0)
            half_copy.start()

        for k, steps in UNIT_STEPS.items():
            @pl.when(u == k)
            def _(steps=steps):
                for stage, p in steps:
                    getattr(big[p], stage)()

        @pl.when(u == 7)
        def _():
            half_copy.wait_recv()
            hsum[...] = (sbuf[1, rows_of(far + c), :].astype(F32) + rhalf[...].astype(F32)).astype(BF)
            far_copy.start()

        @pl.when(h == 0)
        def _():
            for blk in range(4):
                pltpu.make_async_copy(do_in.at[0, pl.ds(0, 192)], do_ref.at[g, blk], landed.at[g * 4 + blk]).wait()

        same = (row64 == seg_ref[pl.ds(jnp.where(g == 2, 1, own_seq), 1), :]).astype(F32)
        ro = pl.multiple_of(h * 192, 64)
        qh, kh, vh = pl.ds(ro, 64), pl.ds(ro + 64, 64), pl.ds(ro + 128, 64)
        l1, l2, l3 = split3(-lse_ref[g * 3 + h])
        qa[0:64, :] = qkv_ref[g, h, 0:64, :]
        qa[64:128, :] = jnp.where(row64 == 8, l1, jnp.where(row64 == 9, l2, jnp.where(row64 == 10, l3, same))).astype(BF)
        key_mark = jnp.where(row64 >= 8, 1.0, (same - 1.0) * BIG).astype(BF)
        ka[...] = jnp.concatenate([qkv_ref[g, h, 64:128, :], key_mark], axis=0).T
        va[...] = jnp.concatenate([qkv_ref[g, h, 128:192, :], jnp.ones((64, length), BF)], axis=0).T
        hs = pl.ds(pl.multiple_of(h * 64, 64), 64)
        for b in range(4):
            bs = slice(b * BLK, (b + 1) * BLK)
            do = do_ref[g, b, hs, :]
            e1, e2, e3 = split3(-jnp.sum(do.astype(F32) * o_ref[g, b, hs, :].astype(F32), axis=0, keepdims=True))
            da[0:64, bs] = do
            rb = row64[:, bs]
            da[64:128, bs] = jnp.where(rb == 8, e1, jnp.where(rb == 9, e2, jnp.where(rb == 10, e3, 0.0))).astype(BF)
        dk[...] = jnp.zeros_like(dk)
        dv[...] = jnp.zeros_like(dv)

        def chunk(n, _):
            cs = pl.ds(pl.multiple_of(n * 512, 512), 512)
            s = jnp.dot(ka[...], qa[:, cs], preferred_element_type=F32)
            p = jnp.exp2(s)
            dp = jnp.dot(va[...], da[:, cs], preferred_element_type=F32)
            pb = p.astype(BF)
            ds = (p * dp).astype(BF)
            dv[...] += dg(da[0:64, cs], pb, 1, 1)
            dk[...] += dg(qa[0:64, cs], ds, 1, 1)
            dq = jnp.dot(qkv_ref[g, h, 64:128, :], ds, preferred_element_type=F32)
            dq_s[g, qh, cs] = (dq * (HEAD_DIM ** (-0.5))).astype(BF)
            return 0

        lax.fori_loop(0, length // 512, chunk, 0)
        dq_s[g, kh, :] = (dk[...] * math.log(2.0)).astype(BF)
        dq_s[g, vh, :] = dv[...].astype(BF)

        @pl.when(u >= 6)
        def _():
            rows = pl.ds(ro, 192)
            r = jnp.dot(dq_s[0, rows, :], xab_ref[0], preferred_element_type=F32)
            sv[1 + h] = (r + jnp.dot(dq_s[2, rows, :], xab_ref[1], preferred_element_type=F32)).astype(BF)

        return 0

    lax.fori_loop(0, 9, unit, 0)
    ones = jnp.ones((8, length), BF)
    tv[12:13, 0:576] = (dg(ones, dq_s[0], 1, 1) + dg(ones, dq_s[2], 1, 1))[0:1]
    tv[13:14, 0:576] = dg(ones, dq_s[1], 1, 1)[0:1]
    to[...] = tv[...]
    tiny.to_y().start()
    lax.fori_loop(0, 4, into_own, 0)
    for middle, copy in core_copies:
        copy.start()

    named = {"p%d" % p: piece for p, piece in enumerate(big)}
    named.update({"w%d" % p: piece for p, piece in enumerate(thin)})
    named["t"] = tiny
    for k, (stage, name) in enumerate(TAIL_STEPS):
        getattr(named[name], stage)()
        if k == TAIL_INPUT:
            for i in range(3):
                core_copies[i][1].wait_recv()
                middle, blk = block_of(t, i)
                rs = pl.ds(i * BLK, BLK)

                @pl.when(middle == 0)
                def _():
                    din_ref[rs, :] = (dz1_ref[rs, :] + rcore[i].astype(F32)).astype(BF)

                @pl.when(middle == 1)
                def _():
                    k = blk % 2
                    pltpu.make_async_copy(hsum, rmid.at[k], recv.at[4 + k]).wait()
                    din_ref[rs, :] = (dz1_ref[rs, :] + rcore[i].astype(F32) + rmid[k].astype(F32)).astype(BF)

    for p, piece in enumerate(big):
        piece.finish(p >= early)
    for piece in thin + [tiny]:
        piece.finish()
    for copy in [c for _, c in core_copies] + [half_copy, far_copy] + go_core + [small_core]:
        copy.wait_send()
    for cond, copy in pending:
        if cond is None:
            copy.wait_send()
        else:
            pl.when(cond)(copy.wait_send)

def finish(
    out_in, din_in, ff_in, fs_in, sm,
    out_o, din_o, gwq, gbq, gwk, gwv, gbv, gwo, gbo, gg1, gs1, gwin, gbin, gwback, gbback, gg2, gs2,
    out_v, din_v, ff, fs, win_v, wback_v, q_v, wo_v, local,
):
    loads = [
        pltpu.make_async_copy(ff_in, ff, local.at[0]),
        pltpu.make_async_copy(fs_in, fs, local.at[1]),
        pltpu.make_async_copy(out_in, out_v, local.at[2]),
        pltpu.make_async_copy(din_in, din_v, local.at[3]),
    ]
    start_all(loads)
    stores = []

    def store(src, dst):
        copy = pltpu.make_async_copy(src, dst, local.at[4 + len(stores)])
        copy.start()
        stores.append(copy)

    for k, ref in ((0, gbo), (1, gg1), (2, gs1), (8, gbin), (3, gbback), (4, gg2), (5, gs2)):
        ref[...] = sm[k : k + 1, :].reshape(768)
    heads = sm[12:13, 0:576]
    for k, ref in ((0, gbq), (2, gbv)):
        ref[...] = jnp.concatenate([heads[:, 192 * h + 64 * k : 192 * h + 64 * k + 64] for h in range(3)], axis=1).reshape(192)
    loads[0].wait()
    for ch in range(3):
        cs = slice(ch * BLK, (ch + 1) * BLK)
        wback_v[cs, :] = ff[2 * ch + 1].T.astype(F32)
        win_v[:, cs] = ff[2 * ch].astype(F32)
    store(wback_v, gwback)
    store(win_v, gwin)
    loads[2].wait()
    store(out_v, out_o)
    loads[3].wait()
    store(din_v, din_o)
    loads[1].wait()
    wo_v[...] = fs[0].astype(F32)
    store(wo_v, gwo)
    for k, ref in enumerate((gwq, gwk, gwv)):
        for h in range(3):
            q_v[k, 64 * h : 64 * h + 64, :] = fs[1 + h, 64 * k : 64 * k + 64, :].astype(F32)
        store(q_v.at[k], ref)
    for copy in stores:
        copy.wait()


def vm(*shape, dtype=BF):
    return pltpu.VMEM(shape, dtype)


def sds(*shape, dtype=BF):
    return jax.ShapeDtypeStruct(shape, dtype)


VM = pl.BlockSpec(memory_space=pltpu.VMEM)
ANY = pl.BlockSpec(memory_space=pl.ANY)


def params(cid):
    return pltpu.CompilerParams(collective_id=cid, has_side_effects=True, vmem_limit_bytes=62 * 2**20)


def local_step(
    line,
    layer_input, segment_ids, w_query, b_query, w_key, w_value, b_value, w_out, b_out, first_gain, first_shift,
    w_in, b_in, w_back, b_back, second_gain, second_shift, cotangent,
):
    dma = pltpu.SemaphoreType.DMA
    qkv, o, lse, xab, wts, out, dz1, do, gf, go, small = pl.pallas_call(
        partial(forward, line),
        out_shape=(
            sds(3, 3, 192, 1024), sds(3, 4, 192, BLK), sds(9, 1, 1024, dtype=F32), sds(2, 1024, 768), sds(2, 576, 768),
            sds(768, 768), sds(768, 768, dtype=F32), sds(3, 768, BLK), sds(2, 3, 2, 768, BLK), sds(4, 192, 768),
            sds(16, 768, dtype=F32),
        ),
        in_specs=[VM, ANY] + [VM] * 13 + [ANY] * 3,
        out_specs=(ANY, ANY, VM, ANY, ANY, VM, ANY, VM, VM, VM, VM),
        scratch_shapes=[
            vm(3, 3, 192, 1024), vm(3, 4, 192, BLK), vm(2, 1024, 768), vm(2, 576, 768),
            vm(8, 768, dtype=F32), vm(3, 8, 768, dtype=F32), vm(576, 1, dtype=F32),
            vm(128, 1024), vm(128, 1024), vm(80, 1024),
            vm(768, 768), vm(3, 768, BLK), vm(768, 768), vm(768, 3072), vm(3072, 768),
            vm(768, 768), vm(768, 768), vm(768, 768, dtype=F32), vm(768, 1, dtype=F32), vm(768, 3072), vm(768, 3072),
            vm(768, 768, dtype=F32), vm(768, 768), vm(768, 768),
            vm(3, 2, 768, BLK), vm(3, 2, 768, BLK), vm(max(Y_EARLY, 1), 2, 768, BLK), vm(max(X_EARLY, 1), 2, 768, BLK),
            dma((72,)), dma((72,)), dma((16,)),
        ],
        compiler_params=params(0),
        name="forward_and_feed_forward",
    )(
        layer_input, cotangent, w_query.T, w_key.T, w_value.T, b_query, b_value, b_in,
        b_out, first_gain, first_shift, b_back, second_gain, second_shift, segment_ids, w_out, w_in, w_back,
    )

    piece, slab, tiny = vm(6, 768, BLK), vm(4, 192, 768), vm(16, 768, dtype=F32)
    din, ff, fs, sm = pl.pallas_call(
        partial(k3, line),
        out_shape=(sds(768, 768), sds(6, 768, BLK), sds(4, 192, 768), sds(16, 768, dtype=F32)),
        in_specs=[VM, VM, VM, VM, VM, VM, ANY, ANY, ANY, VM, VM],
        out_specs=(VM, VM, VM, VM),
        scratch_shapes=[
            vm(768, 768, dtype=F32),
            vm(3, 4, 192, BLK), vm(3, 576, 1024), vm(128, 1024), vm(1024, 128), vm(1024, 128), vm(128, 1024),
            vm(64, 1024, dtype=F32), vm(64, 1024, dtype=F32), vm(2, 1024, 768),
            vm(3, BLK, 768), vm(2, BLK, 768), vm(BLK, 768), vm(BLK, 768),
            piece, piece, piece, piece, piece, slab, slab, slab, slab, slab, slab, vm(2, 192, 768),
            tiny, tiny, tiny, tiny, tiny, tiny, tiny,
            dma((11, 5)), dma((11, 5)), dma((17,)), dma((9,)), dma((12,)), dma((7,)),
        ],
        compiler_params=params(1),
        name="attention_backward",
    )(qkv, segment_ids, o, lse, xab, wts, do, dz1, gf, go, small)
    if not line:
        ff, fs = lax.psum((ff, fs), "dp")
        sm = lax.psum(sm, "dp")
    row = sds(768, dtype=F32)
    cols, thin = sds(192, 768, dtype=F32), sds(192, dtype=F32)
    square = sds(768, 768, dtype=F32)
    outs = pl.pallas_call(
        finish,
        out_shape=(
            sds(768, 768), sds(768, 768), cols, thin, cols, cols, thin, sds(192, 768, dtype=F32),
            row, row, row, square, row, square, row, row, row,
        ),
        in_specs=[ANY, ANY, ANY, ANY, VM],
        out_specs=(ANY, ANY, ANY, VM, ANY, ANY, VM, ANY, VM, VM, VM, ANY, VM, ANY, VM, VM, VM),
        scratch_shapes=[
            vm(768, 768), vm(768, 768), vm(6, 768, BLK), vm(4, 192, 768), vm(768, 768, dtype=F32), vm(768, 768, dtype=F32),
            vm(3, 192, 768, dtype=F32), vm(192, 768, dtype=F32), dma((16,)),
        ],
        compiler_params=pltpu.CompilerParams(vmem_limit_bytes=62 * 2**20),
        name="results",
    )(out, din, ff, fs, sm)
    return (*outs[:2], outs[2].T, outs[3], outs[4].T, outs[5].T, *outs[6:])


def solution(mesh):
    rows = P(("dp", "tensor"), None)
    in_specs = (
        rows, P("dp", None), P(None, "tensor"), P("tensor"), P(None, "tensor"), P(None, "tensor"), P("tensor"),
        P("tensor", None), P(), P(), P(), P(None, "tensor"), P("tensor"), P("tensor", None), P(), P(), P(), rows,
    )
    out_specs = (
        rows, rows, P(None, "tensor"), P("tensor"), P(None, "tensor"), P(None, "tensor"), P("tensor"),
        P("tensor", None), P(), P(), P(), P(None, "tensor"), P("tensor"), P("tensor", None), P(), P(), P(),
    )
    line = mesh.shape["dp"] == 8
    return jax.shard_map(partial(local_step, line), mesh=mesh, in_specs=in_specs, out_specs=out_specs, check_vma=False)
```

```python
import math
from functools import partial

import jax
import jax.numpy as jnp
from jax import lax
from jax.experimental import pallas as pl
from jax.experimental.pallas import tpu as pltpu
from jax.sharding import PartitionSpec as P

F32 = jnp.float32
BF = jnp.bfloat16
MESH = pl.DeviceIdType.MESH
HEAD_DIM = 64
EPSILON = 1e-05
BIG = 1e30
LOG2E = 1.0 / math.log(2.0)
QSCALE = HEAD_DIM ** (-0.5) * LOG2E
BLK = 256
Y_EARLY = 3
X_EARLY = 1
SPLIT = (2, 3, 4, 5)
STEPS = {
    3: (("after_end", "p0"), ("after_x", "p1"),),
    4: (("after_x", "p2"), ("after_y", "w0"),),
    6: (("after_y", "p3"),),
    7: (("after_mate", "p0"), ("after_end", "p1"), ("after_x", "w0"),),
    8: (("after_end", "p2"), ("after_y", "w1"),),
    9: (("after_x", "p3"),),
    10: (("after_end", "w0"),),
    11: (("after_mate", "p1"), ("after_x", "w1"), ("after_y", "p4"),),
    12: (("after_mate", "p2"), ("after_end", "p3"),),
    13: (("after_y", "w2"),),
    14: (("after_mate", "w0"), ("after_end", "w1"), ("after_x", "p4"),),
    16: (("after_mate", "p3"), ("after_x", "w2"), ("after_y", "p5"),),
    17: (("after_end", "p4"),),
}
FIRST_TAIL = (
    ("after_mate", "w1"),
    ("after_x", "p5"),
    ("after_y", "w3"),
)
TAIL_INPUT = 14
TAIL_STEPS = (
    ("after_y", "w4"),
    ("after_y", "w5"),
    ("after_final", "p2"),
    ("after_end", "w2"),
    ("after_mate", "p4"),
    ("after_final", "p3"),
    ("after_y", "t"),
    ("after_x", "w3"),
    ("after_end", "p5"),
    ("after_x", "w4"),
    ("after_end", "w3"),
    ("after_x", "w5"),
    ("after_mate", "w2"),
    ("after_end", "w4"),
    ("after_end", "w5"),
    ("after_final", "p4"),
    ("after_mate", "p5"),
    ("after_mate", "w3"),
    ("after_x", "t"),
    ("after_mate", "w4"),
    ("after_mate", "w5"),
    ("after_end", "t"),
    ("after_final", "p5"),
    ("after_mate", "t"),
)


def dg(a, b, ca, cb):
    return lax.dot_general(a, b, (((ca,), (cb,)), ((), ())), preferred_element_type=F32)


def where_am_i():
    t = lax.axis_index("tensor")
    d = lax.axis_index("dp")
    core = t + 1 - 2 * (t % 2)
    across = (t + 2) % 4
    diag = 3 - t
    side = d + 1 - 2 * (d % 2)
    return t, d, core, across, diag, side


def block_of(t, i):
    b = 3 * t + i
    middle = (b // 4) % 2
    return middle, b % 4


def greet(devices):
    barrier = pltpu.get_barrier_semaphore()
    for dev in devices:
        pl.semaphore_signal(barrier, inc=1, device_id=dev, device_id_type=MESH)
    pl.semaphore_wait(barrier, len(devices))


def half_rows(half, total, pieces, i):
    n = total // 2 // pieces
    return pl.ds(pl.multiple_of(half * (total // 2) + i * n, n), n)


class Copies:
    def __init__(self, send, recv):
        self.send, self.recv, self.used = send, recv, 0

    def new(self, src, dst, **device):
        k = self.used
        self.used += 1
        return pltpu.make_async_remote_copy(
            src_ref=src,
            dst_ref=dst,
            send_sem=self.send.at[k],
            recv_sem=self.recv.at[k],
            device_id=device,
            device_id_type=MESH,
        )


def start_all(copies):
    for copy in copies:
        copy.start()


def layer_stats(z):
    mean = jnp.mean(z, axis=-1, keepdims=True)
    cen = z - mean
    var = jnp.mean(cen * cen, axis=-1, keepdims=True)
    inv = lax.rsqrt(var + EPSILON)
    return cen * inv, inv


def forward(
    line,
    x_ref, cot_in, wq_ref, wk_ref, wv_ref, bq_ref, bv_ref, bin_ref, v0, v1, v2, v3, v4, v5, seg_ref,
    wout_ref, win_ref, wback_ref,
    qkv_out, o_out, lse_ref, xab_out, wts_out, out_out, dz1_out, do_out, gf_out, go_out, small_ref,
    out_ref, do_ref, gf_ref, go_ref, qkv, o_v, xab, w_v, bias_ref, biasg_ref, bcol, qa, ka, va,
    cot_ref, ot, wo, wi, wb, h1b, h1t, xh1, inv1, gg, gp, z2, dz2b, dz2t, gsend, rc, ry, rx, send, recv, local,
):
    length = 1024
    t, d, core, across, diag, side = where_am_i()
    y, c = t // 2, t % 2
    half = d % 2
    x_early = X_EARLY if line else 0

    rows_out, rows_local = [], []
    cp = Copies(send, recv)
    cp.used = 12
    for i in range(3):
        middle, blk = block_of(t, i)
        src = x_ref.at[pl.ds(i * BLK, BLK)]
        dst = xab.at[middle, pl.ds(pl.multiple_of(blk * BLK, BLK), BLK)]
        rows_local.append(pltpu.make_async_copy(src, dst, local.at[i]))
        rows_out.append(cp.new(src, dst, tensor=core))
    own = [
        pltpu.make_async_copy(wout_ref, wo.at[pl.ds(0, 192)], local.at[12]),
        pltpu.make_async_copy(win_ref, wi.at[:, pl.ds(0, 768)], local.at[13]),
        pltpu.make_async_copy(wback_ref, wb.at[pl.ds(0, 768)], local.at[14]),
        pltpu.make_async_copy(cot_in, cot_ref, local.at[15]),
    ]
    start_all(rows_local + own)

    for k, ref in enumerate((wq_ref, wk_ref, wv_ref)):
        for h in range(3):
            n = 192 * h + 64 * k
            w_v[0, n : n + 64, :] = ref[64 * h : 64 * h + 64, :]
    bias_ref[...] = jnp.zeros((8, 768), F32)
    bias_ref[0:1, :] = bin_ref[...].astype(F32).reshape(1, 768)
    bq, bv = bq_ref[...].astype(F32).reshape(1, 192), bv_ref[...].astype(F32).reshape(1, 192)
    parts = []
    for h in range(3):
        parts += [bq[:, 64 * h : 64 * h + 64], jnp.zeros((1, 64), F32), bv[:, 64 * h : 64 * h + 64]]
    bias_ref[1:2, 0:576] = jnp.concatenate(parts, axis=1)

    greet([{"tensor": core}, {"tensor": across}, {"tensor": diag}, {"dp": side}])

    mixed = (t == 1) | (t == 2)
    k_out = jnp.where(mixed, 0, 1)
    block_out = pl.ds(pl.multiple_of((2 * y + k_out) * BLK, BLK), BLK)
    block_in = pl.ds(pl.multiple_of((2 * (1 - y) + c) * BLK, BLK), BLK)
    n = cp.used
    cross_out = cp.new(xab.at[1, block_out], xab.at[1, block_out], tensor=2 * (1 - y) + k_out)
    cross_arrived = pltpu.make_async_remote_copy(
        src_ref=xab.at[1, block_out], dst_ref=xab.at[1, block_in], send_sem=send.at[n], recv_sem=recv.at[n],
        device_id={"tensor": core}, device_id_type=MESH,
    )
    cross_forward = cp.new(xab.at[1, block_in], xab.at[1, block_in], tensor=core)
    wp_first, wp_second = [], []
    for i in range(3):
        part = half_rows(half, 576, 3, i)
        wp_first.append(cp.new(w_v.at[0, part], w_v.at[1, part], tensor=across))
        wp_second.append(cp.new(w_v.at[1, part], w_v.at[1, part], dp=side))
    bias_out = [
        cp.new(bias_ref, biasg_ref.at[0], tensor=core),
        cp.new(bias_ref, biasg_ref.at[1], tensor=across),
        cp.new(bias_ref, biasg_ref.at[2], tensor=diag),
    ]
    part = half_rows(half, 192, 1, 0)
    place = pl.ds(part.start + 384, part.size)
    wo_first = cp.new(wout_ref.at[part], wo.at[place], tensor=across)
    wo_second = cp.new(wo.at[place], wo.at[place], dp=side)
    wo_core = cp.new(wout_ref, wo.at[pl.ds(192, 192)], tensor=core)
    wo_diag = cp.new(wo.at[pl.ds(384, 192)], wo.at[pl.ds(576, 192)], tensor=core)

    def lanes(j):
        return pl.ds(768 * j, 768)

    in_core = cp.new(win_ref, wi.at[:, lanes(1)], tensor=core)
    back_core = cp.new(wback_ref, wb.at[lanes(1)], tensor=core)
    in_first, in_second, in_diag, back_first, back_second, back_diag = [], [], [], [], [], []
    for i in range(3):
        part = half_rows(half, 768, 3, i)
        in_first.append(cp.new(win_ref.at[part], wi.at[part, lanes(2)], tensor=across))
        in_second.append(cp.new(wi.at[part, lanes(2)], wi.at[part, lanes(2)], dp=side))
        place = pl.ds(part.start + 2 * 768, part.size)
        back_first.append(cp.new(wback_ref.at[part], wb.at[place], tensor=across))
        back_second.append(cp.new(wb.at[place], wb.at[place], dp=side))
        for h in range(2):
            both = half_rows(h, 768, 3, i)
            in_diag.append(cp.new(wi.at[both, lanes(2)], wi.at[both, lanes(3)], tensor=core))
            m = h * 384 + i * 128
            back_diag.append(cp.new(wb.at[pl.ds(2 * 768 + m, 128)], wb.at[pl.ds(3 * 768 + m, 128)], tensor=core))

    peers = (t, core, across, diag)

    def heads_to_rows(group):
        found = []
        for j, dev in enumerate(peers):
            if group != 2 and j >= 2:
                continue
            for i in range(3):
                middle, blk = block_of(dev, i)
                slot = j + 2 if group == 1 else j
                src, dst = o_v.at[group, blk], ot.at[i, pl.ds(slot * 192, 192)]
                sem = recv.at[i * 4 + slot]
                if j == 0:
                    copy = pltpu.make_async_copy(src, dst, sem)
                else:
                    copy = pltpu.make_async_remote_copy(
                        src_ref=src, dst_ref=dst, send_sem=send.at[9 + i if group == 1 else 3 * (j - 1) + i],
                        recv_sem=sem, device_id={"tensor": dev}, device_id_type=MESH,
                    )
                found.append((j, (middle == 1) if group == 2 else (middle == 0), copy))
        return found

    def start_heads(group):
        for _, cond, copy in heads_to_rows(group):
            pl.when(cond)(copy.start)

    start_all(rows_out + bias_out + wp_first[:1])
    start_all([wo_core, in_core, back_core])
    va[64:80, :] = jnp.ones((16, length), BF)
    row64 = lax.broadcasted_iota(jnp.int32, (64, length), 0)
    factor = jnp.where(lax.broadcasted_iota(jnp.int32, (576, 1), 0) % 192 < 64, QSCALE, 1.0)

    def outgoing(g):
        return [
            pltpu.make_async_copy(qkv.at[g], qkv_out.at[g], local.at[4 + 2 * (g % 3)]),
            pltpu.make_async_copy(o_v.at[g], o_out.at[g], local.at[5 + 2 * (g % 3)]),
        ]

    def at(n, k, copies_recv, copies_start=()):
        @pl.when(n == k)
        def _():
            for copy in copies_recv:
                copy.wait_recv()
            start_all(copies_start)

    def unit(u, _):
        g = (2 * (u // 3)) % 3
        h = u % 3
        par = jnp.where(g == 1, 1, 0)
        middle = jnp.where(g == 2, 1, 0)

        at(u, 1, wp_first[:1], wp_second[:1])

        @pl.when(u == 3)
        def _():
            cross_arrived.wait_recv()
            cross_forward.start()
            start_heads(0)
            cross_forward.wait_recv()

        at(u, 4, wp_first[1:2], wp_second[1:2])
        at(u, 5, wp_first[2:3], wp_second[2:3])

        @pl.when(u == 6)
        def _():
            start_heads(2)
            start_all(in_first[2:] + back_first)

        at(u, 6, [wo_first], [wo_second])
        at(u, 6, wp_second + [bias_out[1]])
        at(u, 7, in_first[:1], in_second[:1])
        at(u, 8, in_first[1:2], in_second[1:2])
        at(u, 8, [wo_second], [wo_diag])

        @pl.when(h == 0)
        def _():
            @pl.when(u > 0)
            def _():
                start_all(outgoing(jnp.where(g == 2, 0, 2)))

            @pl.when(par == 0)
            def _():
                bcol[...] = jnp.transpose(bias_ref[...])[0:576, 1:2]

            @pl.when(par == 1)
            def _():
                bcol[...] = jnp.transpose(biasg_ref[1])[0:576, 1:2]

            col = bcol[...]

            def body(n, _):
                cs = pl.ds(pl.multiple_of(n * BLK, BLK), BLK)
                r = (dg(w_v[par], xab[middle, cs, :], 1, 1) + col) * factor
                for k in range(3):
                    qkv[g, k, :, cs] = r[192 * k : 192 * (k + 1)].astype(BF)
                return 0

            lax.fori_loop(0, length // BLK, body, 0)
            same = (row64 == seg_ref[pl.ds(jnp.where(g == 2, 1, 2 * y), 1), :]).astype(F32)
            qa[64:128, :] = same.astype(BF)
            ka[64:128, :] = ((same - 1.0) * BIG).astype(BF)

        qa[0:64, :] = qkv[g, h, 0:64, :]
        ka[0:64, :] = qkv[g, h, 64:128, :]
        va[0:64, :] = qkv[g, h, 128:192, :]
        s = jnp.dot(ka[...].T, qa[...], preferred_element_type=F32)
        m = jnp.max(s, axis=0, keepdims=True)
        p = jnp.exp2(s - m).astype(BF)
        o = jnp.dot(va[...], p, preferred_element_type=F32)
        total = o[64:65, :]
        res = (o[0:64] * (1.0 / total)).astype(BF)
        hs = pl.ds(pl.multiple_of(h * 64, 64), 64)
        for b in range(4):
            o_v[g, b, hs, :] = res[:, b * BLK : (b + 1) * BLK]
        lse_ref[g * 3 + h] = m + jnp.log2(total)
        return 0

    for copy in rows_local:
        copy.wait()
    for copy in rows_out:
        copy.wait_recv()
    start_all([cross_out] + wp_first[1:] + [wo_first] + in_first[:2])
    lax.fori_loop(0, 9, unit, 0)
    start_heads(1)
    tail = outgoing(1)
    tail.append(pltpu.make_async_copy(xab, xab_out, local.at[10]))
    tail.append(pltpu.make_async_copy(w_v, wts_out, local.at[11]))
    start_all(tail)

    b_out, gain1, shift1, b_back, gain2, shift2 = [v[...].reshape(1, 768) for v in (v0, v1, v2, v3, v4, v5)]
    own[0].wait()
    for copy in [wo_core, wo_diag, bias_out[0], bias_out[2]]:
        copy.wait_recv()
    for i in range(2):
        in_second[i].wait_recv()
        start_all(in_diag[2 * i : 2 * i + 2])
    for i in range(3):
        for slot in range(4):
            pltpu.make_async_copy(o_v.at[0, 0], ot.at[i, pl.ds(slot * 192, 192)], recv.at[i * 4 + slot]).wait()

    def first(i, _):
        rs = pl.ds(pl.multiple_of(i * BLK, BLK), BLK)
        z = x_ref[rs, :].astype(F32) + dg(ot[i], wo[...], 0, 0) + b_out
        xh, inv = layer_stats(z)
        xh1[rs, :] = xh
        inv1[rs, :] = inv
        h1b[rs, :] = (xh * gain1 + shift1).astype(BF)
        return 0

    lax.fori_loop(0, 3, first, 0)
    h1t[...] = h1b[...].T
    own[1].wait()

    def up(n, _):
        at(n, 1, in_first[2:], in_second[2:])
        at(n, 3, [in_core])
        at(n, 4, back_first[:1], back_second[:1])
        at(n, 6, in_second[2:], in_diag[4:])
        at(n, 7, back_first[1:2], back_second[1:2])
        at(n, 9, in_diag)
        at(n, 9, back_second[:1], back_diag[:2])
        at(n, 10, back_first[2:], back_second[2:])
        at(n, 11, back_second[1:2], back_diag[2:4])
        cs = pl.ds(pl.multiple_of(n * BLK, BLK), BLK)
        j = n // 3
        low = pl.ds(pl.multiple_of((n % 3) * BLK, BLK), BLK)
        bias = jnp.where(j == 0, bias_ref[0:1, low], biasg_ref[jnp.maximum(j - 1, 0), 0:1, low])
        u = jnp.dot(h1b[...], wi[:, cs], preferred_element_type=F32) + bias
        cdf = 0.5 * (1.0 + lax.erf(u * (2.0 ** -0.5)))
        pdf = jnp.exp(-0.5 * u * u) * (1.0 / math.sqrt(2.0 * math.pi))
        gg[:, cs] = (u * cdf).astype(BF)
        gp[:, cs] = (cdf + u * pdf).astype(BF)
        return 0

    lax.fori_loop(0, 12, up, 0)
    own[2].wait()
    back_core.wait_recv()

    def down_near(n, _):
        cs = pl.ds(pl.multiple_of(n * BLK, BLK), BLK)
        z2[:, cs] = jnp.dot(gg[:, 0:1536], wb[0:1536, cs], preferred_element_type=F32)
        return 0

    def down_far(n, _):
        cs = pl.ds(pl.multiple_of(n * BLK, BLK), BLK)
        z2[:, cs] += jnp.dot(gg[:, 1536:3072], wb[1536:3072, cs], preferred_element_type=F32)
        return 0

    lax.fori_loop(0, 3, down_near, 0)
    back_second[2].wait_recv()
    start_all(back_diag[4:])
    own[3].wait()
    for copy in back_diag:
        copy.wait_recv()
    lax.fori_loop(0, 3, down_far, 0)

    def second_norm(i, sums):
        rs = pl.ds(pl.multiple_of(i * BLK, BLK), BLK)
        h1 = xh1[rs, :] * gain1 + shift1
        xh, inv = layer_stats(h1 + z2[rs, :] + b_back)
        out_ref[rs, :] = (xh * gain2 + shift2).astype(BF)
        cot = cot_ref[rs, :].astype(F32)
        dxh = cot * gain2
        dz = inv * (dxh - jnp.mean(dxh, axis=-1, keepdims=True) - xh * jnp.mean(dxh * xh, axis=-1, keepdims=True))
        z2[rs, :] = dz
        dz2b[rs, :] = dz.astype(BF)
        return (
            sums[0] + jnp.sum(dz, axis=0, keepdims=True),
            sums[1] + jnp.sum(cot * xh, axis=0, keepdims=True),
            sums[2] + jnp.sum(cot, axis=0, keepdims=True),
        )

    zero = jnp.zeros((1, 768), F32)
    s3, s4, s5 = lax.fori_loop(0, 3, second_norm, (zero, zero, zero))
    small_ref[3:4, :] = s3
    small_ref[4:5, :] = s4
    small_ref[5:6, :] = s5
    out_copy = pltpu.make_async_copy(out_ref, out_out, local.at[16])
    out_copy.start()
    dz2t[...] = dz2b[...].T

    base = cp.used

    def to_core(stage, ch):
        k = base + stage * 3 + ch
        return pltpu.make_async_remote_copy(
            src_ref=gsend.at[ch], dst_ref=rc.at[ch], send_sem=send.at[k], recv_sem=recv.at[k],
            device_id={"tensor": core}, device_id_type=MESH,
        )

    def to_across(p):
        k = base + 6 + p
        return pltpu.make_async_remote_copy(
            src_ref=gf_ref.at[1, p // 2, p % 2], dst_ref=ry.at[p], send_sem=send.at[k], recv_sem=recv.at[k],
            device_id={"tensor": across}, device_id_type=MESH,
        )

    def to_side(p):
        k = base + 12 + p
        return pltpu.make_async_remote_copy(
            src_ref=gf_ref.at[0, p // 2, p % 2], dst_ref=rx.at[p], send_sem=send.at[k], recv_sem=recv.at[k],
            device_id={"dp": side}, device_id_type=MESH,
        )

    def back(m, _):
        stage = m // 6
        ch = (m % 6) // 2
        slot = 3 - 2 * stage - m % 2
        n = slot * 3 + ch
        cs = pl.ds(pl.multiple_of(n * BLK, BLK), BLK)
        low = pl.ds(pl.multiple_of(ch * BLK, BLK), BLK)
        g_back = jnp.dot(dz2t[...], gg[:, cs], preferred_element_type=F32)
        du = (dg(dz2b[...], wb[cs, :], 1, 1) * gp[:, cs].astype(F32)).astype(BF)
        gg[:, cs] = du
        small_ref[pl.ds(8 + slot, 1), low] = jnp.sum(du.astype(F32), axis=0, keepdims=True)
        g_in = jnp.dot(h1t[...], du, preferred_element_type=F32)

        @pl.when(m % 2 == 0)
        def _():
            pl.when(stage == 1)(to_core(0, ch).wait_send)
            gsend[ch, 0] = g_in.astype(BF)
            gsend[ch, 1] = g_back.astype(BF)
            to_core(stage, ch).start()

        @pl.when(m % 2 == 1)
        def _():
            to_core(stage, ch).wait_recv()
            gf_ref[1 - stage, ch, 0] = (g_in + rc[ch, 0].astype(F32)).astype(BF)
            gf_ref[1 - stage, ch, 1] = (g_back + rc[ch, 1].astype(F32)).astype(BF)
            for p in range(Y_EARLY):
                pl.when((stage == 0) & (ch == p // 2))(to_across(p).start)

        return 0

    lax.fori_loop(0, 12, back, 0)

    def gf_copy(p):
        k = (0, p // 2, p % 2)
        return pltpu.make_async_copy(gf_ref.at[k], gf_out.at[k], local.at[18 + p])

    gf_other = pltpu.make_async_copy(gf_ref.at[1], gf_out.at[1], local.at[17])
    start_all([gf_other] + [gf_copy(p) for p in range(Y_EARLY, 6)])

    def take(p, arrived):
        k = (0, p // 2, p % 2)
        gf_ref[k] = (gf_ref[k].astype(F32) + arrived[p].astype(F32)).astype(BF)

    for p in range(x_early):
        to_across(p).wait_recv()
        take(p, ry)
        to_side(p).start()

    def into_h(n, _):
        cs = pl.ds(pl.multiple_of(n * BLK, BLK), BLK)
        z2[:, cs] += dg(gg[...], wi[cs, :], 1, 1)
        return 0

    lax.fori_loop(0, 3, into_h, 0)

    def first_norm(i, sums):
        rs = pl.ds(pl.multiple_of(i * BLK, BLK), BLK)
        dh = z2[rs, :]
        xh = xh1[rs, :]
        dxh = dh * gain1
        dz = inv1[rs, :] * (dxh - jnp.mean(dxh, axis=-1, keepdims=True) - xh * jnp.mean(dxh * xh, axis=-1, keepdims=True))
        z2[rs, :] = dz
        dzb = dz.astype(BF)
        dz2b[rs, :] = dzb
        do_ref[i] = dg(wo[...], dzb, 1, 1).astype(BF)
        return (
            sums[0] + jnp.sum(dz, axis=0, keepdims=True),
            sums[1] + jnp.sum(dh * xh, axis=0, keepdims=True),
            sums[2] + jnp.sum(dh, axis=0, keepdims=True),
        )

    s0, s1, s2 = lax.fori_loop(0, 3, first_norm, (zero, zero, zero))
    dz1_copy = pltpu.make_async_copy(z2, dz1_out, local.at[0])
    do_copy = pltpu.make_async_copy(do_ref, do_out, local.at[1])
    start_all([dz1_copy, do_copy])
    small_ref[0:1, :] = s0
    small_ref[1:2, :] = s1
    small_ref[2:3, :] = s2
    for j in range(4):
        rows = pl.ds(192 * j, 192)
        acc = jnp.dot(ot[0, rows, :], dz2b[0:BLK, :], preferred_element_type=F32)
        acc += jnp.dot(ot[1, rows, :], dz2b[BLK : 2 * BLK, :], preferred_element_type=F32)
        acc += jnp.dot(ot[2, rows, :], dz2b[2 * BLK : 3 * BLK, :], preferred_element_type=F32)
        go_ref[j] = acc.astype(BF)
    go_copy = pltpu.make_async_copy(go_ref, go_out, local.at[2])
    go_copy.start()
    small_ref[6:8, :] = jnp.zeros((2, 768), F32)
    small_ref[12:16, :] = jnp.zeros((4, 768), F32)

    for group in range(3):
        for j, cond, copy in heads_to_rows(group):
            if j:
                pl.when(cond)(copy.wait_send)
    sent = rows_out + [cross_out, cross_forward] + wp_first + wp_second + bias_out
    sent += [wo_first, wo_second, wo_core, wo_diag, in_core, back_core]
    sent += in_first + in_second + in_diag + back_first + back_second + back_diag
    for copy in sent + [to_core(1, ch) for ch in range(3)]:
        copy.wait_send()
    for copy in outgoing(0) + outgoing(2) + tail + [dz1_copy, do_copy, out_copy, gf_other] + [gf_copy(p) for p in range(Y_EARLY, 6)]:
        copy.wait()
    for p in range(Y_EARLY):
        if p >= x_early:
            to_across(p).wait_recv()
            take(p, ry)
            gf_copy(p).start()
        to_across(p).wait_send()
    for p in range(x_early):
        to_side(p).wait()
        take(p, rx)
        gf_copy(p).start()
    for p in range(Y_EARLY):
        gf_copy(p).wait()
    go_copy.wait()


def split3(v):
    a = v.astype(BF).astype(F32)
    b = (v - a).astype(BF).astype(F32)
    return a, b, v - a - b


class Piece:
    def __init__(self, value, other, from_y, from_x, from_end, from_mate, final, send, recv, where, fold=None, split=False):
        self.value, self.other, self.final = value, other, final
        self.from_y, self.from_x, self.from_end, self.from_mate = from_y, from_x, from_end, from_mate
        self.send, self.recv, self.where, self.fold = send, recv, where, fold
        self.split = split

    def part(self, ref, which):
        if not self.split:
            return ref
        n = 768 // 2
        return ref.at[pl.ds(pl.multiple_of(which * n, n), n)]

    def mine(self, ref):
        return self.part(ref, self.where["half"])

    def copy(self, stage, src, dst, **device):
        return pltpu.make_async_remote_copy(
            src_ref=src, dst_ref=dst, send_sem=self.send.at[stage], recv_sem=self.recv.at[stage],
            device_id=device, device_id_type=MESH,
        )

    def to_y(self):
        return self.copy(0, self.other, self.from_y, tensor=self.where["across"])

    def to_x(self):
        away = 1 - self.where["half"]
        return self.copy(1, self.part(self.value, away), self.part(self.from_x, away), dp=self.where["side"])

    def to_inner(self):
        return self.copy(2, self.mine(self.value), self.mine(self.from_end), dp=self.where["pair"])

    def to_mate(self):
        return self.copy(3, self.mine(self.value), self.mine(self.from_mate), dp=self.where["mate"])

    def to_end(self):
        return self.copy(4, self.mine(self.final), self.mine(self.final), dp=self.where["pair"])

    def to_side(self):
        return self.copy(5, self.mine(self.final), self.mine(self.final), dp=self.where["side"])

    def add(self, arrived, into):
        into[...] = (self.value[...].astype(F32) + arrived[...].astype(F32)).astype(into.dtype)

    def add_mine(self, arrived, into):
        total = self.mine(self.value)[...].astype(F32) + self.mine(arrived)[...].astype(F32)
        self.mine(into)[...] = total.astype(into.dtype)

    def after_y(self):
        self.to_y().wait_recv()
        if self.fold is None:
            self.add(self.from_y, self.value)
        else:
            self.fold(self)
        self.begin_x()

    def begin_x(self):
        if self.where["line"]:
            self.to_x().start()
        else:
            self.final[...] = self.value[...]

    def after_x(self):
        if not self.where["line"]:
            return
        self.to_x().wait()
        self.add_mine(self.from_x, self.value)
        self.begin_z()

    def begin_z(self):
        pl.when(self.where["end"])(lambda: self.to_inner().start())

    def after_end(self):
        if not self.where["line"]:
            return

        @pl.when(self.where["inner"])
        def _():
            self.to_inner().wait_recv()
            self.add_mine(self.from_end, self.value)
            self.to_mate().start()

    def after_mate(self):
        if not self.where["line"]:
            return

        @pl.when(self.where["inner"])
        def _():
            self.to_mate().wait_recv()
            self.add_mine(self.from_mate, self.final)
            self.to_end().start()
            if self.split:
                self.to_side().start()

    def after_final(self):
        if not self.where["line"]:
            return

        @pl.when(self.where["end"])
        def _():
            self.to_end().wait_recv()
            self.to_side().start()

    def finish(self, had_y=True):
        if had_y:
            self.to_y().wait_send()
        if not self.where["line"]:
            return

        @pl.when(self.where["end"])
        def _():
            if not self.split:
                self.to_end().wait_recv()
            self.to_inner().wait_send()

        @pl.when(self.where["inner"])
        def _():
            self.to_mate().wait_send()
            self.to_end().wait_send()

        if self.split:
            self.to_side().wait()


def k3(
    line,
    qkv_in, seg_ref, o_in, lse_ref, xab_in, wts_in, do_in, dz1_in, gf_ref, go_in, small_ref,
    din_ref, ff_ref, fs_ref, sm_ref,
    qkv_ref, o_ref, xab_ref, wts_ref, go_ref, dz1_ref, do_ref, dq_s, qa, ka, va, da, dk, dv, sbuf, rcore, rmid, rhalf, hsum,
    fv, fy, fx, fe, fm, sv, so, sy, sx, se, sm, rgo, tv, to, tc, ty, tx, te, tm,
    psend, precv, send, recv, landed, local,
):
    length = 1024
    t, d, core, across, diag, side = where_am_i()
    y, c = t // 2, t % 2
    where = {"across": across, "side": side, "line": line, "half": d % 2}
    known = [{"tensor": core}, {"tensor": across}, {"tensor": diag}]
    if line:
        z = d // 2
        where["pair"] = d + 2 - 4 * (z % 2)
        where["mate"] = d + 2 - 4 * ((z + 1) % 2)
        where["end"] = (z == 0) | (z == 3)
        where["inner"] = (z == 1) | (z == 2)
        known += [{"dp": side}, {"dp": where["pair"]}]
    load_go, load_qkv, load_o, load_xab, load_wts, load_dz1 = [
        pltpu.make_async_copy(src, dst, local.at[6 + k])
        for k, (src, dst) in enumerate((
            (go_in, go_ref), (qkv_in, qkv_ref), (o_in, o_ref), (xab_in, xab_ref), (wts_in, wts_ref), (dz1_in, dz1_ref),
        ))
    ]
    loads = [pltpu.make_async_copy(gf_ref.at[0, p // 2, p % 2], fv.at[p], local.at[p]) for p in range(6)]
    start_all([load_go] + loads[:Y_EARLY] + [load_qkv, load_o] + loads[Y_EARLY:] + [load_xab, load_wts, load_dz1])
    barrier = pltpu.get_barrier_semaphore()
    for dev in known:
        pl.semaphore_signal(barrier, inc=1, device_id=dev, device_id_type=MESH)
    if line:
        @pl.when(where["inner"])
        def _():
            pl.semaphore_signal(barrier, inc=1, device_id={"dp": where["mate"]}, device_id_type=MESH)
            pl.semaphore_wait(barrier, len(known) + 1)

        @pl.when(where["end"])
        def _():
            pl.semaphore_wait(barrier, len(known))
    else:
        pl.semaphore_wait(barrier, len(known))

    pending = []
    peers = (t, core, across, diag)
    for i in range(3):
        middle, blk = block_of(t, i)
        for j, dev in enumerate(peers):
            src = do_in.at[i, pl.ds(192 * j, 192)]
            group = jnp.where(middle == 1, 2, j // 2)
            dst = do_ref.at[group, blk]
            sem = landed.at[group * 4 + blk]
            if j == 0:
                pltpu.make_async_copy(src, dst, sem).start()
                continue
            if j == 2:
                pl.when(middle == 0)(pltpu.make_async_copy(src, dst, sem).start)
                dev_to, cond = across, middle == 1
            elif j == 1:
                dev_to, cond = core, None
            else:
                dev_to, cond = jnp.where(middle == 1, diag, core), None
            copy = pltpu.make_async_remote_copy(
                src_ref=src, dst_ref=dst, send_sem=send.at[i * 3 + j - 1], recv_sem=sem,
                device_id={"tensor": dev_to}, device_id_type=MESH,
            )
            if cond is None:
                copy.start()
            else:
                pl.when(cond)(copy.start)
            pending.append((cond, copy))

    go_core = [
        pltpu.make_async_remote_copy(
            src_ref=go_in.at[2 * k + 1], dst_ref=rgo.at[k], send_sem=send.at[9 + k], recv_sem=recv.at[6 + k],
            device_id={"tensor": core}, device_id_type=MESH,
        )
        for k in range(2)
    ]
    small_core = pltpu.make_async_remote_copy(
        src_ref=small_ref, dst_ref=tc, send_sem=send.at[11], recv_sem=recv.at[8],
        device_id={"tensor": core}, device_id_type=MESH,
    )
    start_all(go_core + [small_core])
    big = [
        Piece(fv.at[p], gf_ref.at[1, p // 2, p % 2], fy.at[p], fx.at[p], fe.at[p], fm.at[p], ff_ref.at[p],
              psend.at[p], precv.at[p], where, split=line and p in SPLIT)
        for p in range(6)
    ]
    places = [(p, slice(0, 192)) for p in range(3)] + [(3, slice(64 * k, 64 * k + 64)) for k in range(3)]
    thin = [
        Piece(*[ref.at[p, rows] for ref in (sv, so, sy, sx, se, sm, fs_ref)], psend.at[6 + i], precv.at[6 + i], where)
        for i, (p, rows) in enumerate(places)
    ]

    def fold_small(piece):
        got = ty[...]
        add = jnp.concatenate([got[0:8], got[10:11], jnp.zeros((3, 768), F32), got[13:14], jnp.zeros((3, 768), F32)])
        tv[...] = tv[...] + add

    tiny = Piece(tv, to, ty, tx, te, tm, sm_ref, psend.at[12], precv.at[12], where, fold_small)
    early = Y_EARLY
    summed = X_EARLY if line else 0
    load_go.wait()
    for copy in go_core:
        copy.wait_recv()
    sv[0] = (go_ref[0].astype(F32) + rgo[0].astype(F32)).astype(BF)
    so[0] = (go_ref[2].astype(F32) + rgo[1].astype(F32)).astype(BF)
    thin[0].to_y().start()
    big[3].to_y().start()
    for copy in loads:
        copy.wait()
    for p in range(early):
        if p < summed:
            big[p].begin_z()
        else:
            big[p].begin_x()

    named = {"p%d" % p: piece for p, piece in enumerate(big)}
    named.update({"w%d" % p: piece for p, piece in enumerate(thin)})
    named["t"] = tiny
    row64 = lax.broadcasted_iota(jnp.int32, (64, length), 0)

    def rows_of(blk):
        return pl.ds(pl.multiple_of(blk * BLK, BLK), BLK)

    own_seq = 2 * y

    def keep_or_send(middle, blk, r):
        seq = 1 if middle else own_seq
        i = 4 * seq + blk - 3 * t
        mine = (i >= 0) & (i < 3)

        @pl.when(mine)
        def _():
            rs = rows_of(i)
            dz1_ref[rs, :] += r

        @pl.when(jnp.logical_not(mine))
        def _():
            sbuf[1 if middle else 0, rows_of(blk), :] = r.astype(BF)

    def into_middle(n, _):
        keep_or_send(True, n, dg(dq2[:, rows_of(n)], wts_ref[0], 0, 0))
        return 0

    dq0, dq1, dq2 = [dq_s.at[g] for g in range(3)]

    def into_own(n, _):
        r = dg(dq0[:, rows_of(n)], wts_ref[0], 0, 0) + dg(dq1[:, rows_of(n)], wts_ref[1], 0, 0)
        keep_or_send(False, n, r)
        return 0

    far = 2 * (1 - y)
    half_copy = pltpu.make_async_remote_copy(
        src_ref=sbuf.at[1, rows_of(far + 1 - c)], dst_ref=rhalf, send_sem=send.at[12],
        recv_sem=recv.at[3], device_id={"tensor": core}, device_id_type=MESH,
    )
    far_copy = pltpu.make_async_remote_copy(
        src_ref=hsum, dst_ref=rmid.at[c], send_sem=send.at[13], recv_sem=recv.at[4 + c],
        device_id={"tensor": 2 * (1 - y) + y}, device_id_type=MESH,
    )
    core_copies = []
    for i in range(3):
        middle, blk = block_of(core, i)
        core_copies.append((
            middle,
            pltpu.make_async_remote_copy(
                src_ref=sbuf.at[middle, rows_of(blk)], dst_ref=rcore.at[i], send_sem=send.at[14 + i],
                recv_sem=recv.at[i], device_id={"tensor": core}, device_id_type=MESH,
            ),
        ))

    def unit(u, _):
        g = (u % 3 + 1) % 3
        h = u // 3

        @pl.when(u == 1)
        def _():
            small_core.wait_recv()
            a, b = small_ref[...], tc[...]
            swapped = jnp.concatenate([b[0:8], b[9:10], b[8:9], b[11:12], b[10:11], b[12:16]])
            tv[...] = a + swapped

        @pl.when(u == 2)
        def _():
            big[4].to_y().start()

        @pl.when(u == 4)
        def _():
            big[5].to_y().start()

        @pl.when(u == 8)
        def _():
            load_wts.wait()
            load_dz1.wait()
            lax.fori_loop(0, 4, into_middle, 0)
            half_copy.start()

        @pl.when(h == 0)
        def _():
            for blk in range(4):
                pltpu.make_async_copy(do_in.at[0, pl.ds(0, 192)], do_ref.at[g, blk], landed.at[g * 4 + blk]).wait()

        same = (row64 == seg_ref[pl.ds(jnp.where(g == 2, 1, own_seq), 1), :]).astype(F32)
        ro = pl.multiple_of(h * 192, 64)
        qh, kh, vh = pl.ds(ro, 64), pl.ds(ro + 64, 64), pl.ds(ro + 128, 64)
        l1, l2, l3 = split3(-lse_ref[g * 3 + h])
        qa[0:64, :] = qkv_ref[g, h, 0:64, :]
        qa[64:128, :] = jnp.where(row64 == 8, l1, jnp.where(row64 == 9, l2, jnp.where(row64 == 10, l3, same))).astype(BF)
        key_mark = jnp.where(row64 >= 8, 1.0, (same - 1.0) * BIG).astype(BF)
        ka[...] = jnp.concatenate([qkv_ref[g, h, 64:128, :], key_mark], axis=0).T
        va[...] = jnp.concatenate([qkv_ref[g, h, 128:192, :], jnp.ones((64, length), BF)], axis=0).T
        hs = pl.ds(pl.multiple_of(h * 64, 64), 64)
        for b in range(4):
            bs = slice(b * BLK, (b + 1) * BLK)
            do = do_ref[g, b, hs, :]
            e1, e2, e3 = split3(-jnp.sum(do.astype(F32) * o_ref[g, b, hs, :].astype(F32), axis=0, keepdims=True))
            da[0:64, bs] = do
            rb = row64[:, bs]
            da[64:128, bs] = jnp.where(rb == 8, e1, jnp.where(rb == 9, e2, jnp.where(rb == 10, e3, 0.0))).astype(BF)
        dk[...] = jnp.zeros_like(dk)
        dv[...] = jnp.zeros_like(dv)

        def chunk(n, _):
            for k, steps in STEPS.items():
                @pl.when(2 * u + n == k)
                def _(steps=steps):
                    for stage, name in steps:
                        getattr(named[name], stage)()

            cs = pl.ds(pl.multiple_of(n * 512, 512), 512)
            s = jnp.dot(ka[...], qa[:, cs], preferred_element_type=F32)
            p = jnp.exp2(s)
            dp = jnp.dot(va[...], da[:, cs], preferred_element_type=F32)
            pb = p.astype(BF)
            ds = (p * dp).astype(BF)
            dv[...] += dg(da[0:64, cs], pb, 1, 1)
            dk[...] += dg(qa[0:64, cs], ds, 1, 1)
            dq = jnp.dot(qkv_ref[g, h, 64:128, :], ds, preferred_element_type=F32)
            dq_s[g, qh, cs] = (dq * (HEAD_DIM ** (-0.5))).astype(BF)
            return 0

        lax.fori_loop(0, length // 512, chunk, 0)
        dq_s[g, kh, :] = (dk[...] * math.log(2.0)).astype(BF)
        dq_s[g, vh, :] = dv[...].astype(BF)

        @pl.when(g == 1)
        def _():
            pl.when(h == 0)(load_xab.wait)
            so[1 + h] = jnp.dot(dq_s[1, pl.ds(ro, 192), :], xab_ref[0], preferred_element_type=F32).astype(BF)

        for k, pieces in ((0, thin[1:2]), (3, thin[2:3]), (6, thin[3:])):
            @pl.when(u == k)
            def _(pieces=pieces):
                for piece in pieces:
                    piece.to_y().start()

        @pl.when(g == 0)
        def _():
            rows = pl.ds(ro, 192)
            r = jnp.dot(dq_s[0, rows, :], xab_ref[0], preferred_element_type=F32)
            sv[1 + h] = (r + jnp.dot(dq_s[2, rows, :], xab_ref[1], preferred_element_type=F32)).astype(BF)

        return 0

    load_qkv.wait()
    load_o.wait()
    lax.fori_loop(0, 9, unit, 0)
    for stage, name in FIRST_TAIL:
        getattr(named[name], stage)()
    half_copy.wait_recv()
    hsum[...] = (sbuf[1, rows_of(far + c), :].astype(F32) + rhalf[...].astype(F32)).astype(BF)
    far_copy.start()
    ones = jnp.ones((8, length), BF)
    tv[12:13, 0:576] = (dg(ones, dq_s[0], 1, 1) + dg(ones, dq_s[2], 1, 1))[0:1]
    tv[13:14, 0:576] = dg(ones, dq_s[1], 1, 1)[0:1]
    to[...] = tv[...]
    tiny.to_y().start()
    lax.fori_loop(0, 4, into_own, 0)
    for middle, copy in core_copies:
        copy.start()

    for k, (stage, name) in enumerate(TAIL_STEPS):
        getattr(named[name], stage)()
        if k == TAIL_INPUT:
            for i in range(3):
                core_copies[i][1].wait_recv()
                middle, blk = block_of(t, i)
                rs = pl.ds(i * BLK, BLK)

                @pl.when(middle == 0)
                def _():
                    din_ref[rs, :] = (dz1_ref[rs, :] + rcore[i].astype(F32)).astype(BF)

                @pl.when(middle == 1)
                def _():
                    k = blk % 2
                    pltpu.make_async_copy(hsum, rmid.at[k], recv.at[4 + k]).wait()
                    din_ref[rs, :] = (dz1_ref[rs, :] + rcore[i].astype(F32) + rmid[k].astype(F32)).astype(BF)

    for p, piece in enumerate(big):
        piece.finish(p >= early)
    for piece in thin + [tiny]:
        piece.finish()
    for copy in [c for _, c in core_copies] + [half_copy, far_copy] + go_core + [small_core]:
        copy.wait_send()
    for cond, copy in pending:
        if cond is None:
            copy.wait_send()
        else:
            pl.when(cond)(copy.wait_send)

def finish(
    out_in, din_in, ff_in, fs_in, sm,
    out_o, din_o, gwq, gbq, gwk, gwv, gbv, gwo, gbo, gg1, gs1, gwin, gbin, gwback, gbback, gg2, gs2,
    out_v, din_v, ff, fs, win_v, wback_v, q_v, wo_v, local,
):
    loads = [
        pltpu.make_async_copy(ff_in, ff, local.at[0]),
        pltpu.make_async_copy(fs_in, fs, local.at[1]),
        pltpu.make_async_copy(out_in, out_v, local.at[2]),
        pltpu.make_async_copy(din_in, din_v, local.at[3]),
    ]
    start_all(loads)
    stores = []

    def store(src, dst):
        copy = pltpu.make_async_copy(src, dst, local.at[4 + len(stores)])
        copy.start()
        stores.append(copy)

    for k, ref in ((0, gbo), (1, gg1), (2, gs1), (8, gbin), (3, gbback), (4, gg2), (5, gs2)):
        ref[...] = sm[k : k + 1, :].reshape(768)
    heads = sm[12:13, 0:576]
    for k, ref in ((0, gbq), (2, gbv)):
        ref[...] = jnp.concatenate([heads[:, 192 * h + 64 * k : 192 * h + 64 * k + 64] for h in range(3)], axis=1).reshape(192)
    loads[0].wait()
    for ch in range(3):
        cs = slice(ch * BLK, (ch + 1) * BLK)
        wback_v[cs, :] = ff[2 * ch + 1].T.astype(F32)
        win_v[:, cs] = ff[2 * ch].astype(F32)
    store(wback_v, gwback)
    store(win_v, gwin)
    loads[2].wait()
    store(out_v, out_o)
    loads[3].wait()
    store(din_v, din_o)
    loads[1].wait()
    wo_v[...] = fs[0].astype(F32)
    store(wo_v, gwo)
    for k, ref in enumerate((gwq, gwk, gwv)):
        for h in range(3):
            q_v[k, 64 * h : 64 * h + 64, :] = fs[1 + h, 64 * k : 64 * k + 64, :].astype(F32)
        store(q_v.at[k], ref)
    for copy in stores:
        copy.wait()


def vm(*shape, dtype=BF):
    return pltpu.VMEM(shape, dtype)


def sds(*shape, dtype=BF):
    return jax.ShapeDtypeStruct(shape, dtype)


VM = pl.BlockSpec(memory_space=pltpu.VMEM)
ANY = pl.BlockSpec(memory_space=pl.ANY)


def params(cid):
    return pltpu.CompilerParams(collective_id=cid, has_side_effects=True, vmem_limit_bytes=62 * 2**20)


def local_step(
    line,
    layer_input, segment_ids, w_query, b_query, w_key, w_value, b_value, w_out, b_out, first_gain, first_shift,
    w_in, b_in, w_back, b_back, second_gain, second_shift, cotangent,
):
    dma = pltpu.SemaphoreType.DMA
    qkv, o, lse, xab, wts, out, dz1, do, gf, go, small = pl.pallas_call(
        partial(forward, line),
        out_shape=(
            sds(3, 3, 192, 1024), sds(3, 4, 192, BLK), sds(9, 1, 1024, dtype=F32), sds(2, 1024, 768), sds(2, 576, 768),
            sds(768, 768), sds(768, 768, dtype=F32), sds(3, 768, BLK), sds(2, 3, 2, 768, BLK), sds(4, 192, 768),
            sds(16, 768, dtype=F32),
        ),
        in_specs=[VM, ANY] + [VM] * 13 + [ANY] * 3,
        out_specs=(ANY, ANY, VM, ANY, ANY, ANY, ANY, ANY, ANY, ANY, VM),
        scratch_shapes=[
            vm(768, 768), vm(3, 768, BLK), vm(2, 3, 2, 768, BLK), vm(4, 192, 768),
            vm(3, 3, 192, 1024), vm(3, 4, 192, BLK), vm(2, 1024, 768), vm(2, 576, 768),
            vm(8, 768, dtype=F32), vm(3, 8, 768, dtype=F32), vm(576, 1, dtype=F32),
            vm(128, 1024), vm(128, 1024), vm(80, 1024),
            vm(768, 768), vm(3, 768, BLK), vm(768, 768), vm(768, 3072), vm(3072, 768),
            vm(768, 768), vm(768, 768), vm(768, 768, dtype=F32), vm(768, 1, dtype=F32), vm(768, 3072), vm(768, 3072),
            vm(768, 768, dtype=F32), vm(768, 768), vm(768, 768),
            vm(3, 2, 768, BLK), vm(3, 2, 768, BLK), vm(max(Y_EARLY, 1), 768, BLK), vm(max(X_EARLY, 1), 768, BLK),
            dma((80,)), dma((80,)), dma((24,)),
        ],
        compiler_params=params(0),
        name="forward_and_feed_forward",
    )(
        layer_input, cotangent, w_query.T, w_key.T, w_value.T, b_query, b_value, b_in,
        b_out, first_gain, first_shift, b_back, second_gain, second_shift, segment_ids, w_out, w_in, w_back,
    )

    piece, slab, tiny = vm(6, 768, BLK), vm(4, 192, 768), vm(16, 768, dtype=F32)
    din, ff, fs, sm = pl.pallas_call(
        partial(k3, line),
        out_shape=(sds(768, 768), sds(6, 768, BLK), sds(4, 192, 768), sds(16, 768, dtype=F32)),
        in_specs=[ANY, VM, ANY, VM, ANY, ANY, ANY, ANY, ANY, ANY, VM],
        out_specs=(VM, VM, VM, VM),
        scratch_shapes=[
            vm(3, 3, 192, 1024), vm(3, 4, 192, BLK), vm(2, 1024, 768), vm(2, 576, 768), vm(4, 192, 768),
            vm(768, 768, dtype=F32),
            vm(3, 4, 192, BLK), vm(3, 576, 1024), vm(128, 1024), vm(1024, 128), vm(1024, 128), vm(128, 1024),
            vm(64, 1024, dtype=F32), vm(64, 1024, dtype=F32), vm(2, 1024, 768),
            vm(3, BLK, 768), vm(2, BLK, 768), vm(BLK, 768), vm(BLK, 768),
            piece, piece, piece, piece, piece, slab, slab, slab, slab, slab, slab, vm(2, 192, 768),
            tiny, tiny, tiny, tiny, tiny, tiny, tiny,
            dma((13, 6)), dma((13, 6)), dma((17,)), dma((9,)), dma((12,)), dma((12,)),
        ],
        compiler_params=params(1),
        name="attention_backward",
    )(qkv, segment_ids, o, lse, xab, wts, do, dz1, gf, go, small)
    if not line:
        ff, fs = lax.psum((ff, fs), "dp")
        sm = lax.psum(sm, "dp")
    row = sds(768, dtype=F32)
    cols, thin = sds(192, 768, dtype=F32), sds(192, dtype=F32)
    square = sds(768, 768, dtype=F32)
    outs = pl.pallas_call(
        finish,
        out_shape=(
            sds(768, 768), sds(768, 768), cols, thin, cols, cols, thin, sds(192, 768, dtype=F32),
            row, row, row, square, row, square, row, row, row,
        ),
        in_specs=[ANY, ANY, ANY, ANY, VM],
        out_specs=(ANY, ANY, ANY, VM, ANY, ANY, VM, ANY, VM, VM, VM, ANY, VM, ANY, VM, VM, VM),
        scratch_shapes=[
            vm(768, 768), vm(768, 768), vm(6, 768, BLK), vm(4, 192, 768), vm(768, 768, dtype=F32), vm(768, 768, dtype=F32),
            vm(3, 192, 768, dtype=F32), vm(192, 768, dtype=F32), dma((16,)),
        ],
        compiler_params=pltpu.CompilerParams(vmem_limit_bytes=62 * 2**20),
        name="results",
    )(out, din, ff, fs, sm)
    return (*outs[:2], outs[2].T, outs[3], outs[4].T, outs[5].T, *outs[6:])


def solution(mesh):
    rows = P(("dp", "tensor"), None)
    in_specs = (
        rows, P("dp", None), P(None, "tensor"), P("tensor"), P(None, "tensor"), P(None, "tensor"), P("tensor"),
        P("tensor", None), P(), P(), P(), P(None, "tensor"), P("tensor"), P("tensor", None), P(), P(), P(), rows,
    )
    out_specs = (
        rows, rows, P(None, "tensor"), P("tensor"), P(None, "tensor"), P(None, "tensor"), P("tensor"),
        P("tensor", None), P(), P(), P(), P(None, "tensor"), P("tensor"), P("tensor", None), P(), P(), P(),
    )
    line = mesh.shape["dp"] == 8
    return jax.shard_map(partial(local_step, line), mesh=mesh, in_specs=in_specs, out_specs=out_specs, check_vma=False)
```

```python
import math
from functools import partial

import jax
import jax.numpy as jnp
from jax import lax
from jax.experimental import pallas as pl
from jax.experimental.pallas import tpu as pltpu
from jax.sharding import PartitionSpec as P

F32 = jnp.float32
BF = jnp.bfloat16
MESH = pl.DeviceIdType.MESH
HEAD_DIM = 64
EPSILON = 1e-05
BIG = 1e30
LOG2E = 1.0 / math.log(2.0)
QSCALE = HEAD_DIM ** (-0.5) * LOG2E
BLK = 256
Y_EARLY = 3
X_EARLY = 1
SPLIT = (2, 3, 4, 5)
AY, AX, AE, AM, AF = "after_y", "after_x", "after_end", "after_mate", "after_final"
STEPS = {
    3: ((AE, 0), (AX, 1),),
    4: ((AY, 6),),
    5: ((AX, 2),),
    7: ((AM, 0), (AE, 1), (AX, 6), (AY, 3),),
    9: ((AE, 2), (AY, 7),),
    10: ((AX, 3),),
    11: ((AM, 1), (AE, 6),),
    12: ((AX, 7), (AY, 4),),
    13: ((AM, 2), (AE, 3),),
    14: ((AY, 8),),
    15: ((AM, 6), (AE, 7), (AX, 4),),
    16: ((AM, 3),),
    17: ((AX, 8), (AY, 5),),
}
FIRST_TAIL = (
    (AE, 4),
    (AM, 7),
    (AY, 9),
)
TAIL_INPUT = 20
TAIL_STEPS = (
    (AY, 10),
    (AY, 11),
    (AY, 12),
    (AY, 13),
    (AY, 14),
    (AF, 2),
    (AX, 5),
    (AY, -1),
    (AX, 9),
    (AF, 3),
    (AE, 8),
    (AX, 10),
    (AM, 4),
    (AX, 11),
    (AX, 12),
    (AX, 13),
    (AE, 5),
    (AX, 14),
    (AE, 9),
    (AE, 10),
    (AE, 11),
    (AM, 8),
    (AE, 12),
    (AE, 13),
    (AX, -1),
    (AF, 4),
    (AE, 14),
    (AM, 5),
    (AE, -1),
    (AM, 9),
    (AM, 10),
    (AM, 11),
    (AM, 12),
    (AM, 13),
    (AM, 14),
    (AM, -1),
    (AF, 5),
)


def dg(a, b, ca, cb):
    return lax.dot_general(a, b, (((ca,), (cb,)), ((), ())), preferred_element_type=F32)


def where_am_i():
    t = lax.axis_index("tensor")
    d = lax.axis_index("dp")
    core = t + 1 - 2 * (t % 2)
    across = (t + 2) % 4
    diag = 3 - t
    side = d + 1 - 2 * (d % 2)
    return t, d, core, across, diag, side


def block_of(t, i):
    b = 3 * t + i
    middle = (b // 4) % 2
    return middle, b % 4


def greet(devices):
    barrier = pltpu.get_barrier_semaphore()
    for dev in devices:
        pl.semaphore_signal(barrier, inc=1, device_id=dev, device_id_type=MESH)
    pl.semaphore_wait(barrier, len(devices))


def half_rows(half, total, pieces, i):
    n = total // 2 // pieces
    return pl.ds(pl.multiple_of(half * (total // 2) + i * n, n), n)


class Copies:
    def __init__(self, send, recv):
        self.send, self.recv, self.used = send, recv, 0

    def new(self, src, dst, **device):
        k = self.used
        self.used += 1
        return pltpu.make_async_remote_copy(
            src_ref=src,
            dst_ref=dst,
            send_sem=self.send.at[k],
            recv_sem=self.recv.at[k],
            device_id=device,
            device_id_type=MESH,
        )


def start_all(copies):
    for copy in copies:
        copy.start()


def layer_stats(z):
    mean = jnp.mean(z, axis=-1, keepdims=True)
    cen = z - mean
    var = jnp.mean(cen * cen, axis=-1, keepdims=True)
    inv = lax.rsqrt(var + EPSILON)
    return cen * inv, inv


def forward(
    line,
    x_ref, cot_in, wq_ref, wk_ref, wv_ref, bq_ref, bv_ref, bin_ref, v0, v1, v2, v3, v4, v5, seg_ref,
    wout_ref, win_ref, wback_ref,
    qkv_out, o_out, lse_ref, xab_out, wts_out, out_out, dz1_out, do_out, gf_out, go_out, small_ref,
    out_ref, do_ref, gf_ref, go_ref, qkv, o_v, xab, w_v, bias_ref, biasg_ref, bcol, qa, ka, va,
    cot_ref, ot, wo, wi, wb, h1b, h1t, xh1, inv1, gg, gp, z2, dz2b, dz2t, gsend, rc, ry, rx, send, recv, local,
):
    length = 1024
    t, d, core, across, diag, side = where_am_i()
    y, c = t // 2, t % 2
    half = d % 2
    zbit = (d // 2) % 2
    pair = d + 2 - 4 * zbit
    x_early = X_EARLY if line else 0

    rows_out, rows_local = [], []
    cp = Copies(send, recv)
    cp.used = 12
    for i in range(3):
        middle, blk = block_of(t, i)
        src = x_ref.at[pl.ds(i * BLK, BLK)]
        dst = xab.at[middle, pl.ds(pl.multiple_of(blk * BLK, BLK), BLK)]
        rows_local.append(pltpu.make_async_copy(src, dst, local.at[i]))
        rows_out.append(cp.new(src, dst, tensor=core))
    own = [
        pltpu.make_async_copy(wout_ref, wo.at[pl.ds(0, 192)], local.at[12]),
        pltpu.make_async_copy(win_ref, wi.at[:, pl.ds(0, 768)], local.at[13]),
        pltpu.make_async_copy(wback_ref, wb.at[pl.ds(0, 768)], local.at[14]),
        pltpu.make_async_copy(cot_in, cot_ref, local.at[15]),
    ]
    start_all(rows_local + own)

    for k, ref in enumerate((wq_ref, wk_ref, wv_ref)):
        for h in range(3):
            n = 192 * h + 64 * k
            w_v[0, n : n + 64, :] = ref[64 * h : 64 * h + 64, :]
    bias_ref[...] = jnp.zeros((8, 768), F32)
    bias_ref[0:1, :] = bin_ref[...].astype(F32).reshape(1, 768)
    bq, bv = bq_ref[...].astype(F32).reshape(1, 192), bv_ref[...].astype(F32).reshape(1, 192)
    parts = []
    for h in range(3):
        parts += [bq[:, 64 * h : 64 * h + 64], jnp.zeros((1, 64), F32), bv[:, 64 * h : 64 * h + 64]]
    bias_ref[1:2, 0:576] = jnp.concatenate(parts, axis=1)

    greet([{"tensor": core}, {"tensor": across}, {"tensor": diag}, {"dp": side}, {"dp": pair}])

    mixed = (t == 1) | (t == 2)
    k_out = jnp.where(mixed, 0, 1)
    block_out = pl.ds(pl.multiple_of((2 * y + k_out) * BLK, BLK), BLK)
    block_in = pl.ds(pl.multiple_of((2 * (1 - y) + c) * BLK, BLK), BLK)
    n = cp.used
    cross_out = cp.new(xab.at[1, block_out], xab.at[1, block_out], tensor=2 * (1 - y) + k_out)
    cross_arrived = pltpu.make_async_remote_copy(
        src_ref=xab.at[1, block_out], dst_ref=xab.at[1, block_in], send_sem=send.at[n], recv_sem=recv.at[n],
        device_id={"tensor": core}, device_id_type=MESH,
    )
    cross_forward = cp.new(xab.at[1, block_in], xab.at[1, block_in], tensor=core)
    wp_first, wp_second = [], []
    for i in range(3):
        part = half_rows(half, 576, 3, i)
        wp_first.append(cp.new(w_v.at[0, part], w_v.at[1, part], tensor=across))
        wp_second.append(cp.new(w_v.at[1, part], w_v.at[1, part], dp=side))
    bias_out = [
        cp.new(bias_ref, biasg_ref.at[0], tensor=core),
        cp.new(bias_ref, biasg_ref.at[1], tensor=across),
        cp.new(bias_ref, biasg_ref.at[2], tensor=diag),
    ]
    part = half_rows(half, 192, 1, 0)
    place = pl.ds(part.start + 384, part.size)
    wo_first = cp.new(wout_ref.at[part], wo.at[place], tensor=across)
    wo_second = cp.new(wo.at[place], wo.at[place], dp=side)
    wo_core = cp.new(wout_ref, wo.at[pl.ds(192, 192)], tensor=core)
    wo_diag = cp.new(wo.at[pl.ds(384, 192)], wo.at[pl.ds(576, 192)], tensor=core)

    def lanes(j):
        return pl.ds(768 * j, 768)

    in_core = cp.new(win_ref, wi.at[:, lanes(1)], tensor=core)
    back_core = cp.new(wback_ref, wb.at[lanes(1)], tensor=core)
    in_first, in_second, in_third, in_diag, back_first, back_second, back_diag = [], [], [], [], [], [], []
    for i in range(3):
        part = half_rows(half, 768, 3, i)
        first_part = part
        if i < 2:
            z_part = half_rows(zbit, 768, 3, i)
            first_part = pl.ds(pl.multiple_of(z_part.start + 64 * half, 64), 64)
            in_third.append(cp.new(wi.at[z_part, lanes(2)], wi.at[z_part, lanes(2)], dp=pair))
        in_first.append(cp.new(win_ref.at[first_part], wi.at[first_part, lanes(2)], tensor=across))
        in_second.append(cp.new(wi.at[first_part, lanes(2)], wi.at[first_part, lanes(2)], dp=side))
        place = pl.ds(part.start + 2 * 768, part.size)
        back_first.append(cp.new(wback_ref.at[part], wb.at[place], tensor=across))
        back_second.append(cp.new(wb.at[place], wb.at[place], dp=side))
        for h in range(2):
            both = half_rows(h, 768, 3, i)
            in_diag.append(cp.new(wi.at[both, lanes(2)], wi.at[both, lanes(3)], tensor=core))
            m = h * 384 + i * 128
            back_diag.append(cp.new(wb.at[pl.ds(2 * 768 + m, 128)], wb.at[pl.ds(3 * 768 + m, 128)], tensor=core))

    peers = (t, core, across, diag)

    def heads_to_rows(group):
        found = []
        for j, dev in enumerate(peers):
            if group != 2 and j >= 2:
                continue
            for i in range(3):
                middle, blk = block_of(dev, i)
                slot = j + 2 if group == 1 else j
                src, dst = o_v.at[group, blk], ot.at[i, pl.ds(slot * 192, 192)]
                sem = recv.at[i * 4 + slot]
                if j == 0:
                    copy = pltpu.make_async_copy(src, dst, sem)
                else:
                    copy = pltpu.make_async_remote_copy(
                        src_ref=src, dst_ref=dst, send_sem=send.at[9 + i if group == 1 else 3 * (j - 1) + i],
                        recv_sem=sem, device_id={"tensor": dev}, device_id_type=MESH,
                    )
                found.append((j, (middle == 1) if group == 2 else (middle == 0), copy))
        return found

    def start_heads(group):
        for _, cond, copy in heads_to_rows(group):
            pl.when(cond)(copy.start)

    start_all(rows_out + bias_out + wp_first[:1])
    start_all([wo_core, in_core, back_core])
    va[64:80, :] = jnp.ones((16, length), BF)
    row64 = lax.broadcasted_iota(jnp.int32, (64, length), 0)
    factor = jnp.where(lax.broadcasted_iota(jnp.int32, (576, 1), 0) % 192 < 64, QSCALE, 1.0)

    def outgoing(g):
        return [
            pltpu.make_async_copy(qkv.at[g], qkv_out.at[g], local.at[4 + 2 * (g % 3)]),
            pltpu.make_async_copy(o_v.at[g], o_out.at[g], local.at[5 + 2 * (g % 3)]),
        ]

    def at(n, k, copies_recv, copies_start=()):
        @pl.when(n == k)
        def _():
            for copy in copies_recv:
                copy.wait_recv()
            start_all(copies_start)

    def unit(u, _):
        g = (2 * (u // 3)) % 3
        h = u % 3
        par = jnp.where(g == 1, 1, 0)
        middle = jnp.where(g == 2, 1, 0)

        at(u, 1, wp_first[:1], wp_second[:1])

        @pl.when(u == 3)
        def _():
            cross_arrived.wait_recv()
            cross_forward.start()
            start_heads(0)
            cross_forward.wait_recv()

        at(u, 4, wp_first[1:2], wp_second[1:2])
        at(u, 5, wp_first[2:3], wp_second[2:3])

        @pl.when(u == 6)
        def _():
            start_heads(2)
            start_all(in_first[2:] + back_first)

        at(u, 6, [wo_first], [wo_second])
        at(u, 6, wp_second + [bias_out[1]])
        at(u, 7, in_first[:2], in_second[:2])
        at(u, 8, in_second[:1], in_third[:1])
        at(u, 8, [wo_second], [wo_diag])

        @pl.when(h == 0)
        def _():
            @pl.when(u > 0)
            def _():
                start_all(outgoing(jnp.where(g == 2, 0, 2)))

            @pl.when(par == 0)
            def _():
                bcol[...] = jnp.transpose(bias_ref[...])[0:576, 1:2]

            @pl.when(par == 1)
            def _():
                bcol[...] = jnp.transpose(biasg_ref[1])[0:576, 1:2]

            col = bcol[...]

            def body(n, _):
                cs = pl.ds(pl.multiple_of(n * BLK, BLK), BLK)
                r = (dg(w_v[par], xab[middle, cs, :], 1, 1) + col) * factor
                for k in range(3):
                    qkv[g, k, :, cs] = r[192 * k : 192 * (k + 1)].astype(BF)
                return 0

            lax.fori_loop(0, length // BLK, body, 0)
            same = (row64 == seg_ref[pl.ds(jnp.where(g == 2, 1, 2 * y), 1), :]).astype(F32)
            qa[64:128, :] = same.astype(BF)
            ka[64:128, :] = ((same - 1.0) * BIG).astype(BF)

        qa[0:64, :] = qkv[g, h, 0:64, :]
        ka[0:64, :] = qkv[g, h, 64:128, :]
        va[0:64, :] = qkv[g, h, 128:192, :]
        s = jnp.dot(ka[...].T, qa[...], preferred_element_type=F32)
        m = jnp.max(s, axis=0, keepdims=True)
        p = jnp.exp2(s - m).astype(BF)
        o = jnp.dot(va[...], p, preferred_element_type=F32)
        total = o[64:65, :]
        res = (o[0:64] * (1.0 / total)).astype(BF)
        hs = pl.ds(pl.multiple_of(h * 64, 64), 64)
        for b in range(4):
            o_v[g, b, hs, :] = res[:, b * BLK : (b + 1) * BLK]
        lse_ref[g * 3 + h] = m + jnp.log2(total)
        return 0

    for copy in rows_local:
        copy.wait()
    for copy in rows_out:
        copy.wait_recv()
    start_all([cross_out] + wp_first[1:] + [wo_first] + in_first[:2])
    lax.fori_loop(0, 9, unit, 0)
    start_heads(1)
    tail = outgoing(1)
    tail.append(pltpu.make_async_copy(xab, xab_out, local.at[10]))
    tail.append(pltpu.make_async_copy(w_v, wts_out, local.at[11]))
    start_all(tail)

    b_out, gain1, shift1, b_back, gain2, shift2 = [v[...].reshape(1, 768) for v in (v0, v1, v2, v3, v4, v5)]
    own[0].wait()
    for copy in [wo_core, wo_diag, bias_out[0], bias_out[2]]:
        copy.wait_recv()
    in_second[1].wait_recv()
    in_third[1].start()
    for i in range(3):
        for slot in range(4):
            pltpu.make_async_copy(o_v.at[0, 0], ot.at[i, pl.ds(slot * 192, 192)], recv.at[i * 4 + slot]).wait()

    def first(i, _):
        rs = pl.ds(pl.multiple_of(i * BLK, BLK), BLK)
        z = x_ref[rs, :].astype(F32) + dg(ot[i], wo[...], 0, 0) + b_out
        xh, inv = layer_stats(z)
        xh1[rs, :] = xh
        inv1[rs, :] = inv
        h1b[rs, :] = (xh * gain1 + shift1).astype(BF)
        return 0

    lax.fori_loop(0, 3, first, 0)
    h1t[...] = h1b[...].T
    own[1].wait()

    def up(n, _):
        at(n, 0, in_first[2:], in_second[2:])
        at(n, 3, [in_core])
        at(n, 5, back_first[:1], back_second[:1])
        at(n, 6, in_third + in_second[2:], in_diag)
        at(n, 7, back_first[1:2], back_second[1:2])
        at(n, 9, in_diag)
        at(n, 9, back_second[:1], back_diag[:2])
        at(n, 10, back_first[2:], back_second[2:])
        at(n, 11, back_second[1:2], back_diag[2:4])
        cs = pl.ds(pl.multiple_of(n * BLK, BLK), BLK)
        j = n // 3
        low = pl.ds(pl.multiple_of((n % 3) * BLK, BLK), BLK)
        bias = jnp.where(j == 0, bias_ref[0:1, low], biasg_ref[jnp.maximum(j - 1, 0), 0:1, low])
        u = jnp.dot(h1b[...], wi[:, cs], preferred_element_type=F32) + bias
        cdf = 0.5 * (1.0 + lax.erf(u * (2.0 ** -0.5)))
        pdf = jnp.exp(-0.5 * u * u) * (1.0 / math.sqrt(2.0 * math.pi))
        gg[:, cs] = (u * cdf).astype(BF)
        gp[:, cs] = (cdf + u * pdf).astype(BF)
        return 0

    lax.fori_loop(0, 12, up, 0)
    own[2].wait()
    back_core.wait_recv()

    def down_near(n, _):
        cs = pl.ds(pl.multiple_of(n * BLK, BLK), BLK)
        z2[:, cs] = jnp.dot(gg[:, 0:1536], wb[0:1536, cs], preferred_element_type=F32)
        return 0

    def down_far(n, _):
        cs = pl.ds(pl.multiple_of(n * BLK, BLK), BLK)
        z2[:, cs] += jnp.dot(gg[:, 1536:3072], wb[1536:3072, cs], preferred_element_type=F32)
        return 0

    lax.fori_loop(0, 3, down_near, 0)
    back_second[2].wait_recv()
    start_all(back_diag[4:])
    own[3].wait()
    for copy in back_diag:
        copy.wait_recv()
    lax.fori_loop(0, 3, down_far, 0)

    def second_norm(i, sums):
        rs = pl.ds(pl.multiple_of(i * BLK, BLK), BLK)
        h1 = xh1[rs, :] * gain1 + shift1
        xh, inv = layer_stats(h1 + z2[rs, :] + b_back)
        out_ref[rs, :] = (xh * gain2 + shift2).astype(BF)
        cot = cot_ref[rs, :].astype(F32)
        dxh = cot * gain2
        dz = inv * (dxh - jnp.mean(dxh, axis=-1, keepdims=True) - xh * jnp.mean(dxh * xh, axis=-1, keepdims=True))
        z2[rs, :] = dz
        dz2b[rs, :] = dz.astype(BF)
        return (
            sums[0] + jnp.sum(dz, axis=0, keepdims=True),
            sums[1] + jnp.sum(cot * xh, axis=0, keepdims=True),
            sums[2] + jnp.sum(cot, axis=0, keepdims=True),
        )

    zero = jnp.zeros((1, 768), F32)
    s3, s4, s5 = lax.fori_loop(0, 3, second_norm, (zero, zero, zero))
    small_ref[3:4, :] = s3
    small_ref[4:5, :] = s4
    small_ref[5:6, :] = s5
    out_copy = pltpu.make_async_copy(out_ref, out_out, local.at[16])
    out_copy.start()
    dz2t[...] = dz2b[...].T

    base = cp.used

    def to_core(stage, ch):
        k = base + stage * 3 + ch
        return pltpu.make_async_remote_copy(
            src_ref=gsend.at[ch], dst_ref=rc.at[ch], send_sem=send.at[k], recv_sem=recv.at[k],
            device_id={"tensor": core}, device_id_type=MESH,
        )

    def to_across(p):
        k = base + 6 + p
        return pltpu.make_async_remote_copy(
            src_ref=gf_ref.at[1, p // 2, p % 2], dst_ref=ry.at[p], send_sem=send.at[k], recv_sem=recv.at[k],
            device_id={"tensor": across}, device_id_type=MESH,
        )

    def to_side(p):
        k = base + 12 + p
        return pltpu.make_async_remote_copy(
            src_ref=gf_ref.at[0, p // 2, p % 2], dst_ref=rx.at[p], send_sem=send.at[k], recv_sem=recv.at[k],
            device_id={"dp": side}, device_id_type=MESH,
        )

    def back(m, _):
        stage = m // 6
        ch = (m % 6) // 2
        slot = 3 - 2 * stage - m % 2
        n = slot * 3 + ch
        cs = pl.ds(pl.multiple_of(n * BLK, BLK), BLK)
        low = pl.ds(pl.multiple_of(ch * BLK, BLK), BLK)
        g_back = jnp.dot(dz2t[...], gg[:, cs], preferred_element_type=F32)
        du = (dg(dz2b[...], wb[cs, :], 1, 1) * gp[:, cs].astype(F32)).astype(BF)
        gg[:, cs] = du
        small_ref[pl.ds(8 + slot, 1), low] = jnp.sum(du.astype(F32), axis=0, keepdims=True)
        g_in = jnp.dot(h1t[...], du, preferred_element_type=F32)

        @pl.when(m % 2 == 0)
        def _():
            pl.when(stage == 1)(to_core(0, ch).wait_send)
            gsend[ch, 0] = g_in.astype(BF)
            gsend[ch, 1] = g_back.astype(BF)
            to_core(stage, ch).start()

        @pl.when(m % 2 == 1)
        def _():
            to_core(stage, ch).wait_recv()
            gf_ref[1 - stage, ch, 0] = (g_in + rc[ch, 0].astype(F32)).astype(BF)
            gf_ref[1 - stage, ch, 1] = (g_back + rc[ch, 1].astype(F32)).astype(BF)
            for p in range(Y_EARLY):
                pl.when((stage == 0) & (ch == p // 2))(to_across(p).start)

        return 0

    lax.fori_loop(0, 12, back, 0)

    def gf_copy(p):
        k = (0, p // 2, p % 2)
        return pltpu.make_async_copy(gf_ref.at[k], gf_out.at[k], local.at[18 + p])

    gf_other = pltpu.make_async_copy(gf_ref.at[1], gf_out.at[1], local.at[17])
    start_all([gf_other] + [gf_copy(p) for p in range(Y_EARLY, 6)])

    def take(p, arrived):
        k = (0, p // 2, p % 2)
        gf_ref[k] = (gf_ref[k].astype(F32) + arrived[p].astype(F32)).astype(BF)

    for p in range(x_early):
        to_across(p).wait_recv()
        take(p, ry)
        to_side(p).start()

    def into_h(n, _):
        cs = pl.ds(pl.multiple_of(n * BLK, BLK), BLK)
        z2[:, cs] += dg(gg[...], wi[cs, :], 1, 1)
        return 0

    lax.fori_loop(0, 3, into_h, 0)

    def first_norm(i, sums):
        rs = pl.ds(pl.multiple_of(i * BLK, BLK), BLK)
        dh = z2[rs, :]
        xh = xh1[rs, :]
        dxh = dh * gain1
        dz = inv1[rs, :] * (dxh - jnp.mean(dxh, axis=-1, keepdims=True) - xh * jnp.mean(dxh * xh, axis=-1, keepdims=True))
        z2[rs, :] = dz
        dzb = dz.astype(BF)
        dz2b[rs, :] = dzb
        do_ref[i] = dg(wo[...], dzb, 1, 1).astype(BF)
        return (
            sums[0] + jnp.sum(dz, axis=0, keepdims=True),
            sums[1] + jnp.sum(dh * xh, axis=0, keepdims=True),
            sums[2] + jnp.sum(dh, axis=0, keepdims=True),
        )

    s0, s1, s2 = lax.fori_loop(0, 3, first_norm, (zero, zero, zero))
    dz1_copy = pltpu.make_async_copy(z2, dz1_out, local.at[0])
    do_copy = pltpu.make_async_copy(do_ref, do_out, local.at[1])
    start_all([dz1_copy, do_copy])
    small_ref[0:1, :] = s0
    small_ref[1:2, :] = s1
    small_ref[2:3, :] = s2
    for j in range(4):
        rows = pl.ds(192 * j, 192)
        acc = jnp.dot(ot[0, rows, :], dz2b[0:BLK, :], preferred_element_type=F32)
        acc += jnp.dot(ot[1, rows, :], dz2b[BLK : 2 * BLK, :], preferred_element_type=F32)
        acc += jnp.dot(ot[2, rows, :], dz2b[2 * BLK : 3 * BLK, :], preferred_element_type=F32)
        go_ref[j] = acc.astype(BF)
    go_copy = pltpu.make_async_copy(go_ref, go_out, local.at[2])
    go_copy.start()
    small_ref[6:8, :] = jnp.zeros((2, 768), F32)
    small_ref[12:16, :] = jnp.zeros((4, 768), F32)

    for group in range(3):
        for j, cond, copy in heads_to_rows(group):
            if j:
                pl.when(cond)(copy.wait_send)
    sent = rows_out + [cross_out, cross_forward] + wp_first + wp_second + bias_out
    sent += [wo_first, wo_second, wo_core, wo_diag, in_core, back_core]
    sent += in_first + in_second + in_third + in_diag + back_first + back_second + back_diag
    for copy in sent + [to_core(1, ch) for ch in range(3)]:
        copy.wait_send()
    for copy in outgoing(0) + outgoing(2) + tail + [dz1_copy, do_copy, out_copy, gf_other] + [gf_copy(p) for p in range(Y_EARLY, 6)]:
        copy.wait()
    for p in range(Y_EARLY):
        if p >= x_early:
            to_across(p).wait_recv()
            take(p, ry)
            gf_copy(p).start()
        to_across(p).wait_send()
    for p in range(x_early):
        to_side(p).wait()
        take(p, rx)
        gf_copy(p).start()
    for p in range(Y_EARLY):
        gf_copy(p).wait()
    go_copy.wait()


def split3(v):
    a = v.astype(BF).astype(F32)
    b = (v - a).astype(BF).astype(F32)
    return a, b, v - a - b


class Piece:
    def __init__(self, value, other, from_y, from_x, from_end, from_mate, final, send, recv, where, fold=None, split=False):
        self.value, self.other, self.final = value, other, final
        self.from_y, self.from_x, self.from_end, self.from_mate = from_y, from_x, from_end, from_mate
        self.send, self.recv, self.where, self.fold = send, recv, where, fold
        self.split = split

    def part(self, ref, which):
        if not self.split:
            return ref
        n = 768 // 2
        return ref.at[pl.ds(pl.multiple_of(which * n, n), n)]

    def mine(self, ref):
        return self.part(ref, self.where["half"])

    def copy(self, stage, src, dst, **device):
        return pltpu.make_async_remote_copy(
            src_ref=src, dst_ref=dst, send_sem=self.send.at[stage], recv_sem=self.recv.at[stage],
            device_id=device, device_id_type=MESH,
        )

    def to_y(self):
        return self.copy(0, self.other, self.from_y, tensor=self.where["across"])

    def to_x(self):
        away = 1 - self.where["half"]
        return self.copy(1, self.part(self.value, away), self.part(self.from_x, away), dp=self.where["side"])

    def to_inner(self):
        return self.copy(2, self.mine(self.value), self.mine(self.from_end), dp=self.where["pair"])

    def to_mate(self):
        return self.copy(3, self.mine(self.value), self.mine(self.from_mate), dp=self.where["mate"])

    def to_end(self):
        return self.copy(4, self.mine(self.final), self.mine(self.final), dp=self.where["pair"])

    def to_side(self):
        return self.copy(5, self.mine(self.final), self.mine(self.final), dp=self.where["side"])

    def add(self, arrived, into):
        into[...] = (self.value[...].astype(F32) + arrived[...].astype(F32)).astype(into.dtype)

    def add_mine(self, arrived, into):
        total = self.mine(self.value)[...].astype(F32) + self.mine(arrived)[...].astype(F32)
        self.mine(into)[...] = total.astype(into.dtype)

    def after_y(self):
        self.to_y().wait_recv()
        if self.fold is None:
            self.add(self.from_y, self.value)
        else:
            self.fold(self)
        self.begin_x()

    def begin_x(self):
        if self.where["line"]:
            self.to_x().start()
        else:
            self.final[...] = self.value[...]

    def after_x(self):
        if not self.where["line"]:
            return
        self.to_x().wait()
        self.add_mine(self.from_x, self.value)
        self.begin_z()

    def begin_z(self):
        pl.when(self.where["end"])(lambda: self.to_inner().start())

    def after_end(self):
        if not self.where["line"]:
            return

        @pl.when(self.where["inner"])
        def _():
            self.to_inner().wait_recv()
            self.add_mine(self.from_end, self.value)
            self.to_mate().start()

    def after_mate(self):
        if not self.where["line"]:
            return

        @pl.when(self.where["inner"])
        def _():
            self.to_mate().wait_recv()
            self.add_mine(self.from_mate, self.final)
            self.to_end().start()
            if self.split:
                self.to_side().start()

    def after_final(self):
        if not self.where["line"]:
            return

        @pl.when(self.where["end"])
        def _():
            self.to_end().wait_recv()
            self.to_side().start()

    def finish(self, had_y=True):
        if had_y:
            self.to_y().wait_send()
        if not self.where["line"]:
            return

        @pl.when(self.where["end"])
        def _():
            if not self.split:
                self.to_end().wait_recv()
            self.to_inner().wait_send()

        @pl.when(self.where["inner"])
        def _():
            self.to_mate().wait_send()
            self.to_end().wait_send()

        if self.split:
            self.to_side().wait()


def k3(
    line,
    qkv_in, seg_ref, o_in, lse_ref, xab_in, wts_in, do_in, dz1_in, gf_ref, go_in, small_ref,
    din_ref, ff_ref, fs_ref, sm_ref,
    qkv_ref, o_ref, xab_ref, wts_ref, go_ref, dz1_ref, do_ref, dq_s, qa, ka, va, da, dk, dv, sbuf, rcore, rmid, rhalf, hsum,
    fv, fy, fx, fe, fm, sv, so, sy, sx, se, sm, rgo, tv, to, tc, ty, tx, te, tm,
    psend, precv, send, recv, landed, local,
):
    length = 1024
    t, d, core, across, diag, side = where_am_i()
    y, c = t // 2, t % 2
    where = {"across": across, "side": side, "line": line, "half": d % 2}
    known = [{"tensor": core}, {"tensor": across}, {"tensor": diag}]
    if line:
        z = d // 2
        where["pair"] = d + 2 - 4 * (z % 2)
        where["mate"] = d + 2 - 4 * ((z + 1) % 2)
        where["end"] = (z == 0) | (z == 3)
        where["inner"] = (z == 1) | (z == 2)
        known += [{"dp": side}, {"dp": where["pair"]}]
    load_go, load_qkv, load_o, load_xab, load_wts, load_dz1 = [
        pltpu.make_async_copy(src, dst, local.at[6 + k])
        for k, (src, dst) in enumerate((
            (go_in, go_ref), (qkv_in, qkv_ref), (o_in, o_ref), (xab_in, xab_ref), (wts_in, wts_ref), (dz1_in, dz1_ref),
        ))
    ]
    loads = [pltpu.make_async_copy(gf_ref.at[0, p // 2, p % 2], fv.at[p], local.at[p]) for p in range(6)]
    start_all([load_go] + loads[:Y_EARLY] + [load_qkv, load_o] + loads[Y_EARLY:] + [load_xab, load_wts, load_dz1])
    barrier = pltpu.get_barrier_semaphore()
    for dev in known:
        pl.semaphore_signal(barrier, inc=1, device_id=dev, device_id_type=MESH)
    if line:
        @pl.when(where["inner"])
        def _():
            pl.semaphore_signal(barrier, inc=1, device_id={"dp": where["mate"]}, device_id_type=MESH)
            pl.semaphore_wait(barrier, len(known) + 1)

        @pl.when(where["end"])
        def _():
            pl.semaphore_wait(barrier, len(known))
    else:
        pl.semaphore_wait(barrier, len(known))

    pending = []
    peers = (t, core, across, diag)
    for i in range(3):
        middle, blk = block_of(t, i)
        for j, dev in enumerate(peers):
            src = do_in.at[i, pl.ds(192 * j, 192)]
            group = jnp.where(middle == 1, 2, j // 2)
            dst = do_ref.at[group, blk]
            sem = landed.at[group * 4 + blk]
            if j == 0:
                pltpu.make_async_copy(src, dst, sem).start()
                continue
            if j == 2:
                pl.when(middle == 0)(pltpu.make_async_copy(src, dst, sem).start)
                dev_to, cond = across, middle == 1
            elif j == 1:
                dev_to, cond = core, None
            else:
                dev_to, cond = jnp.where(middle == 1, diag, core), None
            copy = pltpu.make_async_remote_copy(
                src_ref=src, dst_ref=dst, send_sem=send.at[i * 3 + j - 1], recv_sem=sem,
                device_id={"tensor": dev_to}, device_id_type=MESH,
            )
            if cond is None:
                copy.start()
            else:
                pl.when(cond)(copy.start)
            pending.append((cond, copy))

    go_core = [
        pltpu.make_async_remote_copy(
            src_ref=go_in.at[2 * k + 1], dst_ref=rgo.at[k], send_sem=send.at[9 + k], recv_sem=recv.at[6 + k],
            device_id={"tensor": core}, device_id_type=MESH,
        )
        for k in range(2)
    ]
    small_core = pltpu.make_async_remote_copy(
        src_ref=small_ref, dst_ref=tc, send_sem=send.at[11], recv_sem=recv.at[8],
        device_id={"tensor": core}, device_id_type=MESH,
    )
    start_all(go_core + [small_core])
    big = [
        Piece(fv.at[p], gf_ref.at[1, p // 2, p % 2], fy.at[p], fx.at[p], fe.at[p], fm.at[p], ff_ref.at[p],
              psend.at[p], precv.at[p], where, split=line and p in SPLIT)
        for p in range(6)
    ]
    places = [(p, slice(0, 192)) for p in range(3)] + [(3, slice(32 * k, 32 * k + 32)) for k in range(6)]
    thin = [
        Piece(*[ref.at[p, rows] for ref in (sv, so, sy, sx, se, sm, fs_ref)], psend.at[6 + i], precv.at[6 + i], where)
        for i, (p, rows) in enumerate(places)
    ]

    def fold_small(piece):
        got = ty[...]
        add = jnp.concatenate([got[0:8], got[10:11], jnp.zeros((3, 768), F32), got[13:14], jnp.zeros((3, 768), F32)])
        tv[...] = tv[...] + add

    tiny = Piece(tv, to, ty, tx, te, tm, sm_ref, psend.at[15], precv.at[15], where, fold_small)
    early = Y_EARLY
    summed = X_EARLY if line else 0
    load_go.wait()
    for copy in go_core:
        copy.wait_recv()
    sv[0] = (go_ref[0].astype(F32) + rgo[0].astype(F32)).astype(BF)
    so[0] = (go_ref[2].astype(F32) + rgo[1].astype(F32)).astype(BF)
    thin[0].to_y().start()
    big[3].to_y().start()
    for copy in loads:
        copy.wait()
    for p in range(early):
        if p < summed:
            big[p].begin_z()
        else:
            big[p].begin_x()

    every = big + thin + [tiny]
    row64 = lax.broadcasted_iota(jnp.int32, (64, length), 0)

    def rows_of(blk):
        return pl.ds(pl.multiple_of(blk * BLK, BLK), BLK)

    own_seq = 2 * y

    def keep_or_send(middle, blk, r):
        seq = 1 if middle else own_seq
        i = 4 * seq + blk - 3 * t
        mine = (i >= 0) & (i < 3)

        @pl.when(mine)
        def _():
            rs = rows_of(i)
            dz1_ref[rs, :] += r

        @pl.when(jnp.logical_not(mine))
        def _():
            sbuf[1 if middle else 0, rows_of(blk), :] = r.astype(BF)

    def into_middle(n, _):
        keep_or_send(True, n, dg(dq2[:, rows_of(n)], wts_ref[0], 0, 0))
        return 0

    dq0, dq1, dq2 = [dq_s.at[g] for g in range(3)]

    def into_own(n, _):
        r = dg(dq0[:, rows_of(n)], wts_ref[0], 0, 0) + dg(dq1[:, rows_of(n)], wts_ref[1], 0, 0)
        keep_or_send(False, n, r)
        return 0

    far = 2 * (1 - y)
    half_copy = pltpu.make_async_remote_copy(
        src_ref=sbuf.at[1, rows_of(far + 1 - c)], dst_ref=rhalf, send_sem=send.at[12],
        recv_sem=recv.at[3], device_id={"tensor": core}, device_id_type=MESH,
    )
    far_copy = pltpu.make_async_remote_copy(
        src_ref=hsum, dst_ref=rmid.at[c], send_sem=send.at[13], recv_sem=recv.at[4 + c],
        device_id={"tensor": 2 * (1 - y) + y}, device_id_type=MESH,
    )
    core_copies = []
    for i in range(3):
        middle, blk = block_of(core, i)
        core_copies.append((
            middle,
            pltpu.make_async_remote_copy(
                src_ref=sbuf.at[middle, rows_of(blk)], dst_ref=rcore.at[i], send_sem=send.at[14 + i],
                recv_sem=recv.at[i], device_id={"tensor": core}, device_id_type=MESH,
            ),
        ))

    def unit(u, _):
        g = (u % 3 + 1) % 3
        h = u // 3

        @pl.when(u == 1)
        def _():
            small_core.wait_recv()
            a, b = small_ref[...], tc[...]
            swapped = jnp.concatenate([b[0:8], b[9:10], b[8:9], b[11:12], b[10:11], b[12:16]])
            tv[...] = a + swapped

        @pl.when(u == 2)
        def _():
            big[4].to_y().start()

        @pl.when(u == 5)
        def _():
            big[5].to_y().start()

        @pl.when(u == 8)
        def _():
            load_wts.wait()
            load_dz1.wait()
            lax.fori_loop(0, 4, into_middle, 0)
            half_copy.start()

        @pl.when(h == 0)
        def _():
            for blk in range(4):
                pltpu.make_async_copy(do_in.at[0, pl.ds(0, 192)], do_ref.at[g, blk], landed.at[g * 4 + blk]).wait()

        same = (row64 == seg_ref[pl.ds(jnp.where(g == 2, 1, own_seq), 1), :]).astype(F32)
        ro = pl.multiple_of(h * 192, 64)
        qh, kh, vh = pl.ds(ro, 64), pl.ds(ro + 64, 64), pl.ds(ro + 128, 64)
        l1, l2, l3 = split3(-lse_ref[g * 3 + h])
        qa[0:64, :] = qkv_ref[g, h, 0:64, :]
        qa[64:128, :] = jnp.where(row64 == 8, l1, jnp.where(row64 == 9, l2, jnp.where(row64 == 10, l3, same))).astype(BF)
        key_mark = jnp.where(row64 >= 8, 1.0, (same - 1.0) * BIG).astype(BF)
        ka[...] = jnp.concatenate([qkv_ref[g, h, 64:128, :], key_mark], axis=0).T
        va[...] = jnp.concatenate([qkv_ref[g, h, 128:192, :], jnp.ones((64, length), BF)], axis=0).T
        hs = pl.ds(pl.multiple_of(h * 64, 64), 64)
        for b in range(4):
            bs = slice(b * BLK, (b + 1) * BLK)
            do = do_ref[g, b, hs, :]
            e1, e2, e3 = split3(-jnp.sum(do.astype(F32) * o_ref[g, b, hs, :].astype(F32), axis=0, keepdims=True))
            da[0:64, bs] = do
            rb = row64[:, bs]
            da[64:128, bs] = jnp.where(rb == 8, e1, jnp.where(rb == 9, e2, jnp.where(rb == 10, e3, 0.0))).astype(BF)
        dk[...] = jnp.zeros_like(dk)
        dv[...] = jnp.zeros_like(dv)

        def chunk(n, _):
            for k, steps in STEPS.items():
                @pl.when(2 * u + n == k)
                def _(steps=steps):
                    for stage, name in steps:
                        getattr(every[name], stage)()

            cs = pl.ds(pl.multiple_of(n * 512, 512), 512)
            s = jnp.dot(ka[...], qa[:, cs], preferred_element_type=F32)
            p = jnp.exp2(s)
            dp = jnp.dot(va[...], da[:, cs], preferred_element_type=F32)
            pb = p.astype(BF)
            ds = (p * dp).astype(BF)
            dv[...] += dg(da[0:64, cs], pb, 1, 1)
            dk[...] += dg(qa[0:64, cs], ds, 1, 1)
            dq = jnp.dot(qkv_ref[g, h, 64:128, :], ds, preferred_element_type=F32)
            dq_s[g, qh, cs] = (dq * (HEAD_DIM ** (-0.5))).astype(BF)
            return 0

        lax.fori_loop(0, length // 512, chunk, 0)
        dq_s[g, kh, :] = (dk[...] * math.log(2.0)).astype(BF)
        dq_s[g, vh, :] = dv[...].astype(BF)

        @pl.when(g == 1)
        def _():
            pl.when(h == 0)(load_xab.wait)
            so[1 + h] = jnp.dot(dq_s[1, pl.ds(ro, 192), :], xab_ref[0], preferred_element_type=F32).astype(BF)

        for k, pieces in ((0, thin[1:2]), (3, thin[2:3]), (6, thin[3:])):
            @pl.when(u == k)
            def _(pieces=pieces):
                for piece in pieces:
                    piece.to_y().start()

        @pl.when(g == 0)
        def _():
            rows = pl.ds(ro, 192)
            r = jnp.dot(dq_s[0, rows, :], xab_ref[0], preferred_element_type=F32)
            sv[1 + h] = (r + jnp.dot(dq_s[2, rows, :], xab_ref[1], preferred_element_type=F32)).astype(BF)

        return 0

    load_qkv.wait()
    load_o.wait()
    lax.fori_loop(0, 9, unit, 0)
    for stage, name in FIRST_TAIL:
        getattr(every[name], stage)()
    half_copy.wait_recv()
    hsum[...] = (sbuf[1, rows_of(far + c), :].astype(F32) + rhalf[...].astype(F32)).astype(BF)
    far_copy.start()
    ones = jnp.ones((8, length), BF)
    tv[12:13, 0:576] = (dg(ones, dq_s[0], 1, 1) + dg(ones, dq_s[2], 1, 1))[0:1]
    tv[13:14, 0:576] = dg(ones, dq_s[1], 1, 1)[0:1]
    to[...] = tv[...]
    tiny.to_y().start()
    lax.fori_loop(0, 4, into_own, 0)
    for middle, copy in core_copies:
        copy.start()

    for k, (stage, name) in enumerate(TAIL_STEPS):
        getattr(every[name], stage)()
        if k == TAIL_INPUT:
            for i in range(3):
                core_copies[i][1].wait_recv()
                middle, blk = block_of(t, i)
                rs = pl.ds(i * BLK, BLK)

                @pl.when(middle == 0)
                def _():
                    din_ref[rs, :] = (dz1_ref[rs, :] + rcore[i].astype(F32)).astype(BF)

                @pl.when(middle == 1)
                def _():
                    k = blk % 2
                    pltpu.make_async_copy(hsum, rmid.at[k], recv.at[4 + k]).wait()
                    din_ref[rs, :] = (dz1_ref[rs, :] + rcore[i].astype(F32) + rmid[k].astype(F32)).astype(BF)

    for p, piece in enumerate(big):
        piece.finish(p >= early)
    for piece in thin + [tiny]:
        piece.finish()
    for copy in [c for _, c in core_copies] + [half_copy, far_copy] + go_core + [small_core]:
        copy.wait_send()
    for cond, copy in pending:
        if cond is None:
            copy.wait_send()
        else:
            pl.when(cond)(copy.wait_send)

def finish(
    out_in, din_in, ff_in, fs_in, sm,
    out_o, din_o, gwq, gbq, gwk, gwv, gbv, gwo, gbo, gg1, gs1, gwin, gbin, gwback, gbback, gg2, gs2,
    out_v, din_v, ff, fs, win_v, wback_v, q_v, wo_v, local,
):
    loads = [
        pltpu.make_async_copy(ff_in, ff, local.at[0]),
        pltpu.make_async_copy(fs_in, fs, local.at[1]),
        pltpu.make_async_copy(out_in, out_v, local.at[2]),
        pltpu.make_async_copy(din_in, din_v, local.at[3]),
    ]
    start_all(loads)
    stores = []

    def store(src, dst):
        copy = pltpu.make_async_copy(src, dst, local.at[4 + len(stores)])
        copy.start()
        stores.append(copy)

    for k, ref in ((0, gbo), (1, gg1), (2, gs1), (8, gbin), (3, gbback), (4, gg2), (5, gs2)):
        ref[...] = sm[k : k + 1, :].reshape(768)
    heads = sm[12:13, 0:576]
    for k, ref in ((0, gbq), (2, gbv)):
        ref[...] = jnp.concatenate([heads[:, 192 * h + 64 * k : 192 * h + 64 * k + 64] for h in range(3)], axis=1).reshape(192)
    loads[0].wait()
    for ch in range(3):
        cs = slice(ch * BLK, (ch + 1) * BLK)
        wback_v[cs, :] = ff[2 * ch + 1].T.astype(F32)
        win_v[:, cs] = ff[2 * ch].astype(F32)
    store(wback_v, gwback)
    store(win_v, gwin)
    loads[2].wait()
    store(out_v, out_o)
    loads[3].wait()
    store(din_v, din_o)
    loads[1].wait()
    wo_v[...] = fs[0].astype(F32)
    store(wo_v, gwo)
    for k, ref in enumerate((gwq, gwk, gwv)):
        for h in range(3):
            q_v[k, 64 * h : 64 * h + 64, :] = fs[1 + h, 64 * k : 64 * k + 64, :].astype(F32)
        store(q_v.at[k], ref)
    for copy in stores:
        copy.wait()


def vm(*shape, dtype=BF):
    return pltpu.VMEM(shape, dtype)


def sds(*shape, dtype=BF):
    return jax.ShapeDtypeStruct(shape, dtype)


VM = pl.BlockSpec(memory_space=pltpu.VMEM)
ANY = pl.BlockSpec(memory_space=pl.ANY)


def params(cid):
    return pltpu.CompilerParams(collective_id=cid, has_side_effects=True, vmem_limit_bytes=62 * 2**20)


def local_step(
    line,
    layer_input, segment_ids, w_query, b_query, w_key, w_value, b_value, w_out, b_out, first_gain, first_shift,
    w_in, b_in, w_back, b_back, second_gain, second_shift, cotangent,
):
    dma = pltpu.SemaphoreType.DMA
    qkv, o, lse, xab, wts, out, dz1, do, gf, go, small = pl.pallas_call(
        partial(forward, line),
        out_shape=(
            sds(3, 3, 192, 1024), sds(3, 4, 192, BLK), sds(9, 1, 1024, dtype=F32), sds(2, 1024, 768), sds(2, 576, 768),
            sds(768, 768), sds(768, 768, dtype=F32), sds(3, 768, BLK), sds(2, 3, 2, 768, BLK), sds(4, 192, 768),
            sds(16, 768, dtype=F32),
        ),
        in_specs=[VM, ANY] + [VM] * 13 + [ANY] * 3,
        out_specs=(ANY, ANY, VM, ANY, ANY, ANY, ANY, ANY, ANY, ANY, VM),
        scratch_shapes=[
            vm(768, 768), vm(3, 768, BLK), vm(2, 3, 2, 768, BLK), vm(4, 192, 768),
            vm(3, 3, 192, 1024), vm(3, 4, 192, BLK), vm(2, 1024, 768), vm(2, 576, 768),
            vm(8, 768, dtype=F32), vm(3, 8, 768, dtype=F32), vm(576, 1, dtype=F32),
            vm(128, 1024), vm(128, 1024), vm(80, 1024),
            vm(768, 768), vm(3, 768, BLK), vm(768, 768), vm(768, 3072), vm(3072, 768),
            vm(768, 768), vm(768, 768), vm(768, 768, dtype=F32), vm(768, 1, dtype=F32), vm(768, 3072), vm(768, 3072),
            vm(768, 768, dtype=F32), vm(768, 768), vm(768, 768),
            vm(3, 2, 768, BLK), vm(3, 2, 768, BLK), vm(max(Y_EARLY, 1), 768, BLK), vm(max(X_EARLY, 1), 768, BLK),
            dma((80,)), dma((80,)), dma((24,)),
        ],
        compiler_params=params(0),
        name="forward_and_feed_forward",
    )(
        layer_input, cotangent, w_query.T, w_key.T, w_value.T, b_query, b_value, b_in,
        b_out, first_gain, first_shift, b_back, second_gain, second_shift, segment_ids, w_out, w_in, w_back,
    )

    piece, slab, tiny = vm(6, 768, BLK), vm(4, 192, 768), vm(16, 768, dtype=F32)
    din, ff, fs, sm = pl.pallas_call(
        partial(k3, line),
        out_shape=(sds(768, 768), sds(6, 768, BLK), sds(4, 192, 768), sds(16, 768, dtype=F32)),
        in_specs=[ANY, VM, ANY, VM, ANY, ANY, ANY, ANY, ANY, ANY, VM],
        out_specs=(VM, VM, VM, VM),
        scratch_shapes=[
            vm(3, 3, 192, 1024), vm(3, 4, 192, BLK), vm(2, 1024, 768), vm(2, 576, 768), vm(4, 192, 768),
            vm(768, 768, dtype=F32),
            vm(3, 4, 192, BLK), vm(3, 576, 1024), vm(128, 1024), vm(1024, 128), vm(1024, 128), vm(128, 1024),
            vm(64, 1024, dtype=F32), vm(64, 1024, dtype=F32), vm(2, 1024, 768),
            vm(3, BLK, 768), vm(2, BLK, 768), vm(BLK, 768), vm(BLK, 768),
            piece, piece, piece, piece, piece, slab, slab, slab, slab, slab, slab, vm(2, 192, 768),
            tiny, tiny, tiny, tiny, tiny, tiny, tiny,
            dma((16, 6)), dma((16, 6)), dma((17,)), dma((9,)), dma((12,)), dma((12,)),
        ],
        compiler_params=params(1),
        name="attention_backward",
    )(qkv, segment_ids, o, lse, xab, wts, do, dz1, gf, go, small)
    if not line:
        ff, fs = lax.psum((ff, fs), "dp")
        sm = lax.psum(sm, "dp")
    row = sds(768, dtype=F32)
    cols, thin = sds(192, 768, dtype=F32), sds(192, dtype=F32)
    square = sds(768, 768, dtype=F32)
    outs = pl.pallas_call(
        finish,
        out_shape=(
            sds(768, 768), sds(768, 768), cols, thin, cols, cols, thin, sds(192, 768, dtype=F32),
            row, row, row, square, row, square, row, row, row,
        ),
        in_specs=[ANY, ANY, ANY, ANY, VM],
        out_specs=(ANY, ANY, ANY, VM, ANY, ANY, VM, ANY, VM, VM, VM, ANY, VM, ANY, VM, VM, VM),
        scratch_shapes=[
            vm(768, 768), vm(768, 768), vm(6, 768, BLK), vm(4, 192, 768), vm(768, 768, dtype=F32), vm(768, 768, dtype=F32),
            vm(3, 192, 768, dtype=F32), vm(192, 768, dtype=F32), dma((16,)),
        ],
        compiler_params=pltpu.CompilerParams(vmem_limit_bytes=62 * 2**20),
        name="results",
    )(out, din, ff, fs, sm)
    return (*outs[:2], outs[2].T, outs[3], outs[4].T, outs[5].T, *outs[6:])


def solution(mesh):
    rows = P(("dp", "tensor"), None)
    in_specs = (
        rows, P("dp", None), P(None, "tensor"), P("tensor"), P(None, "tensor"), P(None, "tensor"), P("tensor"),
        P("tensor", None), P(), P(), P(), P(None, "tensor"), P("tensor"), P("tensor", None), P(), P(), P(), rows,
    )
    out_specs = (
        rows, rows, P(None, "tensor"), P("tensor"), P(None, "tensor"), P(None, "tensor"), P("tensor"),
        P("tensor", None), P(), P(), P(), P(None, "tensor"), P("tensor"), P("tensor", None), P(), P(), P(),
    )
    line = mesh.shape["dp"] == 8
    return jax.shard_map(partial(local_step, line), mesh=mesh, in_specs=in_specs, out_specs=out_specs, check_vma=False)
```

```python
import math
from functools import partial

import jax
import jax.numpy as jnp
from jax import lax
from jax.experimental import pallas as pl
from jax.experimental.pallas import tpu as pltpu
from jax.sharding import PartitionSpec as P

F32 = jnp.float32
BF = jnp.bfloat16
MESH = pl.DeviceIdType.MESH
HEAD_DIM = 64
EPSILON = 1e-05
BIG = 1e30
LOG2E = 1.0 / math.log(2.0)
QSCALE = HEAD_DIM ** (-0.5) * LOG2E
BLK = 256
Y_EARLY = 3
X_EARLY = 1
SPLIT = (2, 3, 4, 5)
AY, AX, AE, AM, AF = "after_y", "after_x", "after_end", "after_mate", "after_final"
STEPS = {
    3: ((AE, 0), (AX, 1),),
    4: ((AY, 6),),
    5: ((AX, 2),),
    7: ((AM, 0), (AE, 1), (AX, 6), (AY, 3),),
    9: ((AE, 2), (AY, 7),),
    10: ((AX, 3),),
    11: ((AM, 1), (AE, 6),),
    12: ((AX, 7), (AY, 4),),
    13: ((AM, 2), (AE, 3),),
    14: ((AY, 8),),
    15: ((AM, 6), (AE, 7), (AX, 4),),
    16: ((AM, 3),),
    17: ((AX, 8), (AY, 5),),
}
FIRST_TAIL = (
    (AE, 4),
    (AM, 7),
    (AY, 9),
)
TAIL_INPUT = 20
TAIL_STEPS = (
    (AY, 10),
    (AY, 11),
    (AY, 12),
    (AY, 13),
    (AY, 14),
    (AF, 2),
    (AX, 5),
    (AY, -1),
    (AX, 9),
    (AF, 3),
    (AE, 8),
    (AX, 10),
    (AM, 4),
    (AX, 11),
    (AX, 12),
    (AX, 13),
    (AE, 5),
    (AX, 14),
    (AE, 9),
    (AE, 10),
    (AE, 11),
    (AM, 8),
    (AE, 12),
    (AE, 13),
    (AX, -1),
    (AF, 4),
    (AE, 14),
    (AM, 5),
    (AE, -1),
    (AM, 9),
    (AM, 10),
    (AM, 11),
    (AM, 12),
    (AM, 13),
    (AM, 14),
    (AM, -1),
    (AF, 5),
)


def dg(a, b, ca, cb):
    return lax.dot_general(a, b, (((ca,), (cb,)), ((), ())), preferred_element_type=F32)


def where_am_i():
    t = lax.axis_index("tensor")
    d = lax.axis_index("dp")
    core = t + 1 - 2 * (t % 2)
    across = (t + 2) % 4
    diag = 3 - t
    side = d + 1 - 2 * (d % 2)
    return t, d, core, across, diag, side


def block_of(t, i):
    b = 3 * t + i
    middle = (b // 4) % 2
    return middle, b % 4


def greet(devices):
    barrier = pltpu.get_barrier_semaphore()
    for dev in devices:
        pl.semaphore_signal(barrier, inc=1, device_id=dev, device_id_type=MESH)
    pl.semaphore_wait(barrier, len(devices))


def half_rows(half, total, pieces, i):
    n = total // 2 // pieces
    return pl.ds(pl.multiple_of(half * (total // 2) + i * n, n), n)


class Copies:
    def __init__(self, send, recv):
        self.send, self.recv, self.used = send, recv, 0

    def new(self, src, dst, **device):
        k = self.used
        self.used += 1
        return pltpu.make_async_remote_copy(
            src_ref=src,
            dst_ref=dst,
            send_sem=self.send.at[k],
            recv_sem=self.recv.at[k],
            device_id=device,
            device_id_type=MESH,
        )


def start_all(copies):
    for copy in copies:
        copy.start()


def layer_stats(z):
    mean = jnp.mean(z, axis=-1, keepdims=True)
    cen = z - mean
    var = jnp.mean(cen * cen, axis=-1, keepdims=True)
    inv = lax.rsqrt(var + EPSILON)
    return cen * inv, inv


def forward(
    line,
    x_ref, cot_in, wq_ref, wk_ref, wv_ref, bq_ref, bv_ref, bin_ref, v0, v1, v2, v3, v4, v5, seg_ref,
    wout_ref, win_ref, wback_ref,
    qkv_out, o_out, lse_ref, xab_out, wts_out, out_out, dz1_out, do_out, gf_out, go_out, small_ref,
    out_ref, do_ref, gf_ref, go_ref, qkv, o_v, xab, w_v, bias_ref, biasg_ref, bcol, qa, ka, va,
    cot_ref, ot, wo, wi, wb, h1b, h1t, xh1, inv1, gg, gp, z2, dz2b, dz2t, gsend, rc, ry, rx, send, recv, local,
):
    length = 1024
    t, d, core, across, diag, side = where_am_i()
    y, c = t // 2, t % 2
    half = d % 2
    zbit = (d // 2) % 2
    pair = d + 2 - 4 * zbit
    x_early = X_EARLY if line else 0

    rows_out, rows_local = [], []
    cp = Copies(send, recv)
    cp.used = 12
    for i in range(3):
        middle, blk = block_of(t, i)
        src = x_ref.at[pl.ds(i * BLK, BLK)]
        dst = xab.at[middle, pl.ds(pl.multiple_of(blk * BLK, BLK), BLK)]
        rows_local.append(pltpu.make_async_copy(src, dst, local.at[i]))
        rows_out.append(cp.new(src, dst, tensor=core))
    own = [
        pltpu.make_async_copy(wout_ref, wo.at[pl.ds(0, 192)], local.at[12]),
        pltpu.make_async_copy(win_ref, wi.at[:, pl.ds(0, 768)], local.at[13]),
        pltpu.make_async_copy(wback_ref, wb.at[pl.ds(0, 768)], local.at[14]),
        pltpu.make_async_copy(cot_in, cot_ref, local.at[15]),
    ]
    start_all(rows_local + own)

    for k, ref in enumerate((wq_ref, wk_ref, wv_ref)):
        for h in range(3):
            n = 192 * h + 64 * k
            w_v[0, n : n + 64, :] = ref[64 * h : 64 * h + 64, :]
    bias_ref[...] = jnp.zeros((8, 768), F32)
    bias_ref[0:1, :] = bin_ref[...].astype(F32).reshape(1, 768)
    bq, bv = bq_ref[...].astype(F32).reshape(1, 192), bv_ref[...].astype(F32).reshape(1, 192)
    parts = []
    for h in range(3):
        parts += [bq[:, 64 * h : 64 * h + 64], jnp.zeros((1, 64), F32), bv[:, 64 * h : 64 * h + 64]]
    bias_ref[1:2, 0:576] = jnp.concatenate(parts, axis=1)

    greet([{"tensor": core}, {"tensor": across}, {"tensor": diag}, {"dp": side}, {"dp": pair}])

    mixed = (t == 1) | (t == 2)
    k_out = jnp.where(mixed, 0, 1)
    block_out = pl.ds(pl.multiple_of((2 * y + k_out) * BLK, BLK), BLK)
    block_in = pl.ds(pl.multiple_of((2 * (1 - y) + c) * BLK, BLK), BLK)
    n = cp.used
    cross_out = cp.new(xab.at[1, block_out], xab.at[1, block_out], tensor=2 * (1 - y) + k_out)
    cross_arrived = pltpu.make_async_remote_copy(
        src_ref=xab.at[1, block_out], dst_ref=xab.at[1, block_in], send_sem=send.at[n], recv_sem=recv.at[n],
        device_id={"tensor": core}, device_id_type=MESH,
    )
    cross_forward = cp.new(xab.at[1, block_in], xab.at[1, block_in], tensor=core)
    wp_first, wp_second = [], []
    for i in range(3):
        part = half_rows(half, 576, 3, i)
        wp_first.append(cp.new(w_v.at[0, part], w_v.at[1, part], tensor=across))
        wp_second.append(cp.new(w_v.at[1, part], w_v.at[1, part], dp=side))
    bias_out = [
        cp.new(bias_ref, biasg_ref.at[0], tensor=core),
        cp.new(bias_ref, biasg_ref.at[1], tensor=across),
        cp.new(bias_ref, biasg_ref.at[2], tensor=diag),
    ]
    part = half_rows(half, 192, 1, 0)
    place = pl.ds(part.start + 384, part.size)
    wo_first = cp.new(wout_ref.at[part], wo.at[place], tensor=across)
    wo_second = cp.new(wo.at[place], wo.at[place], dp=side)
    wo_core = cp.new(wout_ref, wo.at[pl.ds(192, 192)], tensor=core)
    wo_diag = cp.new(wo.at[pl.ds(384, 192)], wo.at[pl.ds(576, 192)], tensor=core)

    def lanes(j):
        return pl.ds(768 * j, 768)

    in_core = cp.new(win_ref, wi.at[:, lanes(1)], tensor=core)
    back_core = cp.new(wback_ref, wb.at[lanes(1)], tensor=core)
    in_first, in_second, in_third, in_diag, back_first, back_second, back_diag = [], [], [], [], [], [], []
    for i in range(3):
        part = half_rows(half, 768, 3, i)
        first_part = part
        if i < 2:
            z_part = half_rows(zbit, 768, 3, i)
            first_part = pl.ds(pl.multiple_of(z_part.start + 64 * half, 64), 64)
            in_third.append(cp.new(wi.at[z_part, lanes(2)], wi.at[z_part, lanes(2)], dp=pair))
        in_first.append(cp.new(win_ref.at[first_part], wi.at[first_part, lanes(2)], tensor=across))
        in_second.append(cp.new(wi.at[first_part, lanes(2)], wi.at[first_part, lanes(2)], dp=side))
        place = pl.ds(part.start + 2 * 768, part.size)
        back_first.append(cp.new(wback_ref.at[part], wb.at[place], tensor=across))
        back_second.append(cp.new(wb.at[place], wb.at[place], dp=side))
        for h in range(2):
            both = half_rows(h, 768, 3, i)
            in_diag.append(cp.new(wi.at[both, lanes(2)], wi.at[both, lanes(3)], tensor=core))
            m = h * 384 + i * 128
            back_diag.append(cp.new(wb.at[pl.ds(2 * 768 + m, 128)], wb.at[pl.ds(3 * 768 + m, 128)], tensor=core))

    peers = (t, core, across, diag)

    def heads_to_rows(group):
        found = []
        for j, dev in enumerate(peers):
            if group != 2 and j >= 2:
                continue
            for i in range(3):
                middle, blk = block_of(dev, i)
                slot = j + 2 if group == 1 else j
                src, dst = o_v.at[group, blk], ot.at[i, pl.ds(slot * 192, 192)]
                sem = recv.at[i * 4 + slot]
                if j == 0:
                    copy = pltpu.make_async_copy(src, dst, sem)
                else:
                    copy = pltpu.make_async_remote_copy(
                        src_ref=src, dst_ref=dst, send_sem=send.at[9 + i if group == 1 else 3 * (j - 1) + i],
                        recv_sem=sem, device_id={"tensor": dev}, device_id_type=MESH,
                    )
                found.append((j, (middle == 1) if group == 2 else (middle == 0), copy))
        return found

    def start_heads(group):
        for _, cond, copy in heads_to_rows(group):
            pl.when(cond)(copy.start)

    start_all(rows_out + bias_out + wp_first[:1])
    start_all([wo_core, in_core, back_core])
    va[64:80, :] = jnp.ones((16, length), BF)
    row64 = lax.broadcasted_iota(jnp.int32, (64, length), 0)
    factor = jnp.where(lax.broadcasted_iota(jnp.int32, (576, 1), 0) % 192 < 64, QSCALE, 1.0)

    def outgoing(g):
        return [
            pltpu.make_async_copy(qkv.at[g], qkv_out.at[g], local.at[4 + 2 * (g % 3)]),
            pltpu.make_async_copy(o_v.at[g], o_out.at[g], local.at[5 + 2 * (g % 3)]),
        ]

    def at(n, k, copies_recv, copies_start=()):
        @pl.when(n == k)
        def _():
            for copy in copies_recv:
                copy.wait_recv()
            start_all(copies_start)

    def unit(u, _):
        g = (2 * (u // 3)) % 3
        h = u % 3
        par = jnp.where(g == 1, 1, 0)
        middle = jnp.where(g == 2, 1, 0)

        at(u, 1, wp_first[:1], wp_second[:1])

        @pl.when(u == 3)
        def _():
            cross_arrived.wait_recv()
            cross_forward.start()
            start_heads(0)
            cross_forward.wait_recv()

        at(u, 4, wp_first[1:2], wp_second[1:2])
        at(u, 5, wp_first[2:3], wp_second[2:3])

        @pl.when(u == 6)
        def _():
            start_heads(2)
            start_all(in_first[2:] + back_first)

        at(u, 6, [wo_first], [wo_second])
        at(u, 6, wp_second + [bias_out[1]])
        at(u, 7, in_first[:2], in_second[:2])
        at(u, 8, in_second[:1], in_third[:1])
        at(u, 8, [wo_second], [wo_diag])

        @pl.when(h == 0)
        def _():
            @pl.when(u > 0)
            def _():
                start_all(outgoing(jnp.where(g == 2, 0, 2)))

            @pl.when(par == 0)
            def _():
                bcol[...] = jnp.transpose(bias_ref[...])[0:576, 1:2]

            @pl.when(par == 1)
            def _():
                bcol[...] = jnp.transpose(biasg_ref[1])[0:576, 1:2]

            col = bcol[...]

            def body(n, _):
                cs = pl.ds(pl.multiple_of(n * BLK, BLK), BLK)
                r = (dg(w_v[par], xab[middle, cs, :], 1, 1) + col) * factor
                for k in range(3):
                    qkv[g, k, :, cs] = r[192 * k : 192 * (k + 1)].astype(BF)
                return 0

            lax.fori_loop(0, length // BLK, body, 0)
            same = (row64 == seg_ref[pl.ds(jnp.where(g == 2, 1, 2 * y), 1), :]).astype(F32)
            qa[64:128, :] = same.astype(BF)
            ka[64:128, :] = ((same - 1.0) * BIG).astype(BF)

        qa[0:64, :] = qkv[g, h, 0:64, :]
        ka[0:64, :] = qkv[g, h, 64:128, :]
        va[0:64, :] = qkv[g, h, 128:192, :]
        s = jnp.dot(ka[...].T, qa[...], preferred_element_type=F32)
        m = jnp.max(s, axis=0, keepdims=True)
        p = jnp.exp2(s - m).astype(BF)
        o = jnp.dot(va[...], p, preferred_element_type=F32)
        total = o[64:65, :]
        res = (o[0:64] * (1.0 / total)).astype(BF)
        hs = pl.ds(pl.multiple_of(h * 64, 64), 64)
        for b in range(4):
            o_v[g, b, hs, :] = res[:, b * BLK : (b + 1) * BLK]
        lse_ref[g * 3 + h] = m + jnp.log2(total)
        return 0

    for copy in rows_local:
        copy.wait()
    for copy in rows_out:
        copy.wait_recv()
    start_all([cross_out] + wp_first[1:] + [wo_first] + in_first[:2])
    lax.fori_loop(0, 9, unit, 0)
    start_heads(1)
    tail = outgoing(1)
    tail.append(pltpu.make_async_copy(xab, xab_out, local.at[10]))
    tail.append(pltpu.make_async_copy(w_v, wts_out, local.at[11]))
    start_all(tail)

    b_out, gain1, shift1, b_back, gain2, shift2 = [v[...].reshape(1, 768) for v in (v0, v1, v2, v3, v4, v5)]
    own[0].wait()
    for copy in [wo_core, wo_diag, bias_out[0], bias_out[2]]:
        copy.wait_recv()
    in_second[1].wait_recv()
    in_third[1].start()
    for i in range(3):
        for slot in range(4):
            pltpu.make_async_copy(o_v.at[0, 0], ot.at[i, pl.ds(slot * 192, 192)], recv.at[i * 4 + slot]).wait()

    def first(i, _):
        rs = pl.ds(pl.multiple_of(i * BLK, BLK), BLK)
        z = x_ref[rs, :].astype(F32) + dg(ot[i], wo[...], 0, 0) + b_out
        xh, inv = layer_stats(z)
        xh1[rs, :] = xh
        inv1[rs, :] = inv
        h1b[rs, :] = (xh * gain1 + shift1).astype(BF)
        return 0

    lax.fori_loop(0, 3, first, 0)
    h1t[...] = h1b[...].T
    own[1].wait()

    def up(n, _):
        at(n, 0, in_first[2:], in_second[2:])
        at(n, 3, [in_core])
        at(n, 5, back_first[:1], back_second[:1])
        at(n, 6, in_third + in_second[2:], in_diag)
        at(n, 7, back_first[1:2], back_second[1:2])
        at(n, 9, in_diag)
        at(n, 9, back_second[:1], back_diag[:2])
        at(n, 10, back_first[2:], back_second[2:])
        at(n, 11, back_second[1:2], back_diag[2:4])
        cs = pl.ds(pl.multiple_of(n * BLK, BLK), BLK)
        j = n // 3
        low = pl.ds(pl.multiple_of((n % 3) * BLK, BLK), BLK)
        bias = jnp.where(j == 0, bias_ref[0:1, low], biasg_ref[jnp.maximum(j - 1, 0), 0:1, low])
        u = jnp.dot(h1b[...], wi[:, cs], preferred_element_type=F32) + bias
        cdf = 0.5 * (1.0 + lax.erf(u * (2.0 ** -0.5)))
        pdf = jnp.exp(-0.5 * u * u) * (1.0 / math.sqrt(2.0 * math.pi))
        gg[:, cs] = (u * cdf).astype(BF)
        gp[:, cs] = (cdf + u * pdf).astype(BF)
        return 0

    lax.fori_loop(0, 12, up, 0)
    own[2].wait()
    back_core.wait_recv()

    def down_near(n, _):
        cs = pl.ds(pl.multiple_of(n * BLK, BLK), BLK)
        z2[:, cs] = jnp.dot(gg[:, 0:1536], wb[0:1536, cs], preferred_element_type=F32)
        return 0

    def down_far(n, _):
        cs = pl.ds(pl.multiple_of(n * BLK, BLK), BLK)
        z2[:, cs] += jnp.dot(gg[:, 1536:3072], wb[1536:3072, cs], preferred_element_type=F32)
        return 0

    lax.fori_loop(0, 3, down_near, 0)
    back_second[2].wait_recv()
    start_all(back_diag[4:])
    own[3].wait()
    for copy in back_diag:
        copy.wait_recv()
    lax.fori_loop(0, 3, down_far, 0)

    def second_norm(i, sums):
        rs = pl.ds(pl.multiple_of(i * BLK, BLK), BLK)
        h1 = xh1[rs, :] * gain1 + shift1
        xh, inv = layer_stats(h1 + z2[rs, :] + b_back)
        out_ref[rs, :] = (xh * gain2 + shift2).astype(BF)
        cot = cot_ref[rs, :].astype(F32)
        dxh = cot * gain2
        dz = inv * (dxh - jnp.mean(dxh, axis=-1, keepdims=True) - xh * jnp.mean(dxh * xh, axis=-1, keepdims=True))
        z2[rs, :] = dz
        dz2b[rs, :] = dz.astype(BF)
        return (
            sums[0] + jnp.sum(dz, axis=0, keepdims=True),
            sums[1] + jnp.sum(cot * xh, axis=0, keepdims=True),
            sums[2] + jnp.sum(cot, axis=0, keepdims=True),
        )

    zero = jnp.zeros((1, 768), F32)
    s3, s4, s5 = lax.fori_loop(0, 3, second_norm, (zero, zero, zero))
    small_ref[3:4, :] = s3
    small_ref[4:5, :] = s4
    small_ref[5:6, :] = s5
    out_copy = pltpu.make_async_copy(out_ref, out_out, local.at[16])
    out_copy.start()
    dz2t[...] = dz2b[...].T

    base = cp.used

    def to_core(stage, ch):
        k = base + stage * 3 + ch
        return pltpu.make_async_remote_copy(
            src_ref=gsend.at[ch], dst_ref=rc.at[ch], send_sem=send.at[k], recv_sem=recv.at[k],
            device_id={"tensor": core}, device_id_type=MESH,
        )

    def to_across(p):
        k = base + 6 + p
        return pltpu.make_async_remote_copy(
            src_ref=gf_ref.at[1, p // 2, p % 2], dst_ref=ry.at[p], send_sem=send.at[k], recv_sem=recv.at[k],
            device_id={"tensor": across}, device_id_type=MESH,
        )

    def to_side(p):
        k = base + 12 + p
        return pltpu.make_async_remote_copy(
            src_ref=gf_ref.at[0, p // 2, p % 2], dst_ref=rx.at[p], send_sem=send.at[k], recv_sem=recv.at[k],
            device_id={"dp": side}, device_id_type=MESH,
        )

    def back(m, _):
        stage = m // 6
        ch = (m % 6) // 2
        slot = 3 - 2 * stage - m % 2
        n = slot * 3 + ch
        cs = pl.ds(pl.multiple_of(n * BLK, BLK), BLK)
        low = pl.ds(pl.multiple_of(ch * BLK, BLK), BLK)
        g_back = jnp.dot(dz2t[...], gg[:, cs], preferred_element_type=F32)
        du = (dg(dz2b[...], wb[cs, :], 1, 1) * gp[:, cs].astype(F32)).astype(BF)
        gg[:, cs] = du
        small_ref[pl.ds(8 + slot, 1), low] = jnp.sum(du.astype(F32), axis=0, keepdims=True)
        g_in = jnp.dot(h1t[...], du, preferred_element_type=F32)

        @pl.when(m % 2 == 0)
        def _():
            pl.when(stage == 1)(to_core(0, ch).wait_send)
            gsend[ch, 0] = g_in.astype(BF)
            gsend[ch, 1] = g_back.astype(BF)
            to_core(stage, ch).start()

        @pl.when(m % 2 == 1)
        def _():
            to_core(stage, ch).wait_recv()
            gf_ref[1 - stage, ch, 0] = (g_in + rc[ch, 0].astype(F32)).astype(BF)
            gf_ref[1 - stage, ch, 1] = (g_back + rc[ch, 1].astype(F32)).astype(BF)
            for p in range(Y_EARLY):
                pl.when((stage == 0) & (ch == p // 2))(to_across(p).start)

        return 0

    lax.fori_loop(0, 12, back, 0)

    def gf_copy(p):
        k = (0, p // 2, p % 2)
        return pltpu.make_async_copy(gf_ref.at[k], gf_out.at[k], local.at[18 + p])

    gf_other = pltpu.make_async_copy(gf_ref.at[1], gf_out.at[1], local.at[17])
    start_all([gf_other] + [gf_copy(p) for p in range(Y_EARLY, 6)])

    def take(p, arrived):
        k = (0, p // 2, p % 2)
        gf_ref[k] = (gf_ref[k].astype(F32) + arrived[p].astype(F32)).astype(BF)

    for p in range(x_early):
        to_across(p).wait_recv()
        take(p, ry)
        to_side(p).start()

    def into_h(n, _):
        cs = pl.ds(pl.multiple_of(n * BLK, BLK), BLK)
        z2[:, cs] += dg(gg[...], wi[cs, :], 1, 1)
        return 0

    lax.fori_loop(0, 3, into_h, 0)

    def first_norm(i, sums):
        rs = pl.ds(pl.multiple_of(i * BLK, BLK), BLK)
        dh = z2[rs, :]
        xh = xh1[rs, :]
        dxh = dh * gain1
        dz = inv1[rs, :] * (dxh - jnp.mean(dxh, axis=-1, keepdims=True) - xh * jnp.mean(dxh * xh, axis=-1, keepdims=True))
        z2[rs, :] = dz
        dzb = dz.astype(BF)
        dz2b[rs, :] = dzb
        do_ref[i] = dg(wo[...], dzb, 1, 1).astype(BF)
        return (
            sums[0] + jnp.sum(dz, axis=0, keepdims=True),
            sums[1] + jnp.sum(dh * xh, axis=0, keepdims=True),
            sums[2] + jnp.sum(dh, axis=0, keepdims=True),
        )

    s0, s1, s2 = lax.fori_loop(0, 3, first_norm, (zero, zero, zero))
    dz1_copy = pltpu.make_async_copy(z2, dz1_out, local.at[0])
    do_copy = pltpu.make_async_copy(do_ref, do_out, local.at[1])
    start_all([dz1_copy, do_copy])
    small_ref[0:1, :] = s0
    small_ref[1:2, :] = s1
    small_ref[2:3, :] = s2
    for j in range(4):
        rows = pl.ds(192 * j, 192)
        acc = jnp.dot(ot[0, rows, :], dz2b[0:BLK, :], preferred_element_type=F32)
        acc += jnp.dot(ot[1, rows, :], dz2b[BLK : 2 * BLK, :], preferred_element_type=F32)
        acc += jnp.dot(ot[2, rows, :], dz2b[2 * BLK : 3 * BLK, :], preferred_element_type=F32)
        go_ref[j] = acc.astype(BF)
    go_copy = pltpu.make_async_copy(go_ref, go_out, local.at[2])
    go_copy.start()
    small_ref[6:8, :] = jnp.zeros((2, 768), F32)
    small_ref[12:16, :] = jnp.zeros((4, 768), F32)

    for group in range(3):
        for j, cond, copy in heads_to_rows(group):
            if j:
                pl.when(cond)(copy.wait_send)
    sent = rows_out + [cross_out, cross_forward] + wp_first + wp_second + bias_out
    sent += [wo_first, wo_second, wo_core, wo_diag, in_core, back_core]
    sent += in_first + in_second + in_third + in_diag + back_first + back_second + back_diag
    for copy in sent + [to_core(1, ch) for ch in range(3)]:
        copy.wait_send()
    for copy in outgoing(0) + outgoing(2) + tail + [dz1_copy, do_copy, out_copy, gf_other] + [gf_copy(p) for p in range(Y_EARLY, 6)]:
        copy.wait()
    for p in range(Y_EARLY):
        if p >= x_early:
            to_across(p).wait_recv()
            take(p, ry)
            gf_copy(p).start()
        to_across(p).wait_send()
    for p in range(x_early):
        to_side(p).wait()
        take(p, rx)
        gf_copy(p).start()
    for p in range(Y_EARLY):
        gf_copy(p).wait()
    go_copy.wait()


def split3(v):
    a = v.astype(BF).astype(F32)
    b = (v - a).astype(BF).astype(F32)
    return a, b, v - a - b


class Piece:
    def __init__(self, value, other, from_y, from_x, from_end, from_mate, final, send, recv, where, fold=None, split=False):
        self.value, self.other, self.final = value, other, final
        self.from_y, self.from_x, self.from_end, self.from_mate = from_y, from_x, from_end, from_mate
        self.send, self.recv, self.where, self.fold = send, recv, where, fold
        self.split = split

    def part(self, ref, which):
        if not self.split:
            return ref
        n = 768 // 2
        return ref.at[pl.ds(pl.multiple_of(which * n, n), n)]

    def mine(self, ref):
        return self.part(ref, self.where["half"])

    def copy(self, stage, src, dst, **device):
        return pltpu.make_async_remote_copy(
            src_ref=src, dst_ref=dst, send_sem=self.send.at[stage], recv_sem=self.recv.at[stage],
            device_id=device, device_id_type=MESH,
        )

    def to_y(self):
        return self.copy(0, self.other, self.from_y, tensor=self.where["across"])

    def to_x(self):
        away = 1 - self.where["half"]
        return self.copy(1, self.part(self.value, away), self.part(self.from_x, away), dp=self.where["side"])

    def to_inner(self):
        return self.copy(2, self.mine(self.value), self.mine(self.from_end), dp=self.where["pair"])

    def to_mate(self):
        return self.copy(3, self.mine(self.value), self.mine(self.from_mate), dp=self.where["mate"])

    def to_end(self):
        return self.copy(4, self.mine(self.final), self.mine(self.final), dp=self.where["pair"])

    def to_side(self):
        return self.copy(5, self.mine(self.final), self.mine(self.final), dp=self.where["side"])

    def add(self, arrived, into):
        into[...] = (self.value[...].astype(F32) + arrived[...].astype(F32)).astype(into.dtype)

    def add_mine(self, arrived, into):
        total = self.mine(self.value)[...].astype(F32) + self.mine(arrived)[...].astype(F32)
        self.mine(into)[...] = total.astype(into.dtype)

    def after_y(self):
        self.to_y().wait_recv()
        if self.fold is None:
            self.add(self.from_y, self.value)
        else:
            self.fold(self)
        self.begin_x()

    def begin_x(self):
        if self.where["line"]:
            self.to_x().start()
        else:
            self.final[...] = self.value[...]

    def after_x(self):
        if not self.where["line"]:
            return
        self.to_x().wait()
        self.add_mine(self.from_x, self.value)
        self.begin_z()

    def begin_z(self):
        pl.when(self.where["end"])(lambda: self.to_inner().start())

    def after_end(self):
        if not self.where["line"]:
            return

        @pl.when(self.where["inner"])
        def _():
            self.to_inner().wait_recv()
            self.add_mine(self.from_end, self.value)
            self.to_mate().start()

    def after_mate(self):
        if not self.where["line"]:
            return

        @pl.when(self.where["inner"])
        def _():
            self.to_mate().wait_recv()
            self.add_mine(self.from_mate, self.final)
            self.to_end().start()
            if self.split:
                self.to_side().start()

    def after_final(self):
        if not self.where["line"]:
            return

        @pl.when(self.where["end"])
        def _():
            self.to_end().wait_recv()
            self.to_side().start()

    def finish(self, had_y=True):
        if had_y:
            self.to_y().wait_send()
        if not self.where["line"]:
            return

        @pl.when(self.where["end"])
        def _():
            if not self.split:
                self.to_end().wait_recv()
            self.to_inner().wait_send()

        @pl.when(self.where["inner"])
        def _():
            self.to_mate().wait_send()
            self.to_end().wait_send()

        if self.split:
            self.to_side().wait()


def k3(
    line,
    qkv_in, seg_ref, o_in, lse_ref, xab_in, wts_in, do_in, dz1_in, gf_ref, go_in, small_ref,
    din_ref, ff_ref, fs_ref, sm_ref,
    qkv_ref, o_ref, xab_ref, wts_ref, go_ref, dz1_ref, do_ref, dq_s, qa, ka, va, da, dk, dv, sbuf, rcore, rmid, rhalf, hsum,
    fv, fy, fx, fe, fm, sv, so, sy, sx, se, sm, rgo, tv, to, tc, ty, tx, te, tm,
    psend, precv, send, recv, landed, local,
):
    length = 1024
    t, d, core, across, diag, side = where_am_i()
    y, c = t // 2, t % 2
    where = {"across": across, "side": side, "line": line, "half": d % 2}
    known = [{"tensor": core}, {"tensor": across}, {"tensor": diag}]
    if line:
        z = d // 2
        where["pair"] = d + 2 - 4 * (z % 2)
        where["mate"] = d + 2 - 4 * ((z + 1) % 2)
        where["end"] = (z == 0) | (z == 3)
        where["inner"] = (z == 1) | (z == 2)
        known += [{"dp": side}, {"dp": where["pair"]}]
    load_go, load_qkv, load_o, load_xab, load_wts, load_dz1 = [
        pltpu.make_async_copy(src, dst, local.at[6 + k])
        for k, (src, dst) in enumerate((
            (go_in, go_ref), (qkv_in, qkv_ref), (o_in, o_ref), (xab_in, xab_ref), (wts_in, wts_ref), (dz1_in, dz1_ref),
        ))
    ]
    loads = [pltpu.make_async_copy(gf_ref.at[0, p // 2, p % 2], fv.at[p], local.at[p]) for p in range(6)]
    start_all([load_go] + loads[:Y_EARLY] + [load_qkv, load_o] + loads[Y_EARLY:] + [load_xab, load_wts, load_dz1])
    barrier = pltpu.get_barrier_semaphore()
    for dev in known:
        pl.semaphore_signal(barrier, inc=1, device_id=dev, device_id_type=MESH)
    if line:
        @pl.when(where["inner"])
        def _():
            pl.semaphore_signal(barrier, inc=1, device_id={"dp": where["mate"]}, device_id_type=MESH)
            pl.semaphore_wait(barrier, len(known) + 1)

        @pl.when(where["end"])
        def _():
            pl.semaphore_wait(barrier, len(known))
    else:
        pl.semaphore_wait(barrier, len(known))

    pending = []
    peers = (t, core, across, diag)
    for i in range(3):
        middle, blk = block_of(t, i)
        for j, dev in enumerate(peers):
            src = do_in.at[i, pl.ds(192 * j, 192)]
            group = jnp.where(middle == 1, 2, j // 2)
            dst = do_ref.at[group, blk]
            sem = landed.at[group * 4 + blk]
            if j == 0:
                pltpu.make_async_copy(src, dst, sem).start()
                continue
            if j == 2:
                pl.when(middle == 0)(pltpu.make_async_copy(src, dst, sem).start)
                dev_to, cond = across, middle == 1
            elif j == 1:
                dev_to, cond = core, None
            else:
                dev_to, cond = jnp.where(middle == 1, diag, core), None
            copy = pltpu.make_async_remote_copy(
                src_ref=src, dst_ref=dst, send_sem=send.at[i * 3 + j - 1], recv_sem=sem,
                device_id={"tensor": dev_to}, device_id_type=MESH,
            )
            if cond is None:
                copy.start()
            else:
                pl.when(cond)(copy.start)
            pending.append((cond, copy))

    go_core = [
        pltpu.make_async_remote_copy(
            src_ref=go_in.at[2 * k + 1], dst_ref=rgo.at[k], send_sem=send.at[9 + k], recv_sem=recv.at[6 + k],
            device_id={"tensor": core}, device_id_type=MESH,
        )
        for k in range(2)
    ]
    small_core = pltpu.make_async_remote_copy(
        src_ref=small_ref, dst_ref=tc, send_sem=send.at[11], recv_sem=recv.at[8],
        device_id={"tensor": core}, device_id_type=MESH,
    )
    start_all(go_core + [small_core])
    big = [
        Piece(fv.at[p], gf_ref.at[1, p // 2, p % 2], fy.at[p], fx.at[p], fe.at[p], fm.at[p], ff_ref.at[p],
              psend.at[p], precv.at[p], where, split=line and p in SPLIT)
        for p in range(6)
    ]
    places = [(p, slice(0, 192)) for p in range(3)] + [(3, slice(32 * k, 32 * k + 32)) for k in range(6)]
    thin = [
        Piece(*[ref.at[p, rows] for ref in (sv, so, sy, sx, se, sm, fs_ref)], psend.at[6 + i], precv.at[6 + i], where)
        for i, (p, rows) in enumerate(places)
    ]

    def fold_small(piece):
        got = ty[...]
        add = jnp.concatenate([got[0:8], got[10:11], jnp.zeros((3, 768), F32), got[13:14], jnp.zeros((3, 768), F32)])
        tv[...] = tv[...] + add

    tiny = Piece(tv, to, ty, tx, te, tm, sm_ref, psend.at[15], precv.at[15], where, fold_small)
    early = Y_EARLY
    summed = X_EARLY if line else 0
    load_go.wait()
    for copy in go_core:
        copy.wait_recv()
    sv[0] = (go_ref[0].astype(F32) + rgo[0].astype(F32)).astype(BF)
    so[0] = (go_ref[2].astype(F32) + rgo[1].astype(F32)).astype(BF)
    thin[0].to_y().start()
    big[3].to_y().start()
    for copy in loads:
        copy.wait()
    for p in range(early):
        if p < summed:
            big[p].begin_z()
        else:
            big[p].begin_x()

    every = big + thin + [tiny]
    row64 = lax.broadcasted_iota(jnp.int32, (64, length), 0)

    def rows_of(blk):
        return pl.ds(pl.multiple_of(blk * BLK, BLK), BLK)

    own_seq = 2 * y

    def keep_or_send(middle, blk, r):
        seq = 1 if middle else own_seq
        i = 4 * seq + blk - 3 * t
        mine = (i >= 0) & (i < 3)

        @pl.when(mine)
        def _():
            rs = rows_of(i)
            dz1_ref[rs, :] += r

        @pl.when(jnp.logical_not(mine))
        def _():
            sbuf[1 if middle else 0, rows_of(blk), :] = r.astype(BF)

    def into_middle(n, _):
        keep_or_send(True, n, dg(dq2[:, rows_of(n)], wts_ref[0], 0, 0))
        return 0

    dq0, dq1, dq2 = [dq_s.at[g] for g in range(3)]

    def into_own(n, _):
        r = dg(dq0[:, rows_of(n)], wts_ref[0], 0, 0) + dg(dq1[:, rows_of(n)], wts_ref[1], 0, 0)
        keep_or_send(False, n, r)
        return 0

    far = 2 * (1 - y)
    half_copy = pltpu.make_async_remote_copy(
        src_ref=sbuf.at[1, rows_of(far + 1 - c)], dst_ref=rhalf, send_sem=send.at[12],
        recv_sem=recv.at[3], device_id={"tensor": core}, device_id_type=MESH,
    )
    far_copy = pltpu.make_async_remote_copy(
        src_ref=hsum, dst_ref=rmid.at[c], send_sem=send.at[13], recv_sem=recv.at[4 + c],
        device_id={"tensor": 2 * (1 - y) + y}, device_id_type=MESH,
    )
    core_copies = []
    for i in range(3):
        middle, blk = block_of(core, i)
        core_copies.append((
            middle,
            pltpu.make_async_remote_copy(
                src_ref=sbuf.at[middle, rows_of(blk)], dst_ref=rcore.at[i], send_sem=send.at[14 + i],
                recv_sem=recv.at[i], device_id={"tensor": core}, device_id_type=MESH,
            ),
        ))

    def unit(u, _):
        g = (u % 3 + 1) % 3
        h = u // 3

        @pl.when(u == 1)
        def _():
            small_core.wait_recv()
            a, b = small_ref[...], tc[...]
            swapped = jnp.concatenate([b[0:8], b[9:10], b[8:9], b[11:12], b[10:11], b[12:16]])
            tv[...] = a + swapped

        @pl.when(u == 2)
        def _():
            big[4].to_y().start()

        @pl.when(u == 5)
        def _():
            big[5].to_y().start()

        @pl.when(u == 8)
        def _():
            load_wts.wait()
            load_dz1.wait()
            lax.fori_loop(0, 4, into_middle, 0)
            half_copy.start()

        @pl.when(h == 0)
        def _():
            for blk in range(4):
                pltpu.make_async_copy(do_in.at[0, pl.ds(0, 192)], do_ref.at[g, blk], landed.at[g * 4 + blk]).wait()

        same = (row64 == seg_ref[pl.ds(jnp.where(g == 2, 1, own_seq), 1), :]).astype(F32)
        ro = pl.multiple_of(h * 192, 64)
        qh, kh, vh = pl.ds(ro, 64), pl.ds(ro + 64, 64), pl.ds(ro + 128, 64)
        l1, l2, l3 = split3(-lse_ref[g * 3 + h])
        qa[0:64, :] = qkv_ref[g, h, 0:64, :]
        qa[64:128, :] = jnp.where(row64 == 8, l1, jnp.where(row64 == 9, l2, jnp.where(row64 == 10, l3, same))).astype(BF)
        key_mark = jnp.where(row64 >= 8, 1.0, (same - 1.0) * BIG).astype(BF)
        ka[...] = jnp.concatenate([qkv_ref[g, h, 64:128, :], key_mark], axis=0).T
        va[...] = jnp.concatenate([qkv_ref[g, h, 128:192, :], jnp.ones((64, length), BF)], axis=0).T
        hs = pl.ds(pl.multiple_of(h * 64, 64), 64)
        for b in range(4):
            bs = slice(b * BLK, (b + 1) * BLK)
            do = do_ref[g, b, hs, :]
            e1, e2, e3 = split3(-jnp.sum(do.astype(F32) * o_ref[g, b, hs, :].astype(F32), axis=0, keepdims=True))
            da[0:64, bs] = do
            rb = row64[:, bs]
            da[64:128, bs] = jnp.where(rb == 8, e1, jnp.where(rb == 9, e2, jnp.where(rb == 10, e3, 0.0))).astype(BF)
        dk[...] = jnp.zeros_like(dk)
        dv[...] = jnp.zeros_like(dv)

        def chunk(n, _):
            for k, steps in STEPS.items():
                @pl.when(2 * u + n == k)
                def _(steps=steps):
                    for stage, name in steps:
                        getattr(every[name], stage)()

            cs = pl.ds(pl.multiple_of(n * 512, 512), 512)
            s = jnp.dot(ka[...], qa[:, cs], preferred_element_type=F32)
            p = jnp.exp2(s)
            dp = jnp.dot(va[...], da[:, cs], preferred_element_type=F32)
            pb = p.astype(BF)
            ds = (p * dp).astype(BF)
            dv[...] += dg(da[0:64, cs], pb, 1, 1)
            dk[...] += dg(qa[0:64, cs], ds, 1, 1)
            dq = jnp.dot(qkv_ref[g, h, 64:128, :], ds, preferred_element_type=F32)
            dq_s[g, qh, cs] = (dq * (HEAD_DIM ** (-0.5))).astype(BF)
            return 0

        lax.fori_loop(0, length // 512, chunk, 0)
        dq_s[g, kh, :] = (dk[...] * math.log(2.0)).astype(BF)
        dq_s[g, vh, :] = dv[...].astype(BF)

        @pl.when(g == 1)
        def _():
            pl.when(h == 0)(load_xab.wait)
            so[1 + h] = jnp.dot(dq_s[1, pl.ds(ro, 192), :], xab_ref[0], preferred_element_type=F32).astype(BF)

        for k, pieces in ((0, thin[1:2]), (3, thin[2:3]), (6, thin[3:])):
            @pl.when(u == k)
            def _(pieces=pieces):
                for piece in pieces:
                    piece.to_y().start()

        @pl.when(g == 0)
        def _():
            rows = pl.ds(ro, 192)
            r = jnp.dot(dq_s[0, rows, :], xab_ref[0], preferred_element_type=F32)
            sv[1 + h] = (r + jnp.dot(dq_s[2, rows, :], xab_ref[1], preferred_element_type=F32)).astype(BF)

        return 0

    load_qkv.wait()
    load_o.wait()
    lax.fori_loop(0, 9, unit, 0)
    for stage, name in FIRST_TAIL:
        getattr(every[name], stage)()
    half_copy.wait_recv()
    hsum[...] = (sbuf[1, rows_of(far + c), :].astype(F32) + rhalf[...].astype(F32)).astype(BF)
    far_copy.start()
    ones = jnp.ones((8, length), BF)
    tv[12:13, 0:576] = (dg(ones, dq_s[0], 1, 1) + dg(ones, dq_s[2], 1, 1))[0:1]
    tv[13:14, 0:576] = dg(ones, dq_s[1], 1, 1)[0:1]
    to[...] = tv[...]
    tiny.to_y().start()
    lax.fori_loop(0, 4, into_own, 0)
    for middle, copy in core_copies:
        copy.start()

    for k, (stage, name) in enumerate(TAIL_STEPS):
        getattr(every[name], stage)()
        if k == TAIL_INPUT:
            for i in range(3):
                core_copies[i][1].wait_recv()
                middle, blk = block_of(t, i)
                rs = pl.ds(i * BLK, BLK)

                @pl.when(middle == 0)
                def _():
                    din_ref[rs, :] = (dz1_ref[rs, :] + rcore[i].astype(F32)).astype(BF)

                @pl.when(middle == 1)
                def _():
                    k = blk % 2
                    pltpu.make_async_copy(hsum, rmid.at[k], recv.at[4 + k]).wait()
                    din_ref[rs, :] = (dz1_ref[rs, :] + rcore[i].astype(F32) + rmid[k].astype(F32)).astype(BF)

    for p, piece in enumerate(big):
        piece.finish(p >= early)
    for piece in thin + [tiny]:
        piece.finish()
    for copy in [c for _, c in core_copies] + [half_copy, far_copy] + go_core + [small_core]:
        copy.wait_send()
    for cond, copy in pending:
        if cond is None:
            copy.wait_send()
        else:
            pl.when(cond)(copy.wait_send)

def finish(
    out_in, din_in, ff_in, fs_in, sm,
    out_o, din_o, gwq, gbq, gwk, gwv, gbv, gwo, gbo, gg1, gs1, gwin, gbin, gwback, gbback, gg2, gs2,
    out_v, din_v, ff, fs, win_v, wback_v, q_v, wo_v, local,
):
    pieces = [pltpu.make_async_copy(ff_in.at[p], ff.at[p], local.at[16 + p]) for p in range(6)]
    loads = [
        pltpu.make_async_copy(out_in, out_v, local.at[2]),
        pltpu.make_async_copy(din_in, din_v, local.at[3]),
        pltpu.make_async_copy(fs_in, fs, local.at[1]),
    ]
    start_all(loads[:1] + pieces + loads[1:])
    stores = []

    def store(src, dst):
        copy = pltpu.make_async_copy(src, dst, local.at[4 + len(stores)])
        copy.start()
        stores.append(copy)

    for k, ref in ((0, gbo), (1, gg1), (2, gs1), (8, gbin), (3, gbback), (4, gg2), (5, gs2)):
        ref[...] = sm[k : k + 1, :].reshape(768)
    heads = sm[12:13, 0:576]
    for k, ref in ((0, gbq), (2, gbv)):
        ref[...] = jnp.concatenate([heads[:, 192 * h + 64 * k : 192 * h + 64 * k + 64] for h in range(3)], axis=1).reshape(192)
    loads[0].wait()
    store(out_v, out_o)
    for ch in range(3):
        cs = pl.ds(ch * BLK, BLK)
        pieces[2 * ch].wait()
        win_v[:, ch * BLK : (ch + 1) * BLK] = ff[2 * ch].astype(F32)
        pieces[2 * ch + 1].wait()
        wback_v[cs, :] = ff[2 * ch + 1].T.astype(F32)
        store(wback_v.at[cs], gwback.at[cs])
    store(win_v, gwin)
    loads[1].wait()
    store(din_v, din_o)
    loads[2].wait()
    wo_v[...] = fs[0].astype(F32)
    store(wo_v, gwo)
    for k, ref in enumerate((gwq, gwk, gwv)):
        for h in range(3):
            q_v[k, 64 * h : 64 * h + 64, :] = fs[1 + h, 64 * k : 64 * k + 64, :].astype(F32)
        store(q_v.at[k], ref)
    for copy in stores:
        copy.wait()


def vm(*shape, dtype=BF):
    return pltpu.VMEM(shape, dtype)


def sds(*shape, dtype=BF):
    return jax.ShapeDtypeStruct(shape, dtype)


VM = pl.BlockSpec(memory_space=pltpu.VMEM)
ANY = pl.BlockSpec(memory_space=pl.ANY)


def params(cid):
    return pltpu.CompilerParams(collective_id=cid, has_side_effects=True, vmem_limit_bytes=62 * 2**20)


def local_step(
    line,
    layer_input, segment_ids, w_query, b_query, w_key, w_value, b_value, w_out, b_out, first_gain, first_shift,
    w_in, b_in, w_back, b_back, second_gain, second_shift, cotangent,
):
    dma = pltpu.SemaphoreType.DMA
    qkv, o, lse, xab, wts, out, dz1, do, gf, go, small = pl.pallas_call(
        partial(forward, line),
        out_shape=(
            sds(3, 3, 192, 1024), sds(3, 4, 192, BLK), sds(9, 1, 1024, dtype=F32), sds(2, 1024, 768), sds(2, 576, 768),
            sds(768, 768), sds(768, 768, dtype=F32), sds(3, 768, BLK), sds(2, 3, 2, 768, BLK), sds(4, 192, 768),
            sds(16, 768, dtype=F32),
        ),
        in_specs=[VM, ANY] + [VM] * 13 + [ANY] * 3,
        out_specs=(ANY, ANY, VM, ANY, ANY, ANY, ANY, ANY, ANY, ANY, VM),
        scratch_shapes=[
            vm(768, 768), vm(3, 768, BLK), vm(2, 3, 2, 768, BLK), vm(4, 192, 768),
            vm(3, 3, 192, 1024), vm(3, 4, 192, BLK), vm(2, 1024, 768), vm(2, 576, 768),
            vm(8, 768, dtype=F32), vm(3, 8, 768, dtype=F32), vm(576, 1, dtype=F32),
            vm(128, 1024), vm(128, 1024), vm(80, 1024),
            vm(768, 768), vm(3, 768, BLK), vm(768, 768), vm(768, 3072), vm(3072, 768),
            vm(768, 768), vm(768, 768), vm(768, 768, dtype=F32), vm(768, 1, dtype=F32), vm(768, 3072), vm(768, 3072),
            vm(768, 768, dtype=F32), vm(768, 768), vm(768, 768),
            vm(3, 2, 768, BLK), vm(3, 2, 768, BLK), vm(max(Y_EARLY, 1), 768, BLK), vm(max(X_EARLY, 1), 768, BLK),
            dma((80,)), dma((80,)), dma((24,)),
        ],
        compiler_params=params(0),
        name="forward_and_feed_forward",
    )(
        layer_input, cotangent, w_query.T, w_key.T, w_value.T, b_query, b_value, b_in,
        b_out, first_gain, first_shift, b_back, second_gain, second_shift, segment_ids, w_out, w_in, w_back,
    )

    piece, slab, tiny = vm(6, 768, BLK), vm(4, 192, 768), vm(16, 768, dtype=F32)
    din, ff, fs, sm = pl.pallas_call(
        partial(k3, line),
        out_shape=(sds(768, 768), sds(6, 768, BLK), sds(4, 192, 768), sds(16, 768, dtype=F32)),
        in_specs=[ANY, VM, ANY, VM, ANY, ANY, ANY, ANY, ANY, ANY, VM],
        out_specs=(VM, VM, VM, VM),
        scratch_shapes=[
            vm(3, 3, 192, 1024), vm(3, 4, 192, BLK), vm(2, 1024, 768), vm(2, 576, 768), vm(4, 192, 768),
            vm(768, 768, dtype=F32),
            vm(3, 4, 192, BLK), vm(3, 576, 1024), vm(128, 1024), vm(1024, 128), vm(1024, 128), vm(128, 1024),
            vm(64, 1024, dtype=F32), vm(64, 1024, dtype=F32), vm(2, 1024, 768),
            vm(3, BLK, 768), vm(2, BLK, 768), vm(BLK, 768), vm(BLK, 768),
            piece, piece, piece, piece, piece, slab, slab, slab, slab, slab, slab, vm(2, 192, 768),
            tiny, tiny, tiny, tiny, tiny, tiny, tiny,
            dma((16, 6)), dma((16, 6)), dma((17,)), dma((9,)), dma((12,)), dma((12,)),
        ],
        compiler_params=params(1),
        name="attention_backward",
    )(qkv, segment_ids, o, lse, xab, wts, do, dz1, gf, go, small)
    if not line:
        ff, fs = lax.psum((ff, fs), "dp")
        sm = lax.psum(sm, "dp")
    row = sds(768, dtype=F32)
    cols, thin = sds(192, 768, dtype=F32), sds(192, dtype=F32)
    square = sds(768, 768, dtype=F32)
    outs = pl.pallas_call(
        finish,
        out_shape=(
            sds(768, 768), sds(768, 768), cols, thin, cols, cols, thin, sds(192, 768, dtype=F32),
            row, row, row, square, row, square, row, row, row,
        ),
        in_specs=[ANY, ANY, ANY, ANY, VM],
        out_specs=(ANY, ANY, ANY, VM, ANY, ANY, VM, ANY, VM, VM, VM, ANY, VM, ANY, VM, VM, VM),
        scratch_shapes=[
            vm(768, 768), vm(768, 768), vm(6, 768, BLK), vm(4, 192, 768), vm(768, 768, dtype=F32), vm(768, 768, dtype=F32),
            vm(3, 192, 768, dtype=F32), vm(192, 768, dtype=F32), dma((22,)),
        ],
        compiler_params=pltpu.CompilerParams(vmem_limit_bytes=62 * 2**20),
        name="results",
    )(out, din, ff, fs, sm)
    return (*outs[:2], outs[2].T, outs[3], outs[4].T, outs[5].T, *outs[6:])


def solution(mesh):
    rows = P(("dp", "tensor"), None)
    in_specs = (
        rows, P("dp", None), P(None, "tensor"), P("tensor"), P(None, "tensor"), P(None, "tensor"), P("tensor"),
        P("tensor", None), P(), P(), P(), P(None, "tensor"), P("tensor"), P("tensor", None), P(), P(), P(), rows,
    )
    out_specs = (
        rows, rows, P(None, "tensor"), P("tensor"), P(None, "tensor"), P(None, "tensor"), P("tensor"),
        P("tensor", None), P(), P(), P(), P(None, "tensor"), P("tensor"), P("tensor", None), P(), P(), P(),
    )
    line = mesh.shape["dp"] == 8
    return jax.shard_map(partial(local_step, line), mesh=mesh, in_specs=in_specs, out_specs=out_specs, check_vma=False)
```
